128 devices in a mesh: freq: 2 (over z_lo), tile: 64 (over z_hi, y, x, core).
Axes of the slice: x: 4, y: 4, z: 4 (z_hi: 2, z_lo: 2; z = z_hi * 2 + z_lo), core: 2. Of those that a mesh axis runs over, the one named last changes fastest.
Arguments:
- residual: float32 [2, 3, 65536], P('freq', None, 'tile'), may hold values from -24 to 24
- row_counts: int32 [64, 256], P('tile'), may hold values from 1 to 16, 1024 in all within a row
- recv_owner: int32 [16384, 1], P('tile'), may hold values from 0 to 63; in each aligned block of 256 rows (0 to 255, 256 to 511, ...) at most 16 rows name the same one
- recv_cell: int32 [16384], P('tile'), may hold values from 0 to 262143
- conductivity: float32 [64, 64, 32, 128], P('tile'), may hold values from 0.5 to 4
- laplace: float32 [2], P('freq'), may hold values from 0.25 to 1
- forward_field: bfloat16 [2, 64, 3, 64, 32, 128], P('freq', 'tile'), may hold values from -6 to 6
Outputs:
- gradient: float32 [64, 64, 32, 128], P(None, 'tile', 'freq')
The draws below stay inside these ranges and needn't reach their ends.
Inputs may be any that keep to these rules, and one draw needn't show every extreme that they name: `row_counts`: the 256 counts of one tile sum to 1024; some receiver has exactly 16 rows. `recv_owner`: among the receivers of one tile at most 16 share an owner tile, and in some tile exactly 16 do.
All inputs are finite; a program needn't handle non-finite values.
Results may differ from the reference program's by a relative error of at most 0.0003.
Values sent between devices are 32-bit elements; how exact they have to be, the bound alone decides.
A program may use at most 320 MiB of HBM per device.

```python
import math
import jax
import jax.numpy as jnp
import numpy as np
from jax import lax

CX = 64
CY = 32
CZ = 128
TY = 4
TZ = 4
TX = 4
NFREQ = 2
SWEEPS = 8
RCV = 256
ROWS = 1024
ROW_MOST = 16
CAP = 16
CELLS = 262144
NX = 256
NY = 128
NZ = 512
N_TILE = 64


def touch_ends(values, own_key, smallest, largest):
    longest = values.shape.index(max(values.shape))
    spots = []
    for shift in (0, 1):
        where = [jax.random.randint(jax.random.fold_in(own_key, axis), (), 0, length) for axis, length in enumerate(values.shape)]
        where[longest] = (where[longest] + shift) % values.shape[longest]
        spots.append(tuple(where))
    return values.at[spots[0]].set(smallest).at[spots[1]].set(largest)


def level_of(key, extent, cuts, least, largest):
    def one(axis_at, parts):
        steps = jax.random.uniform(jax.random.fold_in(jax.random.fold_in(key, 6), axis_at), (parts,), jnp.float32, least / len(cuts), largest / len(cuts))
        return jnp.repeat(jnp.exp(steps), extent[axis_at] // parts).reshape((-1,) + (1,) * (len(extent) - axis_at - 1))

    loudness = one(*cuts[0])
    for cut in cuts[1:]:
        loudness = loudness * one(*cut)
    return loudness


def length_profile(number_of, total, bound, slope):
    loads = [(1 << 20) // math.isqrt(standing ** slope) + 1 for standing in range(2, number_of + 1)]
    spare, given = total - bound - (number_of - 1), [1] * (number_of - 1)
    while spare > 0:
        free = [i for i in range(number_of - 1) if given[i] < bound]
        mass, left = sum([loads[i] for i in free]), spare
        for i in free:
            more = min(bound - given[i], max(1, left * loads[i] // mass), spare)
            given[i] = given[i] + more
            spare = spare - more
    return np.array([bound] + given)


def ragged(stream_key, number_of, total, bound, lean):
    if number_of == 2:
        one = jax.random.randint(stream_key, (), max(1, total - bound), min(bound, total - 1) + 1)
        return jnp.stack([one, total - one])
    tallies = jnp.asarray(length_profile(number_of, total, bound, lean), jnp.int32)
    twos = (number_of - 1) // 2
    donor, sink = tallies[1:1 + 2 * twos:2], tallies[2:2 + 2 * twos:2]
    margin = jnp.minimum(donor - 1, bound - sink)
    passed = jax.random.randint(jax.random.fold_in(stream_key, 1), (twos,), 0, 1 << 20) % (margin + 1)
    tallies = tallies.at[1:1 + 2 * twos:2].set(donor - passed).at[2:2 + 2 * twos:2].set(sink + passed)
    return tallies[jax.random.permutation(jax.random.fold_in(stream_key, 2), number_of)]


def deal_out(key, own, number, rows, number_of, top, most, lean):
    ranking = jax.random.permutation(key, number_of)
    crowded, ordinary = load_shares(number_of, rows * top, most, lean, True), load_shares(number_of, rows * top, most, lean, False)
    places = jnp.arange(number_of)

    def named(lengths, offset_by):
        used = int((lengths > 0).sum())
        fixed = max(1, used // 4)
        shifted = fixed + (places - fixed + offset_by * (used - fixed)) % max(1, number_of - fixed)
        return jnp.zeros((number_of,), jnp.int32).at[ranking[jnp.where(places < fixed, places, shifted)]].set(jnp.asarray(lengths, jnp.int32))

    lengths = jnp.where(number % 4 == 0, named(crowded, number // 4), named(ordinary, number - number // 4 - 1))
    mixed = jax.random.permutation(jax.random.fold_in(own, 3), number_of)
    donor, receiver = mixed[0:number_of // 2 * 2:2], mixed[1:number_of // 2 * 2:2]
    room = jnp.minimum(lengths[donor] - 1, most - lengths[receiver]) // 2
    room = jnp.where((donor == ranking[0]) | (receiver == ranking[0]) | (lengths[receiver] == 0), 0, jnp.maximum(room, 0))
    shifted = jax.random.randint(jax.random.fold_in(own, 4), (number_of // 2,), 0, 1 << 20) % (room + 1)
    lengths = lengths.at[donor].add(-shifted).at[receiver].add(shifted)
    members = jnp.searchsorted(jnp.cumsum(lengths), jnp.arange(rows * top), side="right").astype(jnp.int32)
    table = members.reshape(top, rows).T
    table = table[jax.random.permutation(jax.random.fold_in(own, 1), rows)]
    offset_by = jax.random.randint(jax.random.fold_in(own, 2), (rows, 1), 0, top)
    return jnp.take_along_axis(table, (jnp.arange(top)[None, :] + offset_by) % top, axis=1)


def load_shares(count, total, limit, lean, full):
    loads = [(1 << 20) // math.isqrt(grade ** lean) + 1 for grade in range(1, count + 1)]
    largest = limit if full else min(limit, max(-(-total // count), total * loads[0] // sum(loads)))
    least = 1 if total - largest >= count - 1 else 0
    counts, rest = [largest] + [least] * (count - 1), total - largest - least * (count - 1)
    while rest > 0:
        free = [i for i in range(1, count) if counts[i] < largest] or [i for i in range(1, count) if counts[i] < limit]
        whole, left = sum([loads[i] for i in free]), rest
        for i in free:
            extra = min(limit - counts[i], max(1, left * loads[i] // whole), rest)
            counts[i] = counts[i] + extra
            rest = rest - extra
    return np.array(counts)


def scatter_about(key, dims, spread, bound, pieces=(), kind=jnp.bfloat16):
    result = spread * jax.random.normal(key, dims, jnp.float32)
    if pieces:
        result = result * level_of(key, dims, pieces, -0.22, 0.18)
    return jnp.clip(result, -bound, bound).astype(kind)


def setup_inputs(seed: int = 0) -> dict:
    key_of = jax.random.split(jax.random.key(seed), 8)
    residual = scatter_about(key_of[0], (NFREQ, 3, ROWS * N_TILE), 4.0, 24.0, ((0, 2), (2, 64)), jnp.float32)
    row_counts = jax.vmap(lambda own: ragged(own, RCV, ROWS, ROW_MOST, 2))(jax.random.split(key_of[1], N_TILE)).reshape((N_TILE, RCV)).astype(jnp.int32)
    recv_owner_keys = jax.random.split(jax.random.fold_in(key_of[2], 1), (RCV * N_TILE) // RCV)
    recv_owner_turns = jax.random.permutation(jax.random.fold_in(key_of[2], 3), (RCV * N_TILE) // RCV)
    recv_owner = jax.vmap(lambda own, number: deal_out(jax.random.fold_in(key_of[2], 2), own, number, RCV, N_TILE, 1, CAP, 2))(recv_owner_keys, recv_owner_turns).reshape((RCV * N_TILE, 1))
    recv_cell = touch_ends(jax.random.randint(key_of[3], (RCV * N_TILE,), 0, CELLS), jax.random.fold_in(key_of[3], 1), 0, CELLS - 1).astype(jnp.int32)
    conductivity = jnp.clip(jnp.exp(math.log(4.0) - 2.0794415 * jax.random.uniform(key_of[4], (N_TILE, CX, CY, CZ), jnp.float32) ** level_of(key_of[4], (N_TILE, CX, CY, CZ), ((0, 64),), -0.2, 0.2)), 0.5, 4.0)
    laplace = jnp.clip(jnp.exp(math.log(1.0) - 1.3862944 * jax.random.uniform(key_of[5], (NFREQ,), jnp.float32) ** level_of(key_of[5], (NFREQ,), ((0, 2),), -0.2, 0.2)), 0.25, 1.0)
    forward_field = scatter_about(key_of[6], (NFREQ, N_TILE, 3, CX, CY, CZ), 1.0, 6.0, ((0, 2), (1, 64)))
    return dict(residual=residual, row_counts=row_counts, recv_owner=recv_owner, recv_cell=recv_cell, conductivity=conductivity, laplace=laplace, forward_field=forward_field)


RELAXATION = 0.5


def forward_step(values, direction):
    upper_cut = [slice(0, -1)] * 3
    lower_cut = [slice(0, -1)] * 3
    upper_cut[direction] = slice(1, None)
    return values[tuple(upper_cut)] - values[tuple(lower_cut)]


def backward_step(values, direction):
    upper_cut = [slice(1, None)] * 3
    lower_cut = [slice(1, None)] * 3
    lower_cut[direction] = slice(0, -1)
    return values[tuple(upper_cut)] - values[tuple(lower_cut)]


def curl_curl(padded):
    field_x, field_y, field_z = padded[0], padded[1], padded[2]
    swirl_x = forward_step(field_z, 1) - forward_step(field_y, 2)
    swirl_y = forward_step(field_x, 2) - forward_step(field_z, 0)
    swirl_z = forward_step(field_y, 0) - forward_step(field_x, 1)
    return jnp.stack([backward_step(swirl_z, 1) - backward_step(swirl_y, 2),
                      backward_step(swirl_x, 2) - backward_step(swirl_z, 0),
                      backward_step(swirl_y, 0) - backward_step(swirl_x, 1)])


def relax_sweep(padded, source, damping, inside):
    centre = padded[:, 1:-1, 1:-1, 1:-1]
    update = centre + RELAXATION * (source - curl_curl(padded) - damping * centre) / (4.0 + damping)
    return update * inside


def blocks_to_grid(blocks):
    comps = blocks.shape[1]
    shaped = blocks.reshape(TX, TY, TZ, comps, CX, CY, CZ)
    return shaped.transpose(3, 0, 4, 1, 5, 2, 6).reshape(comps, NX, NY, NZ)


def reference(residual, row_counts, recv_owner, recv_cell, conductivity, laplace, forward_field):
    residual_rows = residual.reshape(NFREQ, 3, N_TILE, ROWS)
    row_ends = jnp.cumsum(row_counts, axis=1)
    row_starts = row_ends - row_counts
    positions = jnp.arange(ROWS, dtype=jnp.int32)
    member = ((positions[None, None, :] >= row_starts[:, :, None])
              & (positions[None, None, :] < row_ends[:, :, None])).astype(jnp.float32)
    cell_index = (recv_owner[:, 0] * CELLS + recv_cell).astype(jnp.int32)
    sigma_grid = blocks_to_grid(conductivity[:, None])[0]
    gradient = jnp.zeros((NX, NY, NZ), jnp.float32)
    for frequency in range(NFREQ):
        row_sums = jnp.einsum("ctr,tqr->ctq", residual_rows[frequency], member,
                              precision=lax.Precision.HIGHEST)
        receiver_means = row_sums / row_counts.astype(jnp.float32)[None]
        source_blocks = jnp.zeros((3, N_TILE * CELLS), jnp.float32).at[:, cell_index].add(
            receiver_means.reshape(3, N_TILE * RCV))
        source = blocks_to_grid(source_blocks.reshape(3, N_TILE, CX, CY, CZ).transpose(1, 0, 2, 3, 4))
        damping = laplace[frequency] * sigma_grid
        adjoint = jnp.zeros_like(source)
        for sweep_index in range(SWEEPS):
            padded = jnp.pad(adjoint, ((0, 0), (1, 1), (1, 1), (1, 1)))
            adjoint = relax_sweep(padded, source, damping, 1.0)
        forward_grid = blocks_to_grid(forward_field[frequency]).astype(jnp.float32)
        gradient = gradient + (-laplace[frequency] * sigma_grid * jnp.sum(forward_grid * adjoint, axis=0))
    shaped = gradient.reshape(TX, CX, TY, CY, TZ, CZ).transpose(0, 2, 4, 1, 3, 5)
    return shaped.reshape(N_TILE, CX, CY, CZ)
```

```python
import functools

import jax
import jax.numpy as jnp
from jax import lax
from jax.experimental import pallas as pl
from jax.experimental.pallas import tpu as pltpu
from jax.sharding import PartitionSpec as P

F32 = jnp.float32
BF16 = jnp.bfloat16
I32 = jnp.int32
MESH = pl.DeviceIdType.MESH

TX, TY, TZ = 4, 4, 4
TILES = 64
CX, CY, CZ = 64, 32, 128
RIM = 7

YR = 56
B0 = 81
RUN = 26
SEG = 42
PLANES = 112
OWN = 8


def iota(shape, dim):
    return lax.broadcasted_iota(I32, shape, dim)


def vmem():
    return pl.BlockSpec(memory_space=pltpu.VMEM)


def hbm():
    return pl.BlockSpec(memory_space=pl.ANY)


def place(t):
    return t // (TY * TZ), (t // TZ) % TY, t % TZ


def three(value):
    hi = value.astype(BF16)
    rest = value - hi.astype(F32)
    mid = rest.astype(BF16)
    low = (rest - mid.astype(F32)).astype(BF16)
    return hi, mid, low


def pack_own(read, s, rows, moves):
    lane = iota((rows, 128), 1)
    total = jnp.zeros((rows, 128), F32)
    for g in range(3):
        plane = read(1 + RUN * g + s)
        for begin, end, shift in moves:
            moved = pltpu.roll(plane, (SEG * g + shift) % 128, 1)
            total = jnp.where((lane >= SEG * g + begin) & (lane < SEG * g + end), moved, total)
    return total


def gather_kernel(res_ref, cnt_ref, idx_ref, lap_ref, cond_ref, list_ref, coef_ref,
                  cext, pack, low, high, sends, recvs, zsend, zrecv, gsend, grecv, lsem):
    f, t = lax.axis_index("freq"), lax.axis_index("tile")
    tx, ty, tz = place(t)
    barrier = pltpu.get_barrier_semaphore()

    def greet(i, c):
        pl.semaphore_signal(barrier, inc=1, device_id=(f, (t + i) % TILES), device_id_type=MESH)
        return c

    lax.fori_loop(1, TILES, greet, 0)
    own = pltpu.make_async_copy(cond_ref, cext.at[pl.ds(OWN, CX), pl.ds(8, CY)], lsem)
    own.start()

    counts = cnt_ref[...].astype(F32)
    upto = (iota((256, 256), 0) <= iota((256, 256), 1)).astype(F32)
    ends = jnp.dot(jnp.broadcast_to(counts, (8, 256)).astype(BF16), upto.astype(BF16), preferred_element_type=F32)[0:1]
    starts = ends - counts
    at = iota((1024, 256), 0).astype(F32)
    member = ((at >= starts) & (at < ends)).astype(F32).astype(BF16)
    sums = jnp.zeros((3, 256), F32)
    for part in three(res_ref[0]):
        sums = sums + jnp.dot(part, member, preferred_element_type=F32)
    means = sums / counts
    both = jnp.concatenate([means, idx_ref[...]], axis=0)
    list_ref[t] = jnp.concatenate([both[:, :128], both[:, 128:]], axis=0)

    pl.semaphore_wait(barrier, TILES - 1)

    def share(i, c):
        pltpu.make_async_remote_copy(list_ref.at[t], list_ref.at[t], gsend, grecv,
                                     device_id=(f, (t + i) % TILES), device_id_type=MESH).start()
        return c

    lax.fori_loop(1, TILES, share, 0)

    spans = {1: (CX - 7, 1, 7), -1: (0, 72, 7), 0: (0, 8, CX)}
    rows = {1: (CY - 8, 0, 8), -1: (0, 40, 8), 0: (0, 8, CY)}
    ways = [(dx, dy) for dx in (-1, 0, 1) for dy in (-1, 0, 1) if (dx, dy) != (0, 0)]

    def inside(dx, dy):
        x, y = tx + dx, ty + dy
        return (x >= 0) & (x < TX) & (y >= 0) & (y < TY)

    def halo(n):
        dx, dy = ways[n]
        xs, xd, xn = spans[dx]
        ys, yd, yn = rows[dy]
        return pltpu.make_async_remote_copy(
            cond_ref.at[pl.ds(xs, xn), pl.ds(ys, yn)], cext.at[pl.ds(xd, xn), pl.ds(yd, yn)],
            sends.at[n], recvs.at[n], device_id=(f, t + dx * TY * TZ + dy * TZ), device_id_type=MESH)

    for n, (dx, dy) in enumerate(ways):
        @pl.when(inside(dx, dy))
        def _(n=n):
            halo(n).start()
    own.wait()
    for n, (dx, dy) in enumerate(ways):
        @pl.when(inside(-dx, -dy))
        def _(n=n):
            halo(n).wait_recv()

    def read(i):
        return cext[i]

    def fill(s, c):
        pack[s] = pack_own(read, s, 48, ((0, 7, -121), (35, 42, 35)))
        return c

    lax.fori_loop(0, RUN, fill, 0)

    def rim(up):
        return pltpu.make_async_remote_copy(
            pack, low if up else high, zsend.at[up], zrecv.at[up],
            device_id=(f, t + (1 if up else -1)), device_id_type=MESH)

    @pl.when(tz < TZ - 1)
    def _():
        rim(1).start()

    @pl.when(tz > 0)
    def _():
        rim(0).start()

    lap = lap_ref[0]
    yrow = iota((48, 128), 0) - 8
    yin = (yrow + ty * CY >= 0) & (yrow + ty * CY < TY * CY)

    def fill_a(i, c):
        x = i - 8 + tx * CX
        good = yin & (x >= 0) & (x < TX * CX)
        coef_ref[i, pl.ds(0, 48), :] = jnp.where(good, 1.0 / (4.0 + lap * cext[i]), 0.0)
        return c

    lax.fori_loop(0, 80, fill_a, 0)

    @pl.when(tz > 0)
    def _():
        rim(1).wait_recv()

    @pl.when(tz < TZ - 1)
    def _():
        rim(0).wait_recv()

    lane = iota((48, 128), 1)
    run = (lane >= SEG).astype(I32) + (lane >= 2 * SEG).astype(I32)
    seg = lane - run * SEG
    z = jnp.where(seg < 21, seg - 7, seg + 93) + tz * CZ
    zin = (z >= 0) & (z < TZ * CZ) & (lane < 3 * SEG)

    def fill_b(s, c):
        value = pack_own(read, s, 48, ((7, 21, 7), (21, 35, -93)))
        value = jnp.where(seg < 7, low[s], jnp.where(seg >= 35, high[s], value))
        x = RUN * run + s - 7 + tx * CX
        good = yin & zin & (x >= 0) & (x < TX * CX)
        coef_ref[B0 + s, pl.ds(0, 48), :] = jnp.where(good, 1.0 / (4.0 + lap * value), 0.0)
        return c

    lax.fori_loop(0, RUN, fill_b, 0)

    for n, (dx, dy) in enumerate(ways):
        @pl.when(inside(dx, dy))
        def _(n=n):
            halo(n).wait_send()

    @pl.when(tz < TZ - 1)
    def _():
        rim(1).wait_send()

    @pl.when(tz > 0)
    def _():
        rim(0).wait_send()

    everyone = list_ref.at[pl.ds(0, TILES - 1)]
    pltpu.make_async_copy(everyone, everyone, gsend).wait()
    pltpu.make_async_copy(everyone, everyone, grecv).wait()


def stencil(src, dst, base, coef, hx_ref, hy_ref, hz_ref, lo, hi, y0, nk, nh, scale):
    rk, rh, h0 = 8 * nk, 8 * nh, y0 - 1
    hr, hy_rows, kr, kl = pl.ds(h0, rh), pl.ds(y0, rh), pl.ds(y0, rk), pl.ds(h0, rk)

    def swirl(x):
        vx, vy, vz = src[0, x, hr, :], src[1, x, hr, :], src[2, x, hr, :]
        vyz, vxz = pltpu.roll(vy, 127, 1), pltpu.roll(vx, 127, 1)
        hx_ref[x, hr, :] = (src[2, x, hy_rows, :] - vz) - (vyz - vy)
        hy_ref[x, hr, :] = (vxz - vx) - (src[2, x + 1, hr, :] - vz)
        hz_ref[x, hr, :] = (src[1, x + 1, hr, :] - vy) - (src[0, x, hy_rows, :] - vx)

    def relax(x):
        hx, hy, hz = hx_ref[x, kr, :], hy_ref[x, kr, :], hz_ref[x, kr, :]
        kx = (hz - hz_ref[x, kl, :]) - (hy - pltpu.roll(hy, 1, 1))
        ky = (hx - pltpu.roll(hx, 1, 1)) - (hz - hz_ref[x - 1, kr, :])
        kz = (hy - hy_ref[x - 1, kr, :]) - (hx - hx_ref[x, kl, :])
        c = coef[x, kr, :]
        keep = 1.0 + 4.0 * c
        for i, k in enumerate((kx, ky, kz)):
            new = keep * src[i, x, kr, :] - c * k
            if base is not None:
                new = base[i, x, kr, :] + scale * new
            dst[i, x, kr, :] = new

    swirl(lo - 1)
    swirl(lo)

    def body(x, c):
        relax(x)
        swirl(x + 1)
        return c

    lax.fori_loop(lo, hi, body, 0)


def relax_kernel(list_ref, lap_ref, coef_hbm, cond_hbm, field_hbm, out_ref,
                 u, p, q, hx_ref, hy_ref, hz_ref, coef, cond, field, spots, vals, val_s, cnt_s,
                 sems, cnt_v):
    t = lax.axis_index("tile")
    tx, ty, tz = place(t)
    loads = [pltpu.make_async_copy(a, b, sems.at[n])
             for n, (a, b) in enumerate(((coef_hbm, coef), (cond_hbm, cond), (field_hbm, field)))]
    for copy in loads:
        copy.start()

    flat = u.reshape(3, PLANES * YR, 128)

    def clear(i, c):
        for k in range(3):
            u[k, i] = jnp.zeros((YR, 128), F32)
        return c

    lax.fori_loop(0, PLANES, clear, 0)

    before = (iota((128, 128), 0) < iota((128, 128), 1)).astype(F32).astype(BF16)
    for half in range(2):
        code = list_ref[:, 4 * half + 3, :].astype(I32)
        x = (code >> 16) - tx * CX + RIM
        y = ((code >> 9) & 127) - ty * CY + RIM
        z = (code & 511) - tz * CZ
        ok = (x >= 0) & (x < CX + 2 * RIM) & (y >= 0) & (y < CY + 2 * RIM) & (z >= -RIM) & (z < CZ + RIM)
        run = (x >= RUN).astype(I32) + (x >= 2 * RUN).astype(I32)
        in_a = (z >= 0) & (z < CZ)
        plane = jnp.where(in_a, x + 1, x - RUN * run + B0)
        lane = jnp.where(in_a, z, SEG * run + jnp.where(z < 0, z + 7, z - 93))
        spot = (plane * YR + y + 1) * 128 + lane
        flag = ok.astype(F32)
        rank = jnp.dot(flag.astype(BF16), before, preferred_element_type=F32)
        spots[half, 0] = jnp.where(ok, spot, 0).astype(F32)
        spots[half, 1] = jnp.where(ok, rank, -1.0)
        cnt_v[half] = jnp.broadcast_to(jnp.sum(flag, axis=1, keepdims=True), (TILES, 128)).astype(I32)
    place_k = iota((128, 128), 0).astype(F32)

    def squeeze(b, c):
        for half in range(2):
            values = list_ref[b, pl.ds(4 * half, 3), :]
            both = jnp.concatenate([values, spots[half, 0, pl.ds(b, 1), :]], axis=0)
            pick = (place_k == spots[half, 1, pl.ds(b, 1), :]).astype(F32).astype(BF16)
            got = jnp.zeros((4, 128), F32)
            for part in three(both):
                got = got + lax.dot_general(part, pick, (((1,), (1,)), ((), ())), preferred_element_type=F32)
            vals[2 * b + half] = jnp.concatenate([got, jnp.zeros((4, 128), F32)], axis=0)
        return c

    lax.fori_loop(0, TILES, squeeze, 0)
    to_s = [pltpu.make_async_copy(vals, val_s, sems.at[3]), pltpu.make_async_copy(cnt_v, cnt_s, sems.at[4])]
    for copy in to_s:
        copy.start()
    for copy in to_s:
        copy.wait()
    lane_id = iota((1, 128), 1)

    def drop(b, c):
        def one(k, c2):
            spot = val_s[b, 3, k].astype(I32)
            row, lane = spot >> 7, spot & 127
            here = lane_id == lane
            for i in range(3):
                flat[i, pl.ds(row, 1), :] += jnp.where(here, val_s[b, i, k], 0.0)
            return c2

        lax.fori_loop(0, cnt_s[b % 2, b // 2, 0], one, 0)
        return c

    lax.fori_loop(0, 2 * TILES, drop, 0)
    loads[0].wait()

    def scale_b(s, c):
        for i in range(3):
            value = pack_own(lambda k: u[i, k], s, YR, ((7, 21, 7), (21, 35, -93))) + u[i, B0 + s]
            u[i, B0 + s] = 0.5 * coef[B0 + s] * value
        return c

    lax.fori_loop(0, RUN, scale_b, 0)

    def scale_a(k, c):
        for i in range(3):
            u[i, k] = 0.5 * coef[k] * u[i, k]
        return c

    lax.fori_loop(0, 80, scale_a, 0)

    plan = [(u, p, u, 0.5), (p, q, None, 1.0), (q, u, p, 0.25), (u, p, None, 1.0), (p, q, None, 1.0),
            (q, p, None, 1.0), (p, q, u, 0.0625)]
    for n, (src, dst, base, scale) in enumerate(plan):
        e = RIM - 1 - n
        nk, nh = -(-(CY + 2 * e) // 8), -(-(CY + 1 + 2 * e) // 8)
        for i in range(3):
            src[i, B0 - 1] = pltpu.roll(src[i, B0 + RUN - 1], SEG, 1)
            src[i, B0 + RUN] = pltpu.roll(src[i, B0], 128 - SEG, 1)
        stencil(src, dst, base, coef, hx_ref, hy_ref, hz_ref, B0, B0 + RUN, 8 - e, nk, nh, scale)
        stencil(src, dst, base, coef, hx_ref, hy_ref, hz_ref, OWN - e, OWN + CX + e, 8 - e, nk, nh, scale)

    loads[1].wait()
    loads[2].wait()
    lane = iota((CY, 128), 1)
    own_y = pl.ds(8, CY)
    lap = lap_ref[0]
    for g, (begin, end) in enumerate(((0, 19), (19, 45), (45, 64))):
        def combine(x, c, g=g):
            total = jnp.zeros((CY, 128), F32)
            for i in range(3):
                rims = q[i, B0 + x + RIM - RUN * g, own_y, :]
                value = jnp.where(lane < RIM, pltpu.roll(rims, (-(SEG * g + 7)) % 128, 1),
                                  jnp.where(lane >= CZ - RIM, pltpu.roll(rims, (93 - SEG * g) % 128, 1),
                                            q[i, OWN + x, own_y, :]))
                total = total + field[i, x].astype(F32) * value
            out_ref[x] = -lap * cond[x] * total
            return c

        lax.fori_loop(begin, end, combine, 0)


def spread_kernel(part_ref, out_ref, send, recv, lsem):
    f, t = lax.axis_index("freq"), lax.axis_index("tile")
    me = f * TILES + t
    barrier = pltpu.get_barrier_semaphore()

    def peer(i):
        d = (me + i) % (2 * TILES)
        return d // TILES, d % TILES

    def greet(i, c):
        pl.semaphore_signal(barrier, inc=1, device_id=peer(i), device_id_type=MESH)
        return c

    lax.fori_loop(1, 2 * TILES, greet, 0)
    mine = pltpu.make_async_copy(part_ref.at[t, pl.ds(f * 16, 16)], out_ref.at[me], lsem)
    mine.start()
    pl.semaphore_wait(barrier, 2 * TILES - 1)

    def share(i, c):
        df, dt = peer(i)
        pltpu.make_async_remote_copy(part_ref.at[dt, pl.ds(df * 16, 16)], out_ref.at[me], send, recv,
                                     device_id=(df, dt), device_id_type=MESH).start()
        return c

    lax.fori_loop(1, 2 * TILES, share, 0)
    mine.wait()
    others = out_ref.at[pl.ds(0, 2 * TILES - 1)]
    for sem in (send, recv):
        pltpu.make_async_copy(others, others, sem).wait()


def local(residual, row_counts, recv_owner, recv_cell, conductivity, laplace, forward_field):
    owner = recv_owner[:, 0]
    gx = (owner // (TY * TZ)) * CX + recv_cell // (CY * CZ)
    gy = (owner // TZ % TY) * CY + recv_cell // CZ % CY
    gz = (owner % TZ) * CZ + recv_cell % CZ
    codes = ((gx * (TY * CY) + gy) * (TZ * CZ) + gz).astype(F32)[None]
    smem = pl.BlockSpec(memory_space=pltpu.SMEM)
    cond = conductivity[0]
    lists, coef = pl.pallas_call(
        gather_kernel,
        name="gather_lists",
        out_shape=(jax.ShapeDtypeStruct((TILES, 8, 128), F32), jax.ShapeDtypeStruct((PLANES, YR, 128), F32)),
        in_specs=[vmem(), vmem(), vmem(), smem, hbm()],
        out_specs=(vmem(), vmem()),
        scratch_shapes=[
            pltpu.VMEM((80, 48, 128), F32),
            pltpu.VMEM((RUN, 48, 128), F32),
            pltpu.VMEM((RUN, 48, 128), F32),
            pltpu.VMEM((RUN, 48, 128), F32),
            pltpu.SemaphoreType.DMA((8,)),
            pltpu.SemaphoreType.DMA((8,)),
            pltpu.SemaphoreType.DMA((2,)),
            pltpu.SemaphoreType.DMA((2,)),
            pltpu.SemaphoreType.DMA,
            pltpu.SemaphoreType.DMA,
            pltpu.SemaphoreType.DMA,
        ],
        compiler_params=pltpu.CompilerParams(collective_id=0, has_side_effects=True, vmem_limit_bytes=32 * 2**20),
    )(residual, row_counts, codes, laplace, cond)
    partial = pl.pallas_call(
        relax_kernel,
        name="relax_tile",
        out_shape=jax.ShapeDtypeStruct((CX, CY, CZ), F32),
        in_specs=[vmem(), smem, hbm(), hbm(), hbm()],
        out_specs=vmem(),
        scratch_shapes=[pltpu.VMEM((3, PLANES, YR, 128), F32)] * 3
        + [pltpu.VMEM((PLANES, YR, 128), F32)] * 4
        + [
            pltpu.VMEM((CX, CY, CZ), F32),
            pltpu.VMEM((3, CX, CY, CZ), BF16),
            pltpu.VMEM((2, 2, TILES, 128), F32),
            pltpu.VMEM((2 * TILES, 8, 128), F32),
            pltpu.SMEM((2 * TILES, 8, 128), F32),
            pltpu.SMEM((2, TILES, 128), I32),
            pltpu.SemaphoreType.DMA((5,)),
            pltpu.VMEM((2, TILES, 128), I32),
        ],
        compiler_params=pltpu.CompilerParams(vmem_limit_bytes=58 * 2**20),
    )(lists, laplace, coef, cond, forward_field[0, 0])
    both = pl.pallas_call(
        spread_kernel,
        name="spread_rows",
        out_shape=jax.ShapeDtypeStruct((2 * TILES, 16, CZ), F32),
        in_specs=[hbm()],
        out_specs=hbm(),
        scratch_shapes=[pltpu.SemaphoreType.DMA] * 3,
        compiler_params=pltpu.CompilerParams(collective_id=1, has_side_effects=True),
    )(partial)
    return (both[:TILES] + both[TILES:])[:, None]


def solution(mesh):
    placed = (
        P("freq", None, "tile"),
        P("tile", None),
        P("tile", None),
        P("tile"),
        P("tile", None, None, None),
        P("freq"),
        P("freq", "tile", None, None, None, None),
    )
    return jax.shard_map(
        local, mesh=mesh, in_specs=placed, out_specs=P(None, "tile", "freq", None), check_vma=False
    )
```

```python
import functools

import jax
import jax.numpy as jnp
from jax import lax
from jax.experimental import pallas as pl
from jax.experimental.pallas import tpu as pltpu
from jax.sharding import PartitionSpec as P

F32 = jnp.float32
BF16 = jnp.bfloat16
I32 = jnp.int32
MESH = pl.DeviceIdType.MESH

TX, TY, TZ = 4, 4, 4
TILES = 64
CX, CY, CZ = 64, 32, 128
NP = 4
RIM = 7

YR = 56
B0 = 81
RUN = 26
SEG = 42
PLANES = 116
OWN = 8


def iota(shape, dim):
    return lax.broadcasted_iota(I32, shape, dim)


def vmem():
    return pl.BlockSpec(memory_space=pltpu.VMEM)


def hbm():
    return pl.BlockSpec(memory_space=pl.ANY)


def place(t):
    return t // (TY * TZ), (t // TZ) % TY, t % TZ


def three(value):
    hi = value.astype(BF16)
    rest = value - hi.astype(F32)
    mid = rest.astype(BF16)
    low = (rest - mid.astype(F32)).astype(BF16)
    return hi, mid, low


def pack_own(read, s, rows, moves):
    lane = iota((rows, 128), 1)
    total = jnp.zeros((rows, 128), F32)
    for g in range(3):
        plane = read(1 + RUN * g + s)
        for begin, end, shift in moves:
            moved = pltpu.roll(plane, (SEG * g + shift) % 128, 1)
            total = jnp.where((lane >= SEG * g + begin) & (lane < SEG * g + end), moved, total)
    return total


def locate(code, tx, ty, tz):
    x = (code >> 16) - tx * CX + RIM
    y = ((code >> 9) & 127) - ty * CY + RIM
    z = (code & 511) - tz * CZ
    ok = (x >= 0) & (x < CX + 2 * RIM) & (y >= 0) & (y < CY + 2 * RIM) & (z >= -RIM) & (z < CZ + RIM)
    run = (x >= RUN).astype(I32) + (x >= 2 * RUN).astype(I32)
    in_a = (z >= 0) & (z < CZ)
    plane = jnp.where(in_a, x + 1, x - RUN * run + B0)
    lane = jnp.where(in_a, z, SEG * run + jnp.where(z < 0, z + 7, z - 93))
    return ok, jnp.where(ok, (plane * YR + y + 1) * 128 + lane, 0).astype(F32)


def find_all(list_ref, spots, t):
    code = jnp.concatenate([list_ref[:, 3, :], list_ref[:, 7, :]], axis=1).astype(I32)
    ok, spot = locate(code, *place(t))
    before = (iota((256, 256), 0) < iota((256, 256), 1)).astype(F32).astype(BF16)
    flag = ok.astype(F32)
    rank = jnp.dot(flag.astype(BF16), before, preferred_element_type=F32)
    spots[0] = spot
    spots[1] = jnp.where(ok, rank, -1.0)
    return jnp.broadcast_to(jnp.sum(flag, axis=1, keepdims=True), (TILES, 128)).astype(I32)


def squeeze(list_ref, spots, b, first):
    place_k = iota((128, 256), 0).astype(F32)
    values = jnp.concatenate([list_ref[b, pl.ds(0, 3), :], list_ref[b, pl.ds(4, 3), :]], axis=1)
    both = jnp.concatenate([values, spots[0, pl.ds(b, 1), :]], axis=0)
    pick = (place_k == spots[1, pl.ds(b, 1), :] - first).astype(F32).astype(BF16)
    parts = jnp.concatenate([part.astype(F32) for part in three(both)] + [jnp.zeros((4, 256), F32)], axis=0).astype(BF16)
    got = lax.dot_general(parts, pick, (((1,), (1,)), ((), ())), preferred_element_type=F32)
    return (got[0:4] + got[4:8]) + got[8:12]


def gather_kernel(res_hbm, cnt_hbm, idx_hbm, lap_ref, cond_ref, list_ref, coef_ref, short_ref, many_ref,
                  res_ref, cnt_ref, idx_ref, spots, cext, pack, low, high, sends, recvs, zsend, zrecv, gsend, grecv, lsem):
    f, t = lax.axis_index("freq"), lax.axis_index("tile")
    tx, ty, tz = place(t)
    barrier = pltpu.get_barrier_semaphore()

    def greet(i, c):
        pl.semaphore_signal(barrier, inc=1, device_id=(f, (t + i) % TILES), device_id_type=MESH)
        return c

    lax.fori_loop(1, TILES, greet, 0)
    own = pltpu.make_async_copy(cond_ref, cext.at[pl.ds(OWN, CX), pl.ds(8, CY)], lsem.at[0])
    own.start()
    loads = [pltpu.make_async_copy(a, b, lsem.at[n + 1])
             for n, (a, b) in enumerate(((res_hbm, res_ref), (cnt_hbm, cnt_ref), (idx_hbm, idx_ref)))]
    for copy in loads:
        copy.start()
    for copy in loads:
        copy.wait()

    counts = cnt_ref[...].astype(F32)
    upto = (iota((256, 256), 0) <= iota((256, 256), 1)).astype(F32)
    ends = jnp.dot(jnp.broadcast_to(counts, (8, 256)).astype(BF16), upto.astype(BF16), preferred_element_type=F32)[0:1]
    starts = ends - counts
    at = iota((1024, 256), 0).astype(F32)
    member = ((at >= starts) & (at < ends)).astype(F32).astype(BF16)
    sums = jnp.zeros((3, 256), F32)
    for part in three(res_ref[0]):
        sums = sums + jnp.dot(part, member, preferred_element_type=F32)
    means = sums / counts
    both = jnp.concatenate([means, idx_ref[...]], axis=0)
    list_ref[t] = jnp.concatenate([both[:, :128], both[:, 128:]], axis=0)

    pl.semaphore_wait(barrier, TILES - 1)

    def share(i, c):
        pltpu.make_async_remote_copy(list_ref.at[t], list_ref.at[t], gsend, grecv,
                                     device_id=(f, (t + i) % TILES), device_id_type=MESH).start()
        return c

    lax.fori_loop(1, TILES, share, 0)

    spans = {1: (CX - 7, 1, 7), -1: (0, 72, 7), 0: (0, 8, CX)}
    rows = {1: (CY - 7, 1, 7), -1: (0, 40, 7), 0: (0, 8, CY)}
    ways = [(dx, dy) for dx in (-1, 0, 1) for dy in (-1, 0, 1) if (dx, dy) != (0, 0)]

    def inside(dx, dy):
        x, y = tx + dx, ty + dy
        return (x >= 0) & (x < TX) & (y >= 0) & (y < TY)

    def halo(n):
        dx, dy = ways[n]
        xs, xd, xn = spans[dx]
        ys, yd, yn = rows[dy]
        return pltpu.make_async_remote_copy(
            cond_ref.at[pl.ds(xs, xn), pl.ds(ys, yn)], cext.at[pl.ds(xd, xn), pl.ds(yd, yn)],
            sends.at[n], recvs.at[n], device_id=(f, t + dx * TY * TZ + dy * TZ), device_id_type=MESH)

    for n, (dx, dy) in enumerate(ways):
        @pl.when(inside(dx, dy))
        def _(n=n):
            halo(n).start()

    everyone = list_ref.at[pl.ds(0, TILES - 1)]
    pltpu.make_async_copy(everyone, everyone, grecv).wait()
    many_ref[...] = find_all(list_ref, spots, t)

    def compact(k, c):
        for i in range(2):
            parts = [squeeze(list_ref, spots, 4 * k + 2 * i + j, 0.0) for j in range(2)]
            short_ref[2 * k + i] = jnp.concatenate(parts, axis=0)
        return c

    lax.fori_loop(0, TILES // 4, compact, 0)
    own.wait()
    for n, (dx, dy) in enumerate(ways):
        @pl.when(inside(-dx, -dy))
        def _(n=n):
            halo(n).wait_recv()

    def read(i):
        return cext[i]

    lane = iota((48, 128), 1)

    def fill(s, c):
        total = jnp.zeros((48, 128), F32)
        for h in range(8):
            plane = cext[jnp.minimum(1 + 10 * h + s, 79)]
            for begin, shift in ((16 * h, 16 * h - 121), (16 * h + 8, 16 * h + 8)):
                moved = pltpu.roll(plane, shift % 128, 1)
                total = jnp.where((lane >= begin) & (lane < begin + 7), moved, total)
        pack[s] = total
        return c

    lax.fori_loop(0, 10, fill, 0)

    def rim(up):
        return pltpu.make_async_remote_copy(
            pack, low if up else high, zsend.at[up], zrecv.at[up],
            device_id=(f, t + (1 if up else -1)), device_id_type=MESH)

    @pl.when(tz < TZ - 1)
    def _():
        rim(1).start()

    @pl.when(tz > 0)
    def _():
        rim(0).start()

    lap = lap_ref[0]
    yrow = iota((48, 128), 0) - 8
    yin = (yrow + ty * CY >= 0) & (yrow + ty * CY < TY * CY)

    def fill_a(i, c):
        x = i - 8 + tx * CX
        good = yin & (x >= 0) & (x < TX * CX)
        coef_ref[i, pl.ds(0, 48), :] = jnp.where(good, 1.0 / (4.0 + lap * cext[i]), 0.0)
        return c

    lax.fori_loop(0, 80, fill_a, 0)

    @pl.when(tz > 0)
    def _():
        rim(1).wait_recv()

    @pl.when(tz < TZ - 1)
    def _():
        rim(0).wait_recv()

    run = (lane >= SEG).astype(I32) + (lane >= 2 * SEG).astype(I32)
    seg = lane - run * SEG
    z = jnp.where(seg < 21, seg - 7, seg + 93) + tz * CZ
    zin = (z >= 0) & (z < TZ * CZ) & (lane < 3 * SEG)

    def fill_b(s, c):
        value = pack_own(read, s, 48, ((7, 21, 7), (21, 35, -93)))
        for g in range(3):
            i = RUN * g + s
            h = i // 10
            turn = (SEG * g - 16 * h + 256) % 128
            from_low = pltpu.roll(low[i - 10 * h], turn, 1)
            from_high = pltpu.roll(high[i - 10 * h], (turn + 27) % 128, 1)
            value = jnp.where((lane >= SEG * g) & (lane < SEG * g + 7), from_low, value)
            value = jnp.where((lane >= SEG * g + 35) & (lane < SEG * g + 42), from_high, value)
        x = RUN * run + s - 7 + tx * CX
        good = yin & zin & (x >= 0) & (x < TX * CX)
        coef_ref[B0 + s, pl.ds(0, 48), :] = jnp.where(good, 1.0 / (4.0 + lap * value), 0.0)
        return c

    lax.fori_loop(0, RUN, fill_b, 0)

    for n, (dx, dy) in enumerate(ways):
        @pl.when(inside(dx, dy))
        def _(n=n):
            halo(n).wait_send()

    @pl.when(tz < TZ - 1)
    def _():
        rim(1).wait_send()

    @pl.when(tz > 0)
    def _():
        rim(0).wait_send()

    pltpu.make_async_copy(everyone, everyone, gsend).wait()


def stencil(src, dst, base, coef, hx_ref, hy_ref, hz_ref, lo, hi, y0, nk, nh, scale):
    rk, rh, h0 = 8 * nk, 8 * nh, y0 - 1
    hr, hy_rows, kr, kl = pl.ds(h0, rh), pl.ds(y0, rh), pl.ds(y0, rk), pl.ds(h0, rk)

    def swirl(x):
        vx, vy, vz = src[0, x, hr, :], src[1, x, hr, :], src[2, x, hr, :]
        vyz, vxz = pltpu.roll(vy, 127, 1), pltpu.roll(vx, 127, 1)
        hx_ref[x, hr, :] = (src[2, x, hy_rows, :] - vz) - (vyz - vy)
        hy_ref[x, hr, :] = (vxz - vx) - (src[2, x + 1, hr, :] - vz)
        hz_ref[x, hr, :] = (src[1, x + 1, hr, :] - vy) - (src[0, x, hy_rows, :] - vx)

    def relax(x):
        hx, hy, hz = hx_ref[x, kr, :], hy_ref[x, kr, :], hz_ref[x, kr, :]
        kx = (hz - hz_ref[x, kl, :]) - (hy - pltpu.roll(hy, 1, 1))
        ky = (hx - pltpu.roll(hx, 1, 1)) - (hz - hz_ref[x - 1, kr, :])
        kz = (hy - hy_ref[x - 1, kr, :]) - (hx - hx_ref[x, kl, :])
        c = coef[x, kr, :] if scale == 1.0 else scale * coef[x, kr, :]
        keep = (scale if base is not src else 1.0 + scale) + 4.0 * c
        for i, k in enumerate((kx, ky, kz)):
            new = keep * src[i, x, kr, :] - c * k
            if base is not None and base is not src:
                new = base[i, x, kr, :] + new
            dst[i, x, kr, :] = new

    for i in range(-1, NP):
        swirl(lo + i)

    def body(k, c):
        x = jnp.minimum(lo + NP * k, hi - NP)
        for i in range(NP):
            relax(x + i)
        for i in range(NP):
            swirl(x + NP + i)
        return c

    lax.fori_loop(0, (hi - lo + NP - 1) // NP, body, 0)


def relax_kernel(list_hbm, lap_ref, short_s, many_s, coef_hbm, cond_hbm, field_hbm, out_ref,
                 u, p, q, hx_ref, hy_ref, hz_ref, coef, cond, field, list_ref, spots, more, more_s, sems):
    t = lax.axis_index("tile")
    loads = [pltpu.make_async_copy(a, b, sems.at[n])
             for n, (a, b) in enumerate(((coef_hbm, coef), (cond_hbm, cond), (field_hbm, field)))]
    for copy in loads:
        copy.start()

    flat = u.reshape(3, PLANES * YR, 128)

    def clear(i, c):
        for k in range(3):
            u[k, i] = jnp.zeros((YR, 128), F32)
        return c

    lax.fori_loop(0, PLANES, clear, 0)
    lane_id = iota((1, 128), 1)

    def add(ref, j, at, count):
        def four(k, c):
            rows, gains = [], []
            for i in range(4):
                spot = ref[j, at + 3, 4 * k + i].astype(I32)
                rows.append(spot >> 7)
                here = lane_id == (spot & 127)
                gains.append([jnp.where(here, ref[j, at + n, 4 * k + i], 0.0) for n in range(3)])
            held = [[flat[n, pl.ds(row, 1), :] for n in range(3)] for row in rows]
            for i in range(4):
                for n in range(3):
                    total = held[i][n] + gains[i][n]
                    for m in range(i):
                        total = total + jnp.where(rows[m] == rows[i], gains[m][n], 0.0)
                    held[i][n] = total
            for i in range(4):
                for n in range(3):
                    flat[n, pl.ds(rows[i], 1), :] = held[i][n]
            return c

        lax.fori_loop(0, (count + 3) // 4, four, 0)

    def drop(k, most):
        for i in range(2):
            count = many_s[2 * k + i, 0]
            add(short_s, k, 4 * i, jnp.minimum(count, 128))
            most = jnp.maximum(most, count)
        return most

    most = lax.fori_loop(0, TILES // 2, drop, 0)

    @pl.when(most > 128)
    def _():
        copy = pltpu.make_async_copy(list_hbm, list_ref, sems.at[3])
        copy.start()
        copy.wait()
        find_all(list_ref, spots, t)

        def rest(b, c):
            count = many_s[b, 0] - 128

            @pl.when(count > 0)
            def _():
                more[0] = jnp.concatenate([squeeze(list_ref, spots, b, 128.0), jnp.zeros((4, 128), F32)], axis=0)
                copy = pltpu.make_async_copy(more, more_s, sems.at[3])
                copy.start()
                copy.wait()
                add(more_s, 0, 0, count)

            return c

        lax.fori_loop(0, TILES, rest, 0)

    loads[0].wait()

    def scale_b(s, c):
        for i in range(3):
            value = pack_own(lambda k: u[i, k, pl.ds(0, 48), :], s, 48, ((7, 21, 7), (21, 35, -93))) + u[i, B0 + s, pl.ds(0, 48), :]
            u[i, B0 + s, pl.ds(0, 48), :] = 0.5 * coef[B0 + s, pl.ds(0, 48), :] * value
        return c

    lax.fori_loop(0, RUN, scale_b, 0)

    def scale_a(k, c):
        for i in range(3):
            u[i, k] = 0.5 * coef[k] * u[i, k]
        return c

    lax.fori_loop(0, 80, scale_a, 0)

    plan = [(u, p, u, 0.5), (p, q, None, 1.0), (q, u, p, 0.25), (u, p, None, 1.0), (p, q, None, 1.0),
            (q, p, None, 1.0), (p, q, u, 0.0625)]
    for n, (src, dst, base, scale) in enumerate(plan):
        e = RIM - 1 - n
        nk, nh = -(-(CY + 2 * e) // 8), -(-(CY + 1 + 2 * e) // 8)
        for i in range(3):
            src[i, B0 - 1] = pltpu.roll(src[i, B0 + RUN - 1], SEG, 1)
            src[i, B0 + RUN] = pltpu.roll(src[i, B0], 128 - SEG, 1)
        stencil(src, dst, base, coef, hx_ref, hy_ref, hz_ref, B0, B0 + RUN, 8 - e, nk, nh, scale)
        stencil(src, dst, base, coef, hx_ref, hy_ref, hz_ref, OWN - e, OWN + CX + e, 8 - e, nk, nh, scale)

    loads[1].wait()
    loads[2].wait()
    lane = iota((CY, 128), 1)
    own_y = pl.ds(8, CY)
    lap = lap_ref[0]
    for g, (begin, end) in enumerate(((0, 19), (19, 45), (45, 64))):
        def combine(x, c, g=g):
            total = jnp.zeros((CY, 128), F32)
            for i in range(3):
                rims = q[i, B0 + x + RIM - RUN * g, own_y, :]
                value = jnp.where(lane < RIM, pltpu.roll(rims, (-(SEG * g + 7)) % 128, 1),
                                  jnp.where(lane >= CZ - RIM, pltpu.roll(rims, (93 - SEG * g) % 128, 1),
                                            q[i, OWN + x, own_y, :]))
                total = total + field[i, x].astype(F32) * value
            out_ref[x] = -lap * cond[x] * total
            return c

        lax.fori_loop(begin, end, combine, 0)


def spread_kernel(part_ref, out_ref, send, recv, lsem):
    f, t = lax.axis_index("freq"), lax.axis_index("tile")
    me = f * TILES + t
    barrier = pltpu.get_barrier_semaphore()

    def peer(i):
        d = (me + i) % (2 * TILES)
        return d // TILES, d % TILES

    def greet(i, c):
        pl.semaphore_signal(barrier, inc=1, device_id=peer(i), device_id_type=MESH)
        return c

    lax.fori_loop(1, 2 * TILES, greet, 0)
    mine = pltpu.make_async_copy(part_ref.at[t, pl.ds(f * 16, 16)], out_ref.at[me], lsem)
    mine.start()
    pl.semaphore_wait(barrier, 2 * TILES - 1)

    def share(i, c):
        df, dt = peer(i)
        pltpu.make_async_remote_copy(part_ref.at[dt, pl.ds(df * 16, 16)], out_ref.at[me], send, recv,
                                     device_id=(df, dt), device_id_type=MESH).start()
        return c

    lax.fori_loop(1, 2 * TILES, share, 0)
    mine.wait()
    others = out_ref.at[pl.ds(0, 2 * TILES - 1)]
    for sem in (send, recv):
        pltpu.make_async_copy(others, others, sem).wait()


def local(residual, row_counts, recv_owner, recv_cell, conductivity, laplace, forward_field):
    owner = recv_owner[:, 0]
    gx = (owner // (TY * TZ)) * CX + recv_cell // (CY * CZ)
    gy = (owner // TZ % TY) * CY + recv_cell // CZ % CY
    gz = (owner % TZ) * CZ + recv_cell % CZ
    codes = ((gx * (TY * CY) + gy) * (TZ * CZ) + gz).astype(F32)[None]
    smem = pl.BlockSpec(memory_space=pltpu.SMEM)
    cond = conductivity[0]
    lists, coef, short, many = pl.pallas_call(
        gather_kernel,
        name="gather_lists",
        out_shape=(jax.ShapeDtypeStruct((TILES, 8, 128), F32), jax.ShapeDtypeStruct((PLANES, YR, 128), F32),
                   jax.ShapeDtypeStruct((TILES // 2, 8, 128), F32), jax.ShapeDtypeStruct((TILES, 128), I32)),
        in_specs=[hbm(), hbm(), hbm(), smem, hbm()],
        out_specs=(vmem(), vmem(), vmem(), vmem()),
        scratch_shapes=[
            pltpu.VMEM((1, 3, 1024), F32),
            pltpu.VMEM((1, 256), I32),
            pltpu.VMEM((1, 256), F32),
            pltpu.VMEM((2, TILES, 256), F32),
            pltpu.VMEM((80, 48, 128), F32),
            pltpu.VMEM((10, 48, 128), F32),
            pltpu.VMEM((10, 48, 128), F32),
            pltpu.VMEM((10, 48, 128), F32),
            pltpu.SemaphoreType.DMA((8,)),
            pltpu.SemaphoreType.DMA((8,)),
            pltpu.SemaphoreType.DMA((2,)),
            pltpu.SemaphoreType.DMA((2,)),
            pltpu.SemaphoreType.DMA,
            pltpu.SemaphoreType.DMA,
            pltpu.SemaphoreType.DMA((4,)),
        ],
        compiler_params=pltpu.CompilerParams(collective_id=0, has_side_effects=True, vmem_limit_bytes=32 * 2**20),
    )(residual, row_counts, codes, laplace, cond)
    partial = pl.pallas_call(
        relax_kernel,
        name="relax_tile",
        out_shape=jax.ShapeDtypeStruct((CX, CY, CZ), F32),
        in_specs=[hbm(), smem, smem, smem, hbm(), hbm(), hbm()],
        out_specs=vmem(),
        scratch_shapes=[pltpu.VMEM((3, PLANES, YR, 128), F32)] * 3
        + [pltpu.VMEM((PLANES, YR, 128), F32)] * 4
        + [
            pltpu.VMEM((CX, CY, CZ), F32),
            pltpu.VMEM((3, CX, CY, CZ), BF16),
            pltpu.VMEM((TILES, 8, 128), F32),
            pltpu.VMEM((2, TILES, 256), F32),
            pltpu.VMEM((1, 8, 128), F32),
            pltpu.SMEM((1, 8, 128), F32),
            pltpu.SemaphoreType.DMA((4,)),
        ],
        compiler_params=pltpu.CompilerParams(vmem_limit_bytes=58 * 2**20),
    )(lists, laplace, short, many, coef, cond, forward_field[0, 0])
    both = pl.pallas_call(
        spread_kernel,
        name="spread_rows",
        out_shape=jax.ShapeDtypeStruct((2 * TILES, 16, CZ), F32),
        in_specs=[hbm()],
        out_specs=hbm(),
        scratch_shapes=[pltpu.SemaphoreType.DMA] * 3,
        compiler_params=pltpu.CompilerParams(collective_id=1, has_side_effects=True),
    )(partial)
    return (both[:TILES] + both[TILES:])[:, None]


def solution(mesh):
    placed = (
        P("freq", None, "tile"),
        P("tile", None),
        P("tile", None),
        P("tile"),
        P("tile", None, None, None),
        P("freq"),
        P("freq", "tile", None, None, None, None),
    )
    return jax.shard_map(
        local, mesh=mesh, in_specs=placed, out_specs=P(None, "tile", "freq", None), check_vma=False
    )
```

```python
import functools

import jax
import jax.numpy as jnp
from jax import lax
from jax.experimental import pallas as pl
from jax.experimental.pallas import tpu as pltpu
from jax.sharding import PartitionSpec as P

F32 = jnp.float32
BF16 = jnp.bfloat16
I32 = jnp.int32
MESH = pl.DeviceIdType.MESH

TX, TY, TZ = 4, 4, 4
TILES = 64
CX, CY, CZ = 64, 32, 128
NP = 4
RIM = 7

YR = 56
B0 = 81
RUN = 20
SEG = 28
RUNS = 4
ZB = CZ + RIM - SEG
PLANES = 108
KEEP = 64
OWN = 8


def iota(shape, dim):
    return lax.broadcasted_iota(I32, shape, dim)


def vmem():
    return pl.BlockSpec(memory_space=pltpu.VMEM)


def hbm():
    return pl.BlockSpec(memory_space=pl.ANY)


def place(t):
    return t // (TY * TZ), (t // TZ) % TY, t % TZ


def three(value):
    hi = value.astype(BF16)
    rest = value - hi.astype(F32)
    mid = rest.astype(BF16)
    low = (rest - mid.astype(F32)).astype(BF16)
    return hi, mid, low


def runs_of(read, s, rows, begin, end, shift):
    lane = iota((rows, 128), 1)
    total = jnp.zeros((rows, 128), F32)
    for g in range(RUNS):
        plane = read(1 + RUN * g + s)
        moved = pltpu.roll(plane, (SEG * g + shift) % 128, 1)
        total = jnp.where((lane >= SEG * g + begin) & (lane < SEG * g + end), moved, total)
    return total


def locate(code, tx, ty, tz):
    x = (code >> 16) - tx * CX + RIM
    y = ((code >> 9) & 127) - ty * CY + RIM
    z = (code & 511) - tz * CZ
    ok = (x >= 0) & (x < CX + 2 * RIM) & (y >= 0) & (y < CY + 2 * RIM) & (z >= -RIM) & (z < CZ + RIM)
    run = sum((x >= RUN * g).astype(I32) for g in range(1, RUNS))
    in_a = z < 128 - RIM
    plane = jnp.where(in_a, x + 1, x - RUN * run + B0)
    lane = jnp.where(in_a, z + RIM, SEG * run + z - ZB)
    return ok, jnp.where(ok, (plane * YR + y + 1) * 128 + lane, 0).astype(F32)


def find_all(list_ref, spots, t):
    code = jnp.concatenate([list_ref[:, 3, :], list_ref[:, 7, :]], axis=1).astype(I32)
    ok, spot = locate(code, *place(t))
    before = (iota((256, 256), 0) < iota((256, 256), 1)).astype(F32).astype(BF16)
    flag = ok.astype(F32)
    rank = jnp.dot(flag.astype(BF16), before, preferred_element_type=F32)
    spots[0] = spot
    spots[1] = jnp.where(ok, rank, -1.0)
    ones = jnp.ones((8, 256), BF16)
    return lax.dot_general(ones, flag.astype(BF16), (((1,), (1,)), ((), ())), preferred_element_type=F32).astype(I32)


def squeeze(list_ref, spots, b, first):
    place_k = iota((KEEP, 256), 0).astype(F32)
    values = jnp.concatenate([list_ref[b, pl.ds(0, 3), :], list_ref[b, pl.ds(4, 3), :]], axis=1)
    both = jnp.concatenate([values, spots[0, pl.ds(b, 1), :]], axis=0)
    pick = (place_k == spots[1, pl.ds(b, 1), :] - first).astype(F32).astype(BF16)
    parts = jnp.concatenate([part.astype(F32) for part in three(both)] + [jnp.zeros((4, 256), F32)], axis=0).astype(BF16)
    got = lax.dot_general(parts, pick, (((1,), (1,)), ((), ())), preferred_element_type=F32)
    return (got[0:4] + got[4:8]) + got[8:12]


def gather_kernel(res_hbm, cnt_hbm, idx_hbm, lap_ref, cond_ref, list_ref, coef_ref, short_ref, spot_ref, many_ref,
                  res_ref, cnt_ref, idx_ref, spots, cext, pack, low, high, sends, recvs, zsend, zrecv, gsend, grecv, lsem):
    f, t = lax.axis_index("freq"), lax.axis_index("tile")
    tx, ty, tz = place(t)
    barrier = pltpu.get_barrier_semaphore()

    def greet(i, c):
        pl.semaphore_signal(barrier, inc=1, device_id=(f, (t + i) % TILES), device_id_type=MESH)
        return c

    lax.fori_loop(1, TILES, greet, 0)
    own = pltpu.make_async_copy(cond_ref, cext.at[pl.ds(OWN, CX), pl.ds(8, CY)], lsem.at[0])
    own.start()
    loads = [pltpu.make_async_copy(a, b, lsem.at[n + 1])
             for n, (a, b) in enumerate(((res_hbm, res_ref), (cnt_hbm, cnt_ref), (idx_hbm, idx_ref)))]
    for copy in loads:
        copy.start()
    for copy in loads:
        copy.wait()

    counts = cnt_ref[...].astype(F32)
    upto = (iota((256, 256), 0) <= iota((256, 256), 1)).astype(F32)
    ends = jnp.dot(jnp.broadcast_to(counts, (8, 256)).astype(BF16), upto.astype(BF16), preferred_element_type=F32)[0:1]
    starts = ends - counts
    at = iota((1024, 256), 0).astype(F32)
    member = ((at >= starts) & (at < ends)).astype(F32).astype(BF16)
    sums = jnp.zeros((3, 256), F32)
    for part in three(res_ref[0]):
        sums = sums + jnp.dot(part, member, preferred_element_type=F32)
    means = sums / counts
    both = jnp.concatenate([means, idx_ref[...]], axis=0)
    list_ref[t] = jnp.concatenate([both[:, :128], both[:, 128:]], axis=0)

    pl.semaphore_wait(barrier, TILES - 1)

    def share(i, c):
        pltpu.make_async_remote_copy(list_ref.at[t], list_ref.at[t], gsend, grecv,
                                     device_id=(f, (t + i) % TILES), device_id_type=MESH).start()
        return c

    lax.fori_loop(1, TILES, share, 0)

    spans = {1: (CX - 7, 1, 7), -1: (0, 72, 7), 0: (0, 8, CX)}
    rows = {1: (CY - 7, 1, 7), -1: (0, 40, 7), 0: (0, 8, CY)}
    ways = [(dx, dy) for dx in (-1, 0, 1) for dy in (-1, 0, 1) if (dx, dy) != (0, 0)]

    def inside(dx, dy):
        x, y = tx + dx, ty + dy
        return (x >= 0) & (x < TX) & (y >= 0) & (y < TY)

    def halo(n):
        dx, dy = ways[n]
        xs, xd, xn = spans[dx]
        ys, yd, yn = rows[dy]
        return pltpu.make_async_remote_copy(
            cond_ref.at[pl.ds(xs, xn), pl.ds(ys, yn)], cext.at[pl.ds(xd, xn), pl.ds(yd, yn)],
            sends.at[n], recvs.at[n], device_id=(f, t + dx * TY * TZ + dy * TZ), device_id_type=MESH)

    for n, (dx, dy) in enumerate(ways):
        @pl.when(inside(dx, dy))
        def _(n=n):
            halo(n).start()

    everyone = list_ref.at[pl.ds(0, TILES - 1)]
    pltpu.make_async_copy(everyone, everyone, grecv).wait()
    many_ref[:, pl.ds(0, TILES)] = find_all(list_ref, spots, t)

    def compact(k, c):
        for i in range(2):
            pair = jnp.concatenate([squeeze(list_ref, spots, 4 * k + 2 * i + j, 0.0) for j in range(2)], axis=1)
            short_ref[pl.ds(3 * (2 * k + i), 3), :] = pair[0:3]
            spot_ref[pl.ds(2 * k + i, 1), :] = pair[3:4].astype(I32)
        return c

    lax.fori_loop(0, TILES // 4, compact, 0)
    spot = spot_ref[...]
    row, turn = spot >> 7, iota((TILES // 2, 128), 1) & 3
    clash = jnp.zeros((TILES // 2, 128), I32)
    for d in (1, 2, 3):
        same = (pltpu.roll(row, d, 1) == row) & (turn >= d) & (row > 0)
        clash = clash | same.astype(I32)
    for d in (126, 127):
        clash = clash | pltpu.roll(clash, d, 1)
    spot_ref[...] = jnp.where((turn == 0) & (clash > 0), spot + (1 << 24), spot)
    own.wait()
    for n, (dx, dy) in enumerate(ways):
        @pl.when(inside(-dx, -dy))
        def _(n=n):
            halo(n).wait_recv()

    def read(i):
        return cext[jnp.minimum(i, 79)]

    lane = iota((48, 128), 1)

    def fill(s, c):
        total = jnp.zeros((48, 128), F32)
        for h in range(8):
            plane = cext[jnp.minimum(1 + 10 * h + s, 79)]
            for begin, shift in ((16 * h, 16 * h - 121), (16 * h + 8, 16 * h + 8)):
                moved = pltpu.roll(plane, shift % 128, 1)
                total = jnp.where((lane >= begin) & (lane < begin + 7), moved, total)
        pack[s] = total
        return c

    lax.fori_loop(0, 10, fill, 0)

    def rim(up):
        return pltpu.make_async_remote_copy(
            pack, low if up else high, zsend.at[up], zrecv.at[up],
            device_id=(f, t + (1 if up else -1)), device_id_type=MESH)

    @pl.when(tz < TZ - 1)
    def _():
        rim(1).start()

    @pl.when(tz > 0)
    def _():
        rim(0).start()

    lap = lap_ref[0]
    yrow = iota((48, 128), 0) - 8
    yin = (yrow + ty * CY >= 0) & (yrow + ty * CY < TY * CY)

    @pl.when(tz > 0)
    def _():
        rim(1).wait_recv()

    def fill_a(i, c):
        k = jnp.clip(i - 1, 0, 79)
        x = i - 8 + tx * CX
        from_low = pltpu.roll(low[k % 10], (128 - 16 * (k // 10)) % 128, 1)
        value = jnp.where(lane < RIM, from_low, pltpu.roll(cext[i], RIM, 1))
        good = yin & ((lane >= RIM) | (tz > 0)) & (x >= 0) & (x < TX * CX)
        coef_ref[i, pl.ds(0, 48), :] = jnp.where(good, 1.0 / (4.0 + lap * value), 0.0)
        return c

    lax.fori_loop(0, 80, fill_a, 0)

    @pl.when(tz < TZ - 1)
    def _():
        rim(0).wait_recv()

    run = sum((lane >= SEG * g).astype(I32) for g in range(1, RUNS))
    z = lane - run * SEG + ZB
    zin = ((z < CZ) | (tz < TZ - 1)) & (lane < RUNS * SEG)

    def fill_b(s, c):
        value = runs_of(read, s, 48, 0, SEG - RIM, 128 - ZB)
        for g in range(RUNS):
            i = RUN * g + s
            from_high = pltpu.roll(high[i % 10], (SEG * g + SEG - RIM - 8 - 16 * (i // 10) + 256) % 128, 1)
            value = jnp.where((lane >= SEG * g + SEG - RIM) & (lane < SEG * g + SEG), from_high, value)
        x = RUN * run + s - 7 + tx * CX
        good = yin & zin & (x >= 0) & (x < TX * CX)
        coef_ref[B0 + s, pl.ds(0, 48), :] = jnp.where(good, 1.0 / (4.0 + lap * value), 0.0)
        return c

    lax.fori_loop(0, RUN, fill_b, 0)

    for n, (dx, dy) in enumerate(ways):
        @pl.when(inside(dx, dy))
        def _(n=n):
            halo(n).wait_send()

    @pl.when(tz < TZ - 1)
    def _():
        rim(1).wait_send()

    @pl.when(tz > 0)
    def _():
        rim(0).wait_send()

    pltpu.make_async_copy(everyone, everyone, gsend).wait()


def stencil(src, dst, base, coef, hx_ref, hy_ref, hz_ref, lo, hi, y0, nk, nh, scale):
    rk, rh, h0 = 8 * nk, 8 * nh, y0 - 1
    hr, hy_rows, kr, kl = pl.ds(h0, rh), pl.ds(y0, rh), pl.ds(y0, rk), pl.ds(h0, rk)

    def swirl(x):
        vx, vy, vz = src[0, x, hr, :], src[1, x, hr, :], src[2, x, hr, :]
        vyz, vxz = pltpu.roll(vy, 127, 1), pltpu.roll(vx, 127, 1)
        hx_ref[x, hr, :] = (src[2, x, hy_rows, :] - vz) - (vyz - vy)
        hy_ref[x, hr, :] = (vxz - vx) - (src[2, x + 1, hr, :] - vz)
        hz_ref[x, hr, :] = (src[1, x + 1, hr, :] - vy) - (src[0, x, hy_rows, :] - vx)

    def relax(x):
        hx, hy, hz = hx_ref[x, kr, :], hy_ref[x, kr, :], hz_ref[x, kr, :]
        kx = (hz - hz_ref[x, kl, :]) - (hy - pltpu.roll(hy, 1, 1))
        ky = (hx - pltpu.roll(hx, 1, 1)) - (hz - hz_ref[x - 1, kr, :])
        kz = (hy - hy_ref[x - 1, kr, :]) - (hx - hx_ref[x, kl, :])
        c = coef[x, kr, :] if scale == 1.0 else scale * coef[x, kr, :]
        keep = (scale if base is not src else 1.0 + scale) + 4.0 * c
        for i, k in enumerate((kx, ky, kz)):
            new = keep * src[i, x, kr, :] - c * k
            if base is not None and base is not src:
                new = base[i, x, kr, :] + new
            dst[i, x, kr, :] = new

    for i in range(-1, NP):
        swirl(lo + i)

    def body(k, c):
        x = jnp.minimum(lo + NP * k, hi - NP)
        for i in range(NP):
            relax(x + i)
        for i in range(NP):
            swirl(x + NP + i)
        return c

    lax.fori_loop(0, (hi - lo + NP - 1) // NP, body, 0)


def relax_kernel(list_hbm, lap_ref, short_s, spot_s, many_s, coef_hbm, cond_hbm, field_hbm, out_ref,
                 u, p, q, hx_ref, hy_ref, hz_ref, coef, cond, field, list_ref, spots, more, more_i, more_s, more_is, sems):
    t = lax.axis_index("tile")
    loads = [pltpu.make_async_copy(a, b, sems.at[n])
             for n, (a, b) in enumerate(((coef_hbm, coef), (cond_hbm, cond), (field_hbm, field)))]
    for copy in loads:
        copy.start()

    flat = u.reshape(3, PLANES * YR, 128)

    def clear(i, c):
        for k in range(3):
            u[k, i] = jnp.zeros((YR, 128), F32)
        return c

    lax.fori_loop(0, PLANES, clear, 0)
    lane_id = iota((1, 128), 1)

    def add(ref, spot_in, at, at_spot, step, count):
        def four(k, c):
            first, where = at + 4 * k, at_spot + 4 * k
            raw = [spot_in[where + i] for i in range(4)]
            clash = raw[0] >= 1 << 24
            raw[0] = raw[0] & ((1 << 24) - 1)
            rows = [value >> 7 for value in raw]
            here = [lane_id == (value & 127) for value in raw]
            gains = [[jnp.where(here[i], ref[first + n * step + i], 0.0) for n in range(3)] for i in range(4)]

            @pl.when(clash)
            def _():
                for i in range(4):
                    for n in range(3):
                        flat[n, pl.ds(rows[i], 1), :] += gains[i][n]

            @pl.when(jnp.logical_not(clash))
            def _():
                sums = [[flat[n, pl.ds(rows[i], 1), :] + gains[i][n] for n in range(3)] for i in range(4)]
                for i in range(4):
                    for n in range(3):
                        flat[n, pl.ds(rows[i], 1), :] = sums[i][n]

            return c

        lax.fori_loop(0, (count + 3) // 4, four, 0)

    def drop(k, most):
        for i in range(2):
            count = many_s[0, 2 * k + i]
            add(short_s, spot_s, 384 * k + KEEP * i, 128 * k + KEEP * i, 128, jnp.minimum(count, KEEP))
            most = jnp.maximum(most, count)
        return most

    most = lax.fori_loop(0, TILES // 2, drop, 0)

    @pl.when(most > KEEP)
    def _():
        copy = pltpu.make_async_copy(list_hbm, list_ref, sems.at[3])
        copy.start()
        copy.wait()
        find_all(list_ref, spots, t)

        def rest(b, c):
            count = many_s[0, b]

            def chunk(j, c2):
                got = squeeze(list_ref, spots, b, (KEEP * j).astype(F32))
                more[pl.ds(0, 3), pl.ds(0, KEEP)] = got[0:3]
                spot = got[3:4].astype(I32)
                more_i[pl.ds(0, 1), pl.ds(0, KEEP)] = spot
                copies = [pltpu.make_async_copy(more, more_s, sems.at[3]), pltpu.make_async_copy(more_i, more_is, sems.at[4])]
                for copy in copies:
                    copy.start()
                for copy in copies:
                    copy.wait()

                def one(k, c3):
                    spot = more_is[0, k] & ((1 << 24) - 1)
                    here = lane_id == (spot & 127)
                    for n in range(3):
                        flat[n, pl.ds(spot >> 7, 1), :] += jnp.where(here, more_s[n, k], 0.0)
                    return c3

                return lax.fori_loop(0, jnp.minimum(count - KEEP * j, KEEP), one, c2)

            return lax.fori_loop(1, (count + KEEP - 1) // KEEP, chunk, c)

        lax.fori_loop(0, TILES, rest, 0)

    loads[0].wait()

    def scale_b(s, c):
        for i in range(3):
            value = runs_of(lambda k: u[i, jnp.minimum(k, 79), pl.ds(0, 48), :], s, 48, 0, 14, 128 - ZB - RIM) + u[i, B0 + s, pl.ds(0, 48), :]
            u[i, B0 + s, pl.ds(0, 48), :] = 0.5 * coef[B0 + s, pl.ds(0, 48), :] * value
        return c

    lax.fori_loop(0, RUN, scale_b, 0)

    def scale_a(k, c):
        for i in range(3):
            u[i, k] = 0.5 * coef[k] * u[i, k]
        return c

    lax.fori_loop(0, 80, scale_a, 0)

    plan = [(u, p, u, 0.5), (p, q, None, 1.0), (q, u, p, 0.25), (u, p, None, 1.0), (p, q, None, 1.0),
            (q, p, None, 1.0), (p, q, u, 0.0625)]
    for n, (src, dst, base, scale) in enumerate(plan):
        e = RIM - 1 - n
        nk, nh = -(-(CY + 2 * e) // 8), -(-(CY + 1 + 2 * e) // 8)
        for i in range(3):
            src[i, B0 - 1] = pltpu.roll(src[i, B0 + RUN - 1], SEG, 1)
            src[i, B0 + RUN] = pltpu.roll(src[i, B0], 128 - SEG, 1)
        stencil(src, dst, base, coef, hx_ref, hy_ref, hz_ref, B0, B0 + RUN, 8 - e, nk, nh, scale)
        stencil(src, dst, base, coef, hx_ref, hy_ref, hz_ref, OWN - e, OWN + CX + e, 8 - e, nk, nh, scale)

    loads[1].wait()
    loads[2].wait()
    lane = iota((CY, 128), 1)
    own_y = pl.ds(8, CY)
    lap = lap_ref[0]
    for g in range(RUNS):
        begin, end = max(0, RUN * g - RIM), min(CX, RUN * (g + 1) - RIM)

        def combine(k, c, g=g, begin=begin, end=end):
            for j in range(2):
                x = jnp.minimum(begin + 2 * k + j, end - 1)
                total = jnp.zeros((CY, 128), F32)
                for i in range(3):
                    rims = q[i, B0 + x + RIM - RUN * g, own_y, :]
                    value = jnp.where(lane >= CZ - 2 * RIM, pltpu.roll(rims, (ZB - SEG * g) % 128, 1),
                                      pltpu.roll(q[i, OWN + x, own_y, :], 128 - RIM, 1))
                    total = total + field[i, x].astype(F32) * value
                out_ref[x] = -lap * cond[x] * total
            return c

        lax.fori_loop(0, (end - begin + 1) // 2, combine, 0)


def spread_kernel(part_ref, out_ref, send, recv, lsem):
    f, t = lax.axis_index("freq"), lax.axis_index("tile")
    me = f * TILES + t
    barrier = pltpu.get_barrier_semaphore()

    def greet(i, c):
        pl.semaphore_signal(barrier, inc=1, device_id=me ^ i, device_id_type=pl.DeviceIdType.LOGICAL)
        return c

    lax.fori_loop(1, 2 * TILES, greet, 0)
    mine = pltpu.make_async_copy(part_ref.at[t, pl.ds(f * 16, 16)], out_ref.at[me], lsem)
    mine.start()
    pl.semaphore_wait(barrier, 2 * TILES - 1)

    def share(i, c):
        d = me ^ i
        pltpu.make_async_remote_copy(part_ref.at[d & (TILES - 1), pl.ds((d >> 6) * 16, 16)], out_ref.at[me], send, recv,
                                     device_id=d, device_id_type=pl.DeviceIdType.LOGICAL).start()
        return c

    lax.fori_loop(1, 2 * TILES, share, 0)
    mine.wait()
    others = out_ref.at[pl.ds(0, 2 * TILES - 1)]
    for sem in (send, recv):
        pltpu.make_async_copy(others, others, sem).wait()


def local(residual, row_counts, recv_owner, recv_cell, conductivity, laplace, forward_field):
    owner = recv_owner[:, 0]
    gx = (owner // (TY * TZ)) * CX + recv_cell // (CY * CZ)
    gy = (owner // TZ % TY) * CY + recv_cell // CZ % CY
    gz = (owner % TZ) * CZ + recv_cell % CZ
    codes = ((gx * (TY * CY) + gy) * (TZ * CZ) + gz).astype(F32)[None]
    smem = pl.BlockSpec(memory_space=pltpu.SMEM)
    cond = conductivity[0]
    lists, coef, short, spot, many = pl.pallas_call(
        gather_kernel,
        name="gather_lists",
        out_shape=(jax.ShapeDtypeStruct((TILES, 8, 128), F32), jax.ShapeDtypeStruct((PLANES, YR, 128), F32),
                   jax.ShapeDtypeStruct((3 * TILES // 2, 128), F32), jax.ShapeDtypeStruct((TILES // 2, 128), I32),
                   jax.ShapeDtypeStruct((8, 128), I32)),
        in_specs=[hbm(), hbm(), hbm(), smem, hbm()],
        out_specs=(vmem(), vmem(), vmem(), vmem(), vmem()),
        scratch_shapes=[
            pltpu.VMEM((1, 3, 1024), F32),
            pltpu.VMEM((1, 256), I32),
            pltpu.VMEM((1, 256), F32),
            pltpu.VMEM((2, TILES, 256), F32),
            pltpu.VMEM((80, 48, 128), F32),
            pltpu.VMEM((10, 48, 128), F32),
            pltpu.VMEM((10, 48, 128), F32),
            pltpu.VMEM((10, 48, 128), F32),
            pltpu.SemaphoreType.DMA((8,)),
            pltpu.SemaphoreType.DMA((8,)),
            pltpu.SemaphoreType.DMA((2,)),
            pltpu.SemaphoreType.DMA((2,)),
            pltpu.SemaphoreType.DMA,
            pltpu.SemaphoreType.DMA,
            pltpu.SemaphoreType.DMA((4,)),
        ],
        compiler_params=pltpu.CompilerParams(collective_id=0, has_side_effects=True, vmem_limit_bytes=62 * 2**20),
    )(residual, row_counts, codes, laplace, cond)
    partial = pl.pallas_call(
        relax_kernel,
        name="relax_tile",
        out_shape=jax.ShapeDtypeStruct((CX, CY, CZ), F32),
        in_specs=[hbm(), smem, smem, smem, smem, hbm(), hbm(), hbm()],
        out_specs=vmem(),
        scratch_shapes=[pltpu.VMEM((3, PLANES, YR, 128), F32)] * 3
        + [pltpu.VMEM((PLANES, YR, 128), F32)] * 4
        + [
            pltpu.VMEM((CX, CY, CZ), F32),
            pltpu.VMEM((3, CX, CY, CZ), BF16),
            pltpu.VMEM((TILES, 8, 128), F32),
            pltpu.VMEM((2, TILES, 256), F32),
            pltpu.VMEM((8, 128), F32),
            pltpu.VMEM((8, 128), I32),
            pltpu.SMEM((8, 128), F32),
            pltpu.SMEM((8, 128), I32),
            pltpu.SemaphoreType.DMA((5,)),
        ],
        compiler_params=pltpu.CompilerParams(vmem_limit_bytes=62 * 2**20),
    )(lists, laplace, short.reshape(-1), spot.reshape(-1), many, coef, cond, forward_field[0, 0])
    both = pl.pallas_call(
        spread_kernel,
        name="spread_rows",
        out_shape=jax.ShapeDtypeStruct((2 * TILES, 16, CZ), F32),
        in_specs=[hbm()],
        out_specs=hbm(),
        scratch_shapes=[pltpu.SemaphoreType.DMA] * 3,
        compiler_params=pltpu.CompilerParams(collective_id=1, has_side_effects=True, vmem_limit_bytes=62 * 2**20),
    )(partial)
    return (both[:TILES] + both[TILES:])[:, None]


def solution(mesh):
    placed = (
        P("freq", None, "tile"),
        P("tile", None),
        P("tile", None),
        P("tile"),
        P("tile", None, None, None),
        P("freq"),
        P("freq", "tile", None, None, None, None),
    )
    return jax.shard_map(
        local, mesh=mesh, in_specs=placed, out_specs=P(None, "tile", "freq", None), check_vma=False
    )
```

```python
import functools

import jax
import jax.numpy as jnp
from jax import lax
from jax.experimental import pallas as pl
from jax.experimental.pallas import tpu as pltpu
from jax.sharding import PartitionSpec as P

F32 = jnp.float32
BF16 = jnp.bfloat16
I32 = jnp.int32
MESH = pl.DeviceIdType.MESH

TX, TY, TZ = 4, 4, 4
TILES = 64
CX, CY, CZ = 64, 32, 128
NP = 4
RIM = 7

YR = 56
B0 = 81
RUN = 20
SEG = 28
RUNS = 4
ZB = CZ + RIM - SEG
PLANES = 108
KEEP = 64
OWN = 8


def iota(shape, dim):
    return lax.broadcasted_iota(I32, shape, dim)


def vmem():
    return pl.BlockSpec(memory_space=pltpu.VMEM)


def hbm():
    return pl.BlockSpec(memory_space=pl.ANY)


def place(t):
    return t // (TY * TZ), (t // TZ) % TY, t % TZ


def three(value):
    hi = value.astype(BF16)
    rest = value - hi.astype(F32)
    mid = rest.astype(BF16)
    low = (rest - mid.astype(F32)).astype(BF16)
    return hi, mid, low


def runs_of(read, s, rows, begin, end, shift):
    lane = iota((rows, 128), 1)
    total = jnp.zeros((rows, 128), F32)
    for g in range(RUNS):
        plane = read(1 + RUN * g + s)
        moved = pltpu.roll(plane, (SEG * g + shift) % 128, 1)
        total = jnp.where((lane >= SEG * g + begin) & (lane < SEG * g + end), moved, total)
    return total


def locate(code, tx, ty, tz):
    x = (code >> 16) - tx * CX + RIM
    y = ((code >> 9) & 127) - ty * CY + RIM
    z = (code & 511) - tz * CZ
    ok = (x >= 0) & (x < CX + 2 * RIM) & (y >= 0) & (y < CY + 2 * RIM) & (z >= -RIM) & (z < CZ + RIM)
    run = sum((x >= RUN * g).astype(I32) for g in range(1, RUNS))
    in_a = z < 128 - RIM
    plane = jnp.where(in_a, x + 1, x - RUN * run + B0)
    lane = jnp.where(in_a, z + RIM, SEG * run + z - ZB)
    return ok, jnp.where(ok, (plane * YR + y + 1) * 128 + lane, 0).astype(F32)


def find_all(list_ref, spots, t):
    code = jnp.concatenate([list_ref[:, 3, :], list_ref[:, 7, :]], axis=1).astype(I32)
    ok, spot = locate(code, *place(t))
    before = (iota((256, 256), 0) < iota((256, 256), 1)).astype(F32).astype(BF16)
    flag = ok.astype(F32)
    rank = jnp.dot(flag.astype(BF16), before, preferred_element_type=F32)
    spots[0] = spot
    spots[1] = jnp.where(ok, rank, -1.0)
    ones = jnp.ones((8, 256), BF16)
    return lax.dot_general(ones, flag.astype(BF16), (((1,), (1,)), ((), ())), preferred_element_type=F32).astype(I32)


def squeeze(list_ref, spots, b, first):
    place_k = iota((KEEP, 256), 0).astype(F32)
    values = jnp.concatenate([list_ref[b, pl.ds(0, 3), :], list_ref[b, pl.ds(4, 3), :]], axis=1)
    both = jnp.concatenate([values, spots[0, pl.ds(b, 1), :]], axis=0)
    pick = (place_k == spots[1, pl.ds(b, 1), :] - first).astype(F32).astype(BF16)
    parts = jnp.concatenate([part.astype(F32) for part in three(both)] + [jnp.zeros((4, 256), F32)], axis=0).astype(BF16)
    got = lax.dot_general(parts, pick, (((1,), (1,)), ((), ())), preferred_element_type=F32)
    return (got[0:4] + got[4:8]) + got[8:12]


def gather_kernel(res_hbm, cnt_hbm, tile_hbm, cell_hbm, lap_ref, cond_ref, list_ref, coef_ref, short_ref, spot_ref, many_ref,
                  res_ref, cnt_ref, tile_ref, cell_ref, spots, cext, pack, low, high, sends, recvs, zsend, zrecv, gsend, grecv, lsem):
    f, t = lax.axis_index("freq"), lax.axis_index("tile")
    me = f * TILES + t
    tx, ty, tz = place(t)
    barrier = pltpu.get_barrier_semaphore()

    def greet(i, c):
        pl.semaphore_signal(barrier, inc=1, device_id=me ^ i, device_id_type=pl.DeviceIdType.LOGICAL)
        return c

    lax.fori_loop(1, TILES, greet, 0)
    own = pltpu.make_async_copy(cond_ref, cext.at[pl.ds(OWN, CX), pl.ds(8, CY)], lsem.at[0])
    own.start()
    loads = [pltpu.make_async_copy(a, b, lsem.at[n + 1])
             for n, (a, b) in enumerate(((res_hbm, res_ref), (cnt_hbm, cnt_ref), (tile_hbm, tile_ref), (cell_hbm, cell_ref)))]
    for copy in loads:
        copy.start()
    for copy in loads:
        copy.wait()

    counts = cnt_ref[...].astype(F32)
    upto = (iota((256, 256), 0) <= iota((256, 256), 1)).astype(F32)
    ends = jnp.dot(jnp.broadcast_to(counts, (8, 256)).astype(BF16), upto.astype(BF16), preferred_element_type=F32)[0:1]
    starts = ends - counts
    at = iota((1024, 256), 0).astype(F32)
    member = ((at >= starts) & (at < ends)).astype(F32).astype(BF16)
    sums = jnp.zeros((3, 256), F32)
    for part in three(res_ref[:, 0, :]):
        sums = sums + jnp.dot(part, member, preferred_element_type=F32)
    means = sums / counts
    owner, cell = tile_ref[...], cell_ref[...]
    gx = (owner >> 4) * CX + (cell >> 12)
    gy = ((owner >> 2) & 3) * CY + ((cell >> 7) & 31)
    gz = (owner & 3) * CZ + (cell & 127)
    code = ((gx * (TY * CY) + gy) * (TZ * CZ) + gz).astype(F32)
    both = jnp.concatenate([means, code], axis=0)
    list_ref[t] = jnp.concatenate([both[:, :128], both[:, 128:]], axis=0)

    own.wait()
    pl.semaphore_wait(barrier, TILES - 1)

    def share(i, c):
        pltpu.make_async_remote_copy(list_ref.at[t], list_ref.at[t], gsend, grecv,
                                     device_id=me ^ i, device_id_type=pl.DeviceIdType.LOGICAL).start()
        return c

    lax.fori_loop(1, TILES, share, 0)

    spans = {1: (CX - 7, 1, 7), -1: (0, 72, 7), 0: (0, 8, CX)}
    rows = {1: (CY - 7, 1, 7), -1: (0, 40, 7), 0: (0, 8, CY)}
    ways = [(dx, dy) for dx in (-1, 0, 1) for dy in (-1, 0, 1) if (dx, dy) != (0, 0)]

    def inside(dx, dy):
        x, y = tx + dx, ty + dy
        return (x >= 0) & (x < TX) & (y >= 0) & (y < TY)

    def halo(n):
        dx, dy = ways[n]
        xs, xd, xn = spans[dx]
        ys, yd, yn = rows[dy]
        return pltpu.make_async_remote_copy(
            cext.at[pl.ds(OWN + xs, xn), pl.ds(8 + ys, yn)], cext.at[pl.ds(xd, xn), pl.ds(yd, yn)],
            sends.at[n], recvs.at[n], device_id=(f, t + dx * TY * TZ + dy * TZ), device_id_type=MESH)

    for n, (dx, dy) in enumerate(ways):
        @pl.when(inside(dx, dy))
        def _(n=n):
            halo(n).start()

    everyone = list_ref.at[pl.ds(0, TILES - 1)]
    pltpu.make_async_copy(everyone, everyone, grecv).wait()
    many_ref[:, pl.ds(0, TILES)] = find_all(list_ref, spots, t)

    def compact(k, c):
        for i in range(2):
            pair = jnp.concatenate([squeeze(list_ref, spots, 4 * k + 2 * i + j, 0.0) for j in range(2)], axis=1)
            short_ref[pl.ds(3 * (2 * k + i), 3), :] = pair[0:3]
            spot_ref[pl.ds(2 * k + i, 1), :] = pair[3:4].astype(I32)
        return c

    lax.fori_loop(0, TILES // 4, compact, 0)
    for n, (dx, dy) in enumerate(ways):
        @pl.when(inside(-dx, -dy))
        def _(n=n):
            halo(n).wait_recv()

    def read(i):
        return cext[jnp.minimum(i, 79)]

    lane = iota((48, 128), 1)

    def fill(s, c):
        total = jnp.zeros((48, 128), F32)
        for h in range(8):
            plane = cext[jnp.minimum(1 + 10 * h + s, 79)]
            for begin, shift in ((16 * h, 16 * h - 121), (16 * h + 8, 16 * h + 8)):
                moved = pltpu.roll(plane, shift % 128, 1)
                total = jnp.where((lane >= begin) & (lane < begin + 7), moved, total)
        pack[s] = total
        return c

    lax.fori_loop(0, 10, fill, 0)

    def rim(up):
        return pltpu.make_async_remote_copy(
            pack, low if up else high, zsend.at[up], zrecv.at[up],
            device_id=(f, t + (1 if up else -1)), device_id_type=MESH)

    @pl.when(tz < TZ - 1)
    def _():
        rim(1).start()

    @pl.when(tz > 0)
    def _():
        rim(0).start()

    lap = lap_ref[0]
    yrow = iota((48, 128), 0) - 8
    yin = (yrow + ty * CY >= 0) & (yrow + ty * CY < TY * CY)

    @pl.when(tz > 0)
    def _():
        rim(1).wait_recv()

    def fill_a(i, c):
        k = jnp.clip(i - 1, 0, 79)
        x = i - 8 + tx * CX
        from_low = pltpu.roll(low[k % 10], (128 - 16 * (k // 10)) % 128, 1)
        value = jnp.where(lane < RIM, from_low, pltpu.roll(cext[i], RIM, 1))
        good = yin & ((lane >= RIM) | (tz > 0)) & (x >= 0) & (x < TX * CX)
        coef_ref[i, pl.ds(0, 48), :] = jnp.where(good, 1.0 / (4.0 + lap * value), 0.0)
        return c

    lax.fori_loop(0, 80, fill_a, 0)

    @pl.when(tz < TZ - 1)
    def _():
        rim(0).wait_recv()

    run = sum((lane >= SEG * g).astype(I32) for g in range(1, RUNS))
    z = lane - run * SEG + ZB
    zin = ((z < CZ) | (tz < TZ - 1)) & (lane < RUNS * SEG)

    def fill_b(s, c):
        value = runs_of(read, s, 48, 0, SEG - RIM, 128 - ZB)
        for g in range(RUNS):
            i = RUN * g + s
            from_high = pltpu.roll(high[i % 10], (SEG * g + SEG - RIM - 8 - 16 * (i // 10) + 256) % 128, 1)
            value = jnp.where((lane >= SEG * g + SEG - RIM) & (lane < SEG * g + SEG), from_high, value)
        x = RUN * run + s - 7 + tx * CX
        good = yin & zin & (x >= 0) & (x < TX * CX)
        coef_ref[B0 + s, pl.ds(0, 48), :] = jnp.where(good, 1.0 / (4.0 + lap * value), 0.0)
        return c

    lax.fori_loop(0, RUN, fill_b, 0)

    for n, (dx, dy) in enumerate(ways):
        @pl.when(inside(dx, dy))
        def _(n=n):
            halo(n).wait_send()

    @pl.when(tz < TZ - 1)
    def _():
        rim(1).wait_send()

    @pl.when(tz > 0)
    def _():
        rim(0).wait_send()

    pltpu.make_async_copy(everyone, everyone, gsend).wait()


def stencil(src, dst, base, coef, hx_ref, hy_ref, hz_ref, lo, hi, y0, nk, nh, scale):
    rk, rh, h0 = 8 * nk, 8 * nh, y0 - 1
    hr, hy_rows, kr, kl = pl.ds(h0, rh), pl.ds(y0, rh), pl.ds(y0, rk), pl.ds(h0, rk)

    def swirl(x):
        vx, vy, vz = src[0, x, hr, :], src[1, x, hr, :], src[2, x, hr, :]
        vyz, vxz = pltpu.roll(vy, 127, 1), pltpu.roll(vx, 127, 1)
        hx_ref[x, hr, :] = (src[2, x, hy_rows, :] - vz) - (vyz - vy)
        hy_ref[x, hr, :] = (vxz - vx) - (src[2, x + 1, hr, :] - vz)
        hz_ref[x, hr, :] = (src[1, x + 1, hr, :] - vy) - (src[0, x, hy_rows, :] - vx)

    def relax(x):
        hx, hy, hz = hx_ref[x, kr, :], hy_ref[x, kr, :], hz_ref[x, kr, :]
        kx = (hz - hz_ref[x, kl, :]) - (hy - pltpu.roll(hy, 1, 1))
        ky = (hx - pltpu.roll(hx, 1, 1)) - (hz - hz_ref[x - 1, kr, :])
        kz = (hy - hy_ref[x - 1, kr, :]) - (hx - hx_ref[x, kl, :])
        c = coef[x, kr, :] if scale == 1.0 else scale * coef[x, kr, :]
        keep = (scale if base is not src else 1.0 + scale) + 4.0 * c
        for i, k in enumerate((kx, ky, kz)):
            new = keep * src[i, x, kr, :] - c * k
            if base is not None and base is not src:
                new = base[i, x, kr, :] + new
            dst[i, x, kr, :] = new

    for i in range(-1, NP):
        swirl(lo + i)

    def body(k, c):
        x = jnp.minimum(lo + NP * k, hi - NP)
        for i in range(NP):
            relax(x + i)
        for i in range(NP):
            swirl(x + NP + i)
        return c

    lax.fori_loop(0, (hi - lo + NP - 1) // NP, body, 0)


def relax_kernel(list_hbm, lap_ref, short_s, spot_s, many_s, coef_hbm, cond_hbm, field_hbm, out_ref,
                 u, p, q, hx_ref, hy_ref, hz_ref, coef, cond, field, list_ref, spots, more, more_i, more_s, more_is, sems):
    t = lax.axis_index("tile")
    loads = [pltpu.make_async_copy(a, b, sems.at[n])
             for n, (a, b) in enumerate(((coef_hbm, coef), (cond_hbm, cond), (field_hbm, field)))]
    for copy in loads:
        copy.start()

    flat = u.reshape(3, PLANES * YR, 128)

    def clear(i, c):
        for k in range(3):
            u[k, i] = jnp.zeros((YR, 128), F32)
        return c

    lax.fori_loop(0, PLANES, clear, 0)
    lane_id = iota((1, 128), 1)

    def drop(k, most):
        for i in range(2):
            count = many_s[0, 2 * k + i]

            def read(j, i=i):
                at, where = 384 * k + KEEP * i + 4 * j, 128 * k + KEEP * i + 4 * j
                return (tuple(spot_s[where + m] for m in range(4)),
                        tuple(short_s[at + 128 * n + m] for m in range(4) for n in range(3)))

            def four(j, held):
                coming = read(j + 1)
                for m in range(4):
                    here = lane_id == (held[0][m] & 127)
                    row = pl.ds(held[0][m] >> 7, 1)
                    for n in range(3):
                        flat[n, row, :] += jnp.where(here, held[1][3 * m + n], 0.0)
                return coming

            lax.fori_loop(0, (jnp.minimum(count, KEEP) + 3) // 4, four, read(0))
            most = jnp.maximum(most, count)
        return most

    most = lax.fori_loop(0, TILES // 2, drop, 0)

    @pl.when(most > KEEP)
    def _():
        copy = pltpu.make_async_copy(list_hbm, list_ref, sems.at[3])
        copy.start()
        copy.wait()
        find_all(list_ref, spots, t)

        def rest(b, c):
            count = many_s[0, b]

            def chunk(j, c2):
                got = squeeze(list_ref, spots, b, (KEEP * j).astype(F32))
                more[pl.ds(0, 3), pl.ds(0, KEEP)] = got[0:3]
                spot = got[3:4].astype(I32)
                more_i[pl.ds(0, 1), pl.ds(0, KEEP)] = spot
                copies = [pltpu.make_async_copy(more, more_s, sems.at[3]), pltpu.make_async_copy(more_i, more_is, sems.at[4])]
                for copy in copies:
                    copy.start()
                for copy in copies:
                    copy.wait()

                def one(k, c3):
                    spot = more_is[0, k]
                    here = lane_id == (spot & 127)
                    for n in range(3):
                        flat[n, pl.ds(spot >> 7, 1), :] += jnp.where(here, more_s[n, k], 0.0)
                    return c3

                return lax.fori_loop(0, jnp.minimum(count - KEEP * j, KEEP), one, c2)

            return lax.fori_loop(1, (count + KEEP - 1) // KEEP, chunk, c)

        lax.fori_loop(0, TILES, rest, 0)

    loads[0].wait()

    def scale_b(k, c):
        done = []
        for j in range(2):
            s = 2 * k + j
            for i in range(3):
                value = runs_of(lambda k: u[i, jnp.minimum(k, 79), pl.ds(0, 48), :], s, 48, 0, 14, 128 - ZB - RIM)
                done.append((i, B0 + s, 0.5 * coef[B0 + s, pl.ds(0, 48), :] * (value + u[i, B0 + s, pl.ds(0, 48), :])))
        for i, s, value in done:
            u[i, s, pl.ds(0, 48), :] = value
        return c

    lax.fori_loop(0, RUN // 2, scale_b, 0)

    def scale_a(k, c):
        for i in range(3):
            u[i, k] = 0.5 * coef[k] * u[i, k]
        return c

    lax.fori_loop(0, 80, scale_a, 0)

    plan = [(u, p, u, 0.5), (p, q, None, 1.0), (q, u, p, 0.25), (u, p, None, 1.0), (p, q, None, 1.0),
            (q, p, None, 1.0), (p, q, u, 0.0625)]
    for n, (src, dst, base, scale) in enumerate(plan):
        e = RIM - 1 - n
        nk, nh = -(-(CY + 2 * e) // 8), -(-(CY + 1 + 2 * e) // 8)
        for i in range(3):
            src[i, B0 - 1] = pltpu.roll(src[i, B0 + RUN - 1], SEG, 1)
            src[i, B0 + RUN] = pltpu.roll(src[i, B0], 128 - SEG, 1)
        stencil(src, dst, base, coef, hx_ref, hy_ref, hz_ref, B0, B0 + RUN, 8 - e, nk, nh, scale)
        stencil(src, dst, base, coef, hx_ref, hy_ref, hz_ref, OWN - e, OWN + CX + e, 8 - e, nk, nh, scale)

    loads[1].wait()
    loads[2].wait()
    lane = iota((CY, 128), 1)
    own_y = pl.ds(8, CY)
    lap = lap_ref[0]
    for g in range(RUNS):
        begin, end = max(0, RUN * g - RIM), min(CX, RUN * (g + 1) - RIM)

        def combine(k, c, g=g, begin=begin, end=end):
            for j in range(4):
                x = jnp.minimum(begin + 4 * k + j, end - 1)
                total = jnp.zeros((CY, 128), F32)
                for i in range(3):
                    rims = q[i, B0 + x + RIM - RUN * g, own_y, :]
                    value = jnp.where(lane >= CZ - 2 * RIM, pltpu.roll(rims, (ZB - SEG * g) % 128, 1),
                                      pltpu.roll(q[i, OWN + x, own_y, :], 128 - RIM, 1))
                    total = total + field[i, x].astype(F32) * value
                out_ref[x] = -lap * cond[x] * total
            return c

        lax.fori_loop(0, (end - begin + 3) // 4, combine, 0)


def spread_kernel(part_ref, out_ref, send, recv, lsem):
    f, t = lax.axis_index("freq"), lax.axis_index("tile")
    me = f * TILES + t
    barrier = pltpu.get_barrier_semaphore()

    def greet(i, c):
        pl.semaphore_signal(barrier, inc=1, device_id=me ^ i, device_id_type=pl.DeviceIdType.LOGICAL)
        return c

    lax.fori_loop(1, 2 * TILES, greet, 0)
    mine = pltpu.make_async_copy(part_ref.at[t, pl.ds(f * 16, 16)], out_ref.at[me], lsem)
    mine.start()
    pl.semaphore_wait(barrier, 2 * TILES - 1)

    def share(i, c):
        d = me ^ i
        pltpu.make_async_remote_copy(part_ref.at[d & (TILES - 1), pl.ds((d >> 6) * 16, 16)], out_ref.at[me], send, recv,
                                     device_id=d, device_id_type=pl.DeviceIdType.LOGICAL).start()
        return c

    lax.fori_loop(1, 2 * TILES, share, 0)
    mine.wait()
    others = out_ref.at[pl.ds(0, 2 * TILES - 1)]
    for sem in (send, recv):
        pltpu.make_async_copy(others, others, sem).wait()


def local(residual, row_counts, recv_owner, recv_cell, conductivity, laplace, forward_field):
    smem = pl.BlockSpec(memory_space=pltpu.SMEM)
    cond = conductivity[0]
    lists, coef, short, spot, many = pl.pallas_call(
        gather_kernel,
        name="gather_lists",
        out_shape=(jax.ShapeDtypeStruct((TILES, 8, 128), F32), jax.ShapeDtypeStruct((PLANES, YR, 128), F32),
                   jax.ShapeDtypeStruct((104, 128), F32), jax.ShapeDtypeStruct((40, 128), I32),
                   jax.ShapeDtypeStruct((8, 128), I32)),
        in_specs=[hbm(), hbm(), hbm(), hbm(), smem, hbm()],
        out_specs=(vmem(), vmem(), vmem(), vmem(), vmem()),
        scratch_shapes=[
            pltpu.VMEM((3, 1, 1024), F32),
            pltpu.VMEM((1, 256), I32),
            pltpu.VMEM((1, 256), I32),
            pltpu.VMEM((1, 256), I32),
            pltpu.VMEM((2, TILES, 256), F32),
            pltpu.VMEM((80, 48, 128), F32),
            pltpu.VMEM((10, 48, 128), F32),
            pltpu.VMEM((10, 48, 128), F32),
            pltpu.VMEM((10, 48, 128), F32),
            pltpu.SemaphoreType.DMA((8,)),
            pltpu.SemaphoreType.DMA((8,)),
            pltpu.SemaphoreType.DMA((2,)),
            pltpu.SemaphoreType.DMA((2,)),
            pltpu.SemaphoreType.DMA,
            pltpu.SemaphoreType.DMA,
            pltpu.SemaphoreType.DMA((5,)),
        ],
        compiler_params=pltpu.CompilerParams(collective_id=0, has_side_effects=True, vmem_limit_bytes=62 * 2**20),
    )(residual.transpose(1, 0, 2), row_counts, recv_owner.reshape(1, -1), recv_cell.reshape(1, -1), laplace, cond)
    partial = pl.pallas_call(
        relax_kernel,
        name="relax_tile",
        out_shape=jax.ShapeDtypeStruct((CX, CY, CZ), F32),
        in_specs=[hbm(), smem, smem, smem, smem, hbm(), hbm(), hbm()],
        out_specs=vmem(),
        scratch_shapes=[pltpu.VMEM((3, PLANES, YR, 128), F32)] * 3
        + [pltpu.VMEM((PLANES, YR, 128), F32)] * 4
        + [
            pltpu.VMEM((CX, CY, CZ), F32),
            pltpu.VMEM((3, CX, CY, CZ), BF16),
            pltpu.VMEM((TILES, 8, 128), F32),
            pltpu.VMEM((2, TILES, 256), F32),
            pltpu.VMEM((8, 128), F32),
            pltpu.VMEM((8, 128), I32),
            pltpu.SMEM((8, 128), F32),
            pltpu.SMEM((8, 128), I32),
            pltpu.SemaphoreType.DMA((5,)),
        ],
        compiler_params=pltpu.CompilerParams(vmem_limit_bytes=62 * 2**20),
    )(lists, laplace, short.reshape(-1), spot.reshape(-1), many, coef, cond, forward_field[0, 0])
    both = pl.pallas_call(
        spread_kernel,
        name="spread_rows",
        out_shape=jax.ShapeDtypeStruct((2 * TILES, 16, CZ), F32),
        in_specs=[hbm()],
        out_specs=hbm(),
        scratch_shapes=[pltpu.SemaphoreType.DMA] * 3,
        compiler_params=pltpu.CompilerParams(collective_id=1, has_side_effects=True, vmem_limit_bytes=62 * 2**20),
    )(partial)
    return (both[:TILES] + both[TILES:])[:, None]


def solution(mesh):
    placed = (
        P("freq", None, "tile"),
        P("tile", None),
        P("tile", None),
        P("tile"),
        P("tile", None, None, None),
        P("freq"),
        P("freq", "tile", None, None, None, None),
    )
    return jax.shard_map(
        local, mesh=mesh, in_specs=placed, out_specs=P(None, "tile", "freq", None), check_vma=False
    )
```

```python
import functools

import jax
import jax.numpy as jnp
from jax import lax
from jax.experimental import pallas as pl
from jax.experimental.pallas import tpu as pltpu
from jax.sharding import PartitionSpec as P

F32 = jnp.float32
BF16 = jnp.bfloat16
I32 = jnp.int32
MESH = pl.DeviceIdType.MESH

TX, TY, TZ = 4, 4, 4
TILES = 64
CX, CY, CZ = 64, 32, 128
NP = 4
RIM = 7

YR = 56
B0 = 81
RUN = 20
SEG = 28
RUNS = 4
ZB = CZ + RIM - SEG
PLANES = 108
KEEP = 64
OWN = 8


def iota(shape, dim):
    return lax.broadcasted_iota(I32, shape, dim)


def vmem():
    return pl.BlockSpec(memory_space=pltpu.VMEM)


def hbm():
    return pl.BlockSpec(memory_space=pl.ANY)


def place(t):
    return t // (TY * TZ), (t // TZ) % TY, t % TZ


def three(value):
    hi = value.astype(BF16)
    rest = value - hi.astype(F32)
    mid = rest.astype(BF16)
    low = (rest - mid.astype(F32)).astype(BF16)
    return hi, mid, low


def runs_of(read, s, rows, begin, end, shift):
    lane = iota((rows, 128), 1)
    total = jnp.zeros((rows, 128), F32)
    for g in range(RUNS):
        plane = read(1 + RUN * g + s)
        moved = pltpu.roll(plane, (SEG * g + shift) % 128, 1)
        total = jnp.where((lane >= SEG * g + begin) & (lane < SEG * g + end), moved, total)
    return total


def locate(code, tx, ty, tz):
    x = (code >> 16) - tx * CX + RIM
    y = ((code >> 9) & 127) - ty * CY + RIM
    z = (code & 511) - tz * CZ
    ok = (x >= 0) & (x < CX + 2 * RIM) & (y >= 0) & (y < CY + 2 * RIM) & (z >= -RIM) & (z < CZ + RIM)
    run = sum((x >= RUN * g).astype(I32) for g in range(1, RUNS))
    in_a = z < 128 - RIM
    plane = jnp.where(in_a, x + 1, x - RUN * run + B0)
    lane = jnp.where(in_a, z + RIM, SEG * run + z - ZB)
    return ok, jnp.where(ok, (plane * YR + y + 1) * 128 + lane, 0).astype(F32)


def find_all(list_ref, spots, t):
    code = jnp.concatenate([list_ref[:, 3, :], list_ref[:, 7, :]], axis=1).astype(I32)
    ok, spot = locate(code, *place(t))
    before = (iota((256, 256), 0) < iota((256, 256), 1)).astype(F32).astype(BF16)
    flag = ok.astype(F32)
    rank = jnp.dot(flag.astype(BF16), before, preferred_element_type=F32)
    spots[0] = spot
    spots[1] = jnp.where(ok, rank, -1.0)
    ones = jnp.ones((8, 256), BF16)
    return lax.dot_general(ones, flag.astype(BF16), (((1,), (1,)), ((), ())), preferred_element_type=F32).astype(I32)


def squeeze(list_ref, spots, b, first):
    place_k = iota((KEEP, 256), 0).astype(F32)
    values = jnp.concatenate([list_ref[b, pl.ds(0, 3), :], list_ref[b, pl.ds(4, 3), :]], axis=1)
    both = jnp.concatenate([values, spots[0, pl.ds(b, 1), :]], axis=0)
    pick = (place_k == spots[1, pl.ds(b, 1), :] - first).astype(F32).astype(BF16)
    parts = jnp.concatenate([part.astype(F32) for part in three(both)] + [jnp.zeros((4, 256), F32)], axis=0).astype(BF16)
    got = lax.dot_general(parts, pick, (((1,), (1,)), ((), ())), preferred_element_type=F32)
    return (got[0:4] + got[4:8]) + got[8:12]


def gather_kernel(res_hbm, cnt_hbm, tile_hbm, cell_hbm, lap_ref, cond_ref, list_ref, coef_ref, short_ref, spot_ref, many_ref,
                  res_ref, cnt_ref, tile_ref, cell_ref, spots, raw, cext, pack, low, high, sends, recvs, zsend, zrecv, gsend, grecv, lsem):
    f, t = lax.axis_index("freq"), lax.axis_index("tile")
    me = f * TILES + t
    tx, ty, tz = place(t)
    barrier = pltpu.get_barrier_semaphore()

    def greet(i, c):
        pl.semaphore_signal(barrier, inc=1, device_id=me ^ i, device_id_type=pl.DeviceIdType.LOGICAL)
        return c

    lax.fori_loop(1, TILES, greet, 0)
    own = pltpu.make_async_copy(cond_ref, raw, lsem.at[0])
    own.start()
    loads = [pltpu.make_async_copy(a, b, lsem.at[n + 1])
             for n, (a, b) in enumerate(((res_hbm, res_ref), (cnt_hbm, cnt_ref), (tile_hbm, tile_ref), (cell_hbm, cell_ref)))]
    for copy in loads:
        copy.start()
    for copy in loads:
        copy.wait()

    counts = cnt_ref[...].astype(F32)
    upto = (iota((256, 256), 0) <= iota((256, 256), 1)).astype(F32)
    ends = jnp.dot(jnp.broadcast_to(counts, (8, 256)).astype(BF16), upto.astype(BF16), preferred_element_type=F32)[0:1]
    starts = ends - counts
    at = iota((1024, 256), 0).astype(F32)
    member = ((at >= starts) & (at < ends)).astype(F32).astype(BF16)
    sums = jnp.zeros((3, 256), F32)
    for part in three(res_ref[:, 0, :]):
        sums = sums + jnp.dot(part, member, preferred_element_type=F32)
    means = sums / counts
    owner, cell = tile_ref[...], cell_ref[...]
    gx = (owner >> 4) * CX + (cell >> 12)
    gy = ((owner >> 2) & 3) * CY + ((cell >> 7) & 31)
    gz = (owner & 3) * CZ + (cell & 127)
    code = ((gx * (TY * CY) + gy) * (TZ * CZ) + gz).astype(F32)
    both = jnp.concatenate([means, code], axis=0)
    list_ref[t] = jnp.concatenate([both[:, :128], both[:, 128:]], axis=0)

    spans = {1: (CX - 7, 1, 7), -1: (0, 72, 7), 0: (0, 8, CX)}
    rows = {1: (CY - 7, 1, 7), -1: (0, 40, 7), 0: (0, 8, CY)}
    ways = [(dx, dy) for dx in (-1, 0, 1) for dy in (-1, 0, 1) if (dx, dy) != (0, 0)]

    def inside(dx, dy):
        x, y = tx + dx, ty + dy
        return (x >= 0) & (x < TX) & (y >= 0) & (y < TY)

    def halo(n):
        dx, dy = ways[n]
        xs, xd, xn = spans[dx]
        ys, yd, yn = rows[dy]
        return pltpu.make_async_remote_copy(
            cext.at[pl.ds(OWN + xs, xn), pl.ds(8 + ys, yn)], cext.at[pl.ds(xd, xn), pl.ds(yd, yn)],
            sends.at[n], recvs.at[n], device_id=(f, t + dx * TY * TZ + dy * TZ), device_id_type=MESH)

    for dx, dy in ways:
        @pl.when(jnp.logical_not(inside(-dx, -dy)))
        def _(dx=dx, dy=dy):
            def wipe(i, c):
                cext[spans[dx][1] + i, pl.ds(rows[dy][1], rows[dy][2]), :] = jnp.zeros((rows[dy][2], 128), F32)
                return c

            lax.fori_loop(0, spans[dx][2], wipe, 0)
    lap = lap_ref[0]
    lane = iota((48, 128), 1)
    own.wait()

    def invert(k, c):
        done = [1.0 / (4.0 + lap * raw[4 * k + j]) for j in range(4)]
        for j in range(4):
            cext[OWN + 4 * k + j, pl.ds(8, CY), :] = done[j]
        return c

    lax.fori_loop(0, CX // 4, invert, 0)
    pl.semaphore_wait(barrier, TILES - 1)

    def share(i, c):
        pltpu.make_async_remote_copy(list_ref.at[t], list_ref.at[t], gsend, grecv,
                                     device_id=me ^ i, device_id_type=pl.DeviceIdType.LOGICAL).start()
        return c

    lax.fori_loop(1, TILES, share, 0)

    for n, (dx, dy) in enumerate(ways):
        @pl.when(inside(dx, dy))
        def _(n=n):
            halo(n).start()

    def lay(planes, begin, count):
        part = pl.ds(begin, count)
        done = [jnp.where(lane[:count] < RIM, 0.0, pltpu.roll(cext[i, part, :], RIM, 1)) for i in planes]
        for i, value in zip(planes, done):
            coef_ref[i, part, :] = value

    def lay_own(k, c):
        lay([OWN + 4 * k + j for j in range(4)], 8, CY)
        return c

    lax.fori_loop(0, CX // 4, lay_own, 0)
    everyone = list_ref.at[pl.ds(0, TILES - 1)]
    pltpu.make_async_copy(everyone, everyone, grecv).wait()
    many_ref[:, pl.ds(0, TILES)] = find_all(list_ref, spots, t)

    def compact(k, c):
        for i in range(2):
            pair = jnp.concatenate([squeeze(list_ref, spots, 4 * k + 2 * i + j, 0.0) for j in range(2)], axis=1)
            short_ref[pl.ds(3 * (2 * k + i), 3), :] = pair[0:3]
            spot_ref[pl.ds(2 * k + i, 1), :] = pair[3:4].astype(I32)
        return c

    lax.fori_loop(0, TILES // 4, compact, 0)
    for n, (dx, dy) in enumerate(ways):
        @pl.when(inside(-dx, -dy))
        def _(n=n):
            halo(n).wait_recv()

    def read(i):
        return cext[jnp.minimum(i, 79)]

    def fill(k, c):
        done = []
        for j in range(2):
            total = jnp.zeros((48, 128), F32)
            for h in range(8):
                plane = read(1 + 10 * h + 2 * k + j)
                for begin, shift in ((16 * h, 16 * h - 121), (16 * h + 8, 16 * h + 8)):
                    moved = pltpu.roll(plane, shift % 128, 1)
                    total = jnp.where((lane >= begin) & (lane < begin + 7), moved, total)
            done.append(total)
        for j in range(2):
            pack[2 * k + j] = done[j]
        return c

    lax.fori_loop(0, 5, fill, 0)

    def rim(up):
        return pltpu.make_async_remote_copy(
            pack, low if up else high, zsend.at[up], zrecv.at[up],
            device_id=(f, t + (1 if up else -1)), device_id_type=MESH)

    @pl.when(tz < TZ - 1)
    def _():
        rim(1).start()

    @pl.when(tz > 0)
    def _():
        rim(0).start()

    def lay_rows(k, c):
        planes = [OWN + 4 * k + j for j in range(4)]
        lay(planes, 0, 8)
        lay(planes, 40, 8)
        return c

    lax.fori_loop(0, CX // 4, lay_rows, 0)

    def lay_planes(k, c):
        lay([1 + k, 72 + k], 0, 48)
        return c

    lax.fori_loop(0, RIM, lay_planes, 0)

    def fill_b(k, c):
        done = [runs_of(read, 2 * k + j, 48, 0, SEG - RIM, 128 - ZB) for j in range(2)]
        for j in range(2):
            coef_ref[B0 + 2 * k + j, pl.ds(0, 48), :] = done[j]
        return c

    lax.fori_loop(0, RUN // 2, fill_b, 0)

    @pl.when(tz > 0)
    def _():
        rim(1).wait_recv()

        def patch(k, c):
            done = []
            for h in range(8):
                old = coef_ref[1 + 10 * h + k, pl.ds(0, 48), :]
                done.append(jnp.where(lane < RIM, pltpu.roll(low[k], (128 - 16 * h) % 128, 1), old))
            for h in range(8):
                coef_ref[1 + 10 * h + k, pl.ds(0, 48), :] = done[h]
            return c

        lax.fori_loop(0, 10, patch, 0)

    @pl.when(tz < TZ - 1)
    def _():
        rim(0).wait_recv()

        def patch(k, c):
            done = []
            for j in range(2):
                s = 2 * k + j
                value = coef_ref[B0 + s, pl.ds(0, 48), :]
                for g in range(RUNS):
                    i = RUN * g + s
                    turn = (SEG * g + SEG - RIM - 8 - 16 * (i // 10) + 256) % 128
                    inner = (lane >= SEG * g + SEG - RIM) & (lane < SEG * g + SEG)
                    value = jnp.where(inner, pltpu.roll(high[i % 10], turn, 1), value)
                done.append(value)
            for j in range(2):
                coef_ref[B0 + 2 * k + j, pl.ds(0, 48), :] = done[j]
            return c

        lax.fori_loop(0, RUN // 2, patch, 0)

    for n, (dx, dy) in enumerate(ways):
        @pl.when(inside(dx, dy))
        def _(n=n):
            halo(n).wait_send()

    @pl.when(tz < TZ - 1)
    def _():
        rim(1).wait_send()

    @pl.when(tz > 0)
    def _():
        rim(0).wait_send()

    pltpu.make_async_copy(everyone, everyone, gsend).wait()


def stencil(src, dst, base, coef, hx_ref, hy_ref, hz_ref, lo, hi, y0, nk, nh, scale):
    rk, rh, h0 = 8 * nk, 8 * nh, y0 - 1
    hr, hy_rows, kr, kl = pl.ds(h0, rh), pl.ds(y0, rh), pl.ds(y0, rk), pl.ds(h0, rk)

    def swirl(x):
        vx, vy, vz = src[0, x, hr, :], src[1, x, hr, :], src[2, x, hr, :]
        vyz, vxz = pltpu.roll(vy, 127, 1), pltpu.roll(vx, 127, 1)
        hx_ref[x, hr, :] = (src[2, x, hy_rows, :] - vz) - (vyz - vy)
        hy_ref[x, hr, :] = (vxz - vx) - (src[2, x + 1, hr, :] - vz)
        hz_ref[x, hr, :] = (src[1, x + 1, hr, :] - vy) - (src[0, x, hy_rows, :] - vx)

    def relax(x):
        hx, hy, hz = hx_ref[x, kr, :], hy_ref[x, kr, :], hz_ref[x, kr, :]
        kx = (hz - hz_ref[x, kl, :]) - (hy - pltpu.roll(hy, 1, 1))
        ky = (hx - pltpu.roll(hx, 1, 1)) - (hz - hz_ref[x - 1, kr, :])
        kz = (hy - hy_ref[x - 1, kr, :]) - (hx - hx_ref[x, kl, :])
        c = coef[x, kr, :] if scale == 1.0 else scale * coef[x, kr, :]
        keep = (scale if base is not src else 1.0 + scale) + 4.0 * c
        for i, k in enumerate((kx, ky, kz)):
            new = keep * src[i, x, kr, :] - c * k
            if base is not None and base is not src:
                new = base[i, x, kr, :] + new
            dst[i, x, kr, :] = new

    for i in range(-1, NP):
        swirl(lo + i)

    def body(k, c):
        x = jnp.minimum(lo + NP * k, hi - NP)
        for i in range(NP):
            relax(x + i)
        for i in range(NP):
            swirl(x + NP + i)
        return c

    lax.fori_loop(0, (hi - lo + NP - 1) // NP, body, 0)


def relax_kernel(list_hbm, lap_ref, short_s, spot_s, many_s, coef_hbm, cond_hbm, field_hbm, out_ref,
                 u, p, q, hx_ref, hy_ref, hz_ref, coef, cond, field, list_ref, spots, more, more_i, more_s, more_is, sems):
    t = lax.axis_index("tile")
    loads = [pltpu.make_async_copy(a, b, sems.at[n])
             for n, (a, b) in enumerate(((coef_hbm, coef), (cond_hbm, cond), (field_hbm, field)))]
    for copy in loads:
        copy.start()

    flat = u.reshape(3, PLANES * YR, 128)

    def clear(i, c):
        for k in range(3):
            u[k, i] = jnp.zeros((YR, 128), F32)
        return c

    lax.fori_loop(0, PLANES, clear, 0)
    lane_id = iota((1, 128), 1)

    def drop(k, most):
        for i in range(2):
            count = many_s[0, 2 * k + i]

            def read(j, i=i):
                at, where = 384 * k + KEEP * i + 4 * j, 128 * k + KEEP * i + 4 * j
                return (tuple(spot_s[where + m] for m in range(4)),
                        tuple(short_s[at + 128 * n + m] for m in range(4) for n in range(3)))

            def four(j, held):
                coming = read(j + 1)
                for m in range(4):
                    here = lane_id == (held[0][m] & 127)
                    row = pl.ds(held[0][m] >> 7, 1)
                    for n in range(3):
                        flat[n, row, :] += jnp.where(here, held[1][3 * m + n], 0.0)
                return coming

            lax.fori_loop(0, (jnp.minimum(count, KEEP) + 3) // 4, four, read(0))
            most = jnp.maximum(most, count)
        return most

    most = lax.fori_loop(0, TILES // 2, drop, 0)

    @pl.when(most > KEEP)
    def _():
        copy = pltpu.make_async_copy(list_hbm, list_ref, sems.at[3])
        copy.start()
        copy.wait()
        find_all(list_ref, spots, t)

        def rest(b, c):
            count = many_s[0, b]

            def chunk(j, c2):
                got = squeeze(list_ref, spots, b, (KEEP * j).astype(F32))
                more[pl.ds(0, 3), pl.ds(0, KEEP)] = got[0:3]
                spot = got[3:4].astype(I32)
                more_i[pl.ds(0, 1), pl.ds(0, KEEP)] = spot
                copies = [pltpu.make_async_copy(more, more_s, sems.at[3]), pltpu.make_async_copy(more_i, more_is, sems.at[4])]
                for copy in copies:
                    copy.start()
                for copy in copies:
                    copy.wait()

                def one(k, c3):
                    spot = more_is[0, k]
                    here = lane_id == (spot & 127)
                    for n in range(3):
                        flat[n, pl.ds(spot >> 7, 1), :] += jnp.where(here, more_s[n, k], 0.0)
                    return c3

                return lax.fori_loop(0, jnp.minimum(count - KEEP * j, KEEP), one, c2)

            return lax.fori_loop(1, (count + KEEP - 1) // KEEP, chunk, c)

        lax.fori_loop(0, TILES, rest, 0)

    loads[0].wait()

    def scale_b(k, c):
        done = []
        for j in range(2):
            s = 2 * k + j
            for i in range(3):
                value = runs_of(lambda k: u[i, jnp.minimum(k, 79), pl.ds(0, 48), :], s, 48, 0, 14, 128 - ZB - RIM)
                done.append((i, B0 + s, 0.5 * coef[B0 + s, pl.ds(0, 48), :] * (value + u[i, B0 + s, pl.ds(0, 48), :])))
        for i, s, value in done:
            u[i, s, pl.ds(0, 48), :] = value
        return c

    lax.fori_loop(0, RUN // 2, scale_b, 0)

    def scale_a(k, c):
        for i in range(3):
            u[i, k] = 0.5 * coef[k] * u[i, k]
        return c

    lax.fori_loop(0, 80, scale_a, 0)

    plan = [(u, p, u, 0.5), (p, q, None, 1.0), (q, u, p, 0.25), (u, p, None, 1.0), (p, q, None, 1.0),
            (q, p, None, 1.0), (p, q, u, 0.0625)]
    for n, (src, dst, base, scale) in enumerate(plan):
        e = RIM - 1 - n
        nk, nh = -(-(CY + 2 * e) // 8), -(-(CY + 1 + 2 * e) // 8)
        for i in range(3):
            src[i, B0 - 1] = pltpu.roll(src[i, B0 + RUN - 1], SEG, 1)
            src[i, B0 + RUN] = pltpu.roll(src[i, B0], 128 - SEG, 1)
        stencil(src, dst, base, coef, hx_ref, hy_ref, hz_ref, B0, B0 + RUN, 8 - e, nk, nh, scale)
        stencil(src, dst, base, coef, hx_ref, hy_ref, hz_ref, OWN - e, OWN + CX + e, 8 - e, nk, nh, scale)

    loads[1].wait()
    loads[2].wait()
    lane = iota((CY, 128), 1)
    own_y = pl.ds(8, CY)
    lap = lap_ref[0]
    for g in range(RUNS):
        begin, end = max(0, RUN * g - RIM), min(CX, RUN * (g + 1) - RIM)

        def combine(k, c, g=g, begin=begin, end=end):
            for j in range(4):
                x = jnp.minimum(begin + 4 * k + j, end - 1)
                total = jnp.zeros((CY, 128), F32)
                for i in range(3):
                    rims = q[i, B0 + x + RIM - RUN * g, own_y, :]
                    value = jnp.where(lane >= CZ - 2 * RIM, pltpu.roll(rims, (ZB - SEG * g) % 128, 1),
                                      pltpu.roll(q[i, OWN + x, own_y, :], 128 - RIM, 1))
                    total = total + field[i, x].astype(F32) * value
                out_ref[x] = -lap * cond[x] * total
            return c

        lax.fori_loop(0, (end - begin + 3) // 4, combine, 0)


def spread_kernel(part_ref, out_ref, send, recv, lsem):
    f, t = lax.axis_index("freq"), lax.axis_index("tile")
    me = f * TILES + t
    barrier = pltpu.get_barrier_semaphore()

    def greet(i, c):
        pl.semaphore_signal(barrier, inc=1, device_id=me ^ i, device_id_type=pl.DeviceIdType.LOGICAL)
        return c

    lax.fori_loop(1, 2 * TILES, greet, 0)
    mine = pltpu.make_async_copy(part_ref.at[t, pl.ds(f * 16, 16)], out_ref.at[me], lsem)
    mine.start()
    pl.semaphore_wait(barrier, 2 * TILES - 1)

    def share(i, c):
        d = me ^ i
        pltpu.make_async_remote_copy(part_ref.at[d & (TILES - 1), pl.ds((d >> 6) * 16, 16)], out_ref.at[me], send, recv,
                                     device_id=d, device_id_type=pl.DeviceIdType.LOGICAL).start()
        return c

    lax.fori_loop(1, 2 * TILES, share, 0)
    mine.wait()
    others = out_ref.at[pl.ds(0, 2 * TILES - 1)]
    for sem in (send, recv):
        pltpu.make_async_copy(others, others, sem).wait()


def local(residual, row_counts, recv_owner, recv_cell, conductivity, laplace, forward_field):
    smem = pl.BlockSpec(memory_space=pltpu.SMEM)
    cond = conductivity[0]
    lists, coef, short, spot, many = pl.pallas_call(
        gather_kernel,
        name="gather_lists",
        out_shape=(jax.ShapeDtypeStruct((TILES, 8, 128), F32), jax.ShapeDtypeStruct((PLANES, YR, 128), F32),
                   jax.ShapeDtypeStruct((104, 128), F32), jax.ShapeDtypeStruct((40, 128), I32),
                   jax.ShapeDtypeStruct((8, 128), I32)),
        in_specs=[hbm(), hbm(), hbm(), hbm(), smem, hbm()],
        out_specs=(vmem(), vmem(), vmem(), vmem(), vmem()),
        scratch_shapes=[
            pltpu.VMEM((3, 1, 1024), F32),
            pltpu.VMEM((1, 256), I32),
            pltpu.VMEM((1, 256), I32),
            pltpu.VMEM((1, 256), I32),
            pltpu.VMEM((2, TILES, 256), F32),
            pltpu.VMEM((CX, CY, CZ), F32),
            pltpu.VMEM((82, 48, 128), F32),
            pltpu.VMEM((10, 48, 128), F32),
            pltpu.VMEM((10, 48, 128), F32),
            pltpu.VMEM((10, 48, 128), F32),
            pltpu.SemaphoreType.DMA((8,)),
            pltpu.SemaphoreType.DMA((8,)),
            pltpu.SemaphoreType.DMA((2,)),
            pltpu.SemaphoreType.DMA((2,)),
            pltpu.SemaphoreType.DMA,
            pltpu.SemaphoreType.DMA,
            pltpu.SemaphoreType.DMA((5,)),
        ],
        compiler_params=pltpu.CompilerParams(collective_id=0, has_side_effects=True, vmem_limit_bytes=62 * 2**20),
    )(residual.transpose(1, 0, 2), row_counts, recv_owner.reshape(1, -1), recv_cell.reshape(1, -1), laplace, cond)
    partial = pl.pallas_call(
        relax_kernel,
        name="relax_tile",
        out_shape=jax.ShapeDtypeStruct((CX, CY, CZ), F32),
        in_specs=[hbm(), smem, smem, smem, smem, hbm(), hbm(), hbm()],
        out_specs=vmem(),
        scratch_shapes=[pltpu.VMEM((3, PLANES, YR, 128), F32)] * 3
        + [pltpu.VMEM((PLANES, YR, 128), F32)] * 4
        + [
            pltpu.VMEM((CX, CY, CZ), F32),
            pltpu.VMEM((3, CX, CY, CZ), BF16),
            pltpu.VMEM((TILES, 8, 128), F32),
            pltpu.VMEM((2, TILES, 256), F32),
            pltpu.VMEM((8, 128), F32),
            pltpu.VMEM((8, 128), I32),
            pltpu.SMEM((8, 128), F32),
            pltpu.SMEM((8, 128), I32),
            pltpu.SemaphoreType.DMA((5,)),
        ],
        compiler_params=pltpu.CompilerParams(vmem_limit_bytes=62 * 2**20),
    )(lists, laplace, short.reshape(-1), spot.reshape(-1), many, coef, cond, forward_field[0, 0])
    both = pl.pallas_call(
        spread_kernel,
        name="spread_rows",
        out_shape=jax.ShapeDtypeStruct((2 * TILES, 16, CZ), F32),
        in_specs=[hbm()],
        out_specs=hbm(),
        scratch_shapes=[pltpu.SemaphoreType.DMA] * 3,
        compiler_params=pltpu.CompilerParams(collective_id=1, has_side_effects=True, vmem_limit_bytes=62 * 2**20),
    )(partial)
    return (both[:TILES] + both[TILES:])[:, None]


def solution(mesh):
    placed = (
        P("freq", None, "tile"),
        P("tile", None),
        P("tile", None),
        P("tile"),
        P("tile", None, None, None),
        P("freq"),
        P("freq", "tile", None, None, None, None),
    )
    return jax.shard_map(
        local, mesh=mesh, in_specs=placed, out_specs=P(None, "tile", "freq", None), check_vma=False
    )
```

```python
import functools

import jax
import jax.numpy as jnp
from jax import lax
from jax.experimental import pallas as pl
from jax.experimental.pallas import tpu as pltpu
from jax.sharding import PartitionSpec as P

F32 = jnp.float32
BF16 = jnp.bfloat16
I32 = jnp.int32
MESH = pl.DeviceIdType.MESH

TX, TY, TZ = 4, 4, 4
TILES = 64
CX, CY, CZ = 64, 32, 128
NP_A, NP_B = 8, 10
RIM = 7

YR = 56
B0 = 81
RUN = 20
SEG = 28
RUNS = 4
ZB = CZ + RIM - SEG
PLANES = 112
KEEP = 64
OWN = 8


def iota(shape, dim):
    return lax.broadcasted_iota(I32, shape, dim)


def vmem():
    return pl.BlockSpec(memory_space=pltpu.VMEM)


def hbm():
    return pl.BlockSpec(memory_space=pl.ANY)


def place(t):
    return t // (TY * TZ), (t // TZ) % TY, t % TZ


def three(value):
    hi = value.astype(BF16)
    rest = value - hi.astype(F32)
    mid = rest.astype(BF16)
    low = (rest - mid.astype(F32)).astype(BF16)
    return hi, mid, low


def runs_of(read, s, rows, begin, end, shift):
    lane = iota((rows, 128), 1)
    total = jnp.zeros((rows, 128), F32)
    for g in range(RUNS):
        plane = read(1 + RUN * g + s)
        moved = pltpu.roll(plane, (SEG * g + shift) % 128, 1)
        total = jnp.where((lane >= SEG * g + begin) & (lane < SEG * g + end), moved, total)
    return total


def locate(code, tx, ty, tz):
    x = (code >> 16) - tx * CX + RIM
    y = ((code >> 9) & 127) - ty * CY + RIM
    z = (code & 511) - tz * CZ
    ok = (x >= 0) & (x < CX + 2 * RIM) & (y >= 0) & (y < CY + 2 * RIM) & (z >= -RIM) & (z < CZ + RIM)
    run = sum((x >= RUN * g).astype(I32) for g in range(1, RUNS))
    in_a = z < 128 - RIM
    plane = jnp.where(in_a, x + 1, x - RUN * run + B0)
    lane = jnp.where(in_a, z + RIM, SEG * run + z - ZB)
    return ok, jnp.where(ok, (plane * YR + y + 1) * 128 + lane, 0).astype(F32)


def find_all(list_ref, spots, t):
    code = jnp.concatenate([list_ref[:, 3, :], list_ref[:, 7, :]], axis=1).astype(I32)
    ok, spot = locate(code, *place(t))
    before = (iota((256, 256), 0) < iota((256, 256), 1)).astype(F32).astype(BF16)
    flag = ok.astype(F32)
    rank = jnp.dot(flag.astype(BF16), before, preferred_element_type=F32)
    spots[0] = spot
    spots[1] = jnp.where(ok, rank, -1.0)
    ones = jnp.ones((8, 256), BF16)
    return lax.dot_general(ones, flag.astype(BF16), (((1,), (1,)), ((), ())), preferred_element_type=F32).astype(I32)


def squeeze(list_ref, spots, b, first):
    place_k = iota((KEEP, 256), 0).astype(F32)
    values = jnp.concatenate([list_ref[b, pl.ds(0, 3), :], list_ref[b, pl.ds(4, 3), :]], axis=1)
    both = jnp.concatenate([values, spots[0, pl.ds(b, 1), :]], axis=0)
    pick = (place_k == spots[1, pl.ds(b, 1), :] - first).astype(F32).astype(BF16)
    parts = jnp.concatenate([part.astype(F32) for part in three(both)] + [jnp.zeros((4, 256), F32)], axis=0).astype(BF16)
    got = lax.dot_general(parts, pick, (((1,), (1,)), ((), ())), preferred_element_type=F32)
    return (got[0:4] + got[4:8]) + got[8:12]


def gather_kernel(res_hbm, cnt_hbm, tile_hbm, cell_hbm, lap_ref, cond_ref, list_ref, coef_ref, short_ref, spot_ref, many_ref,
                  res_ref, cnt_ref, tile_ref, cell_ref, spots, raw, cext, pack, low, high, sends, recvs, zsend, zrecv, gsend, grecv, lsem):
    f, t = lax.axis_index("freq"), lax.axis_index("tile")
    me = f * TILES + t
    tx, ty, tz = place(t)
    barrier = pltpu.get_barrier_semaphore()

    def greet(i, c):
        pl.semaphore_signal(barrier, inc=1, device_id=me ^ i, device_id_type=pl.DeviceIdType.LOGICAL)
        return c

    lax.fori_loop(1, TILES, greet, 0)
    own = pltpu.make_async_copy(cond_ref, raw, lsem.at[0])
    own.start()
    loads = [pltpu.make_async_copy(a, b, lsem.at[n + 1])
             for n, (a, b) in enumerate(((res_hbm, res_ref), (cnt_hbm, cnt_ref), (tile_hbm, tile_ref), (cell_hbm, cell_ref)))]
    for copy in loads:
        copy.start()
    for copy in loads:
        copy.wait()

    counts = cnt_ref[...].astype(F32)
    upto = (iota((256, 256), 0) <= iota((256, 256), 1)).astype(F32)
    ends = jnp.dot(jnp.broadcast_to(counts, (8, 256)).astype(BF16), upto.astype(BF16), preferred_element_type=F32)[0:1]
    starts = ends - counts
    at = iota((1024, 256), 0).astype(F32)
    member = ((at >= starts) & (at < ends)).astype(F32).astype(BF16)
    sums = jnp.zeros((3, 256), F32)
    for part in three(res_ref[:, 0, :]):
        sums = sums + jnp.dot(part, member, preferred_element_type=F32)
    means = sums / counts
    owner, cell = tile_ref[...], cell_ref[...]
    gx = (owner >> 4) * CX + (cell >> 12)
    gy = ((owner >> 2) & 3) * CY + ((cell >> 7) & 31)
    gz = (owner & 3) * CZ + (cell & 127)
    code = ((gx * (TY * CY) + gy) * (TZ * CZ) + gz).astype(F32)
    both = jnp.concatenate([means, code], axis=0)
    list_ref[t] = jnp.concatenate([both[:, :128], both[:, 128:]], axis=0)

    spans = {1: (CX - 7, 1, 7), -1: (0, 72, 7), 0: (0, 8, CX)}
    rows = {1: (CY - 7, 1, 7), -1: (0, 40, 7), 0: (0, 8, CY)}
    ways = [(dx, dy) for dx in (-1, 0, 1) for dy in (-1, 0, 1) if (dx, dy) != (0, 0)]

    def inside(dx, dy):
        x, y = tx + dx, ty + dy
        return (x >= 0) & (x < TX) & (y >= 0) & (y < TY)

    def halo(n):
        dx, dy = ways[n]
        xs, xd, xn = spans[dx]
        ys, yd, yn = rows[dy]
        return pltpu.make_async_remote_copy(
            cext.at[pl.ds(OWN + xs, xn), pl.ds(8 + ys, yn)], cext.at[pl.ds(xd, xn), pl.ds(yd, yn)],
            sends.at[n], recvs.at[n], device_id=(f, t + dx * TY * TZ + dy * TZ), device_id_type=MESH)

    for dx, dy in ways:
        @pl.when(jnp.logical_not(inside(-dx, -dy)))
        def _(dx=dx, dy=dy):
            def wipe(i, c):
                cext[spans[dx][1] + i, pl.ds(rows[dy][1], rows[dy][2]), :] = jnp.zeros((rows[dy][2], 128), F32)
                return c

            lax.fori_loop(0, spans[dx][2], wipe, 0)
    lap = lap_ref[0]
    lane = iota((48, 128), 1)
    own.wait()

    def invert(k, c):
        done = [1.0 / (4.0 + lap * raw[4 * k + j]) for j in range(4)]
        for j in range(4):
            cext[OWN + 4 * k + j, pl.ds(8, CY), :] = done[j]
        return c

    lax.fori_loop(0, CX // 4, invert, 0)
    pl.semaphore_wait(barrier, TILES - 1)

    def share(i, c):
        pltpu.make_async_remote_copy(list_ref.at[t], list_ref.at[t], gsend, grecv,
                                     device_id=me ^ i, device_id_type=pl.DeviceIdType.LOGICAL).start()
        return c

    lax.fori_loop(1, TILES, share, 0)

    for n, (dx, dy) in enumerate(ways):
        @pl.when(inside(dx, dy))
        def _(n=n):
            halo(n).start()

    def lay(planes, begin, count):
        part = pl.ds(begin, count)
        done = [jnp.where(lane[:count] < RIM, 0.0, pltpu.roll(cext[i, part, :], RIM, 1)) for i in planes]
        for i, value in zip(planes, done):
            coef_ref[i, part, :] = value

    def lay_own(k, c):
        lay([OWN + 4 * k + j for j in range(4)], 8, CY)
        return c

    lax.fori_loop(0, CX // 4, lay_own, 0)
    everyone = list_ref.at[pl.ds(0, TILES - 1)]
    pltpu.make_async_copy(everyone, everyone, grecv).wait()
    many_ref[:, pl.ds(0, TILES)] = find_all(list_ref, spots, t)

    def compact(k, c):
        for i in range(2):
            pair = jnp.concatenate([squeeze(list_ref, spots, 4 * k + 2 * i + j, 0.0) for j in range(2)], axis=1)
            short_ref[pl.ds(3 * (2 * k + i), 3), :] = pair[0:3]
            spot_ref[pl.ds(2 * k + i, 1), :] = pair[3:4].astype(I32)
        return c

    lax.fori_loop(0, TILES // 4, compact, 0)
    for n, (dx, dy) in enumerate(ways):
        @pl.when(inside(-dx, -dy))
        def _(n=n):
            halo(n).wait_recv()

    def read(i):
        return cext[jnp.minimum(i, 79)]

    def fill(k, c):
        done = []
        for j in range(2):
            total = jnp.zeros((48, 128), F32)
            for h in range(8):
                plane = read(1 + 10 * h + 2 * k + j)
                for begin, shift in ((16 * h, 16 * h - 121), (16 * h + 8, 16 * h + 8)):
                    moved = pltpu.roll(plane, shift % 128, 1)
                    total = jnp.where((lane >= begin) & (lane < begin + 7), moved, total)
            done.append(total)
        for j in range(2):
            pack[2 * k + j] = done[j]
        return c

    lax.fori_loop(0, 5, fill, 0)

    def rim(up):
        return pltpu.make_async_remote_copy(
            pack, low if up else high, zsend.at[up], zrecv.at[up],
            device_id=(f, t + (1 if up else -1)), device_id_type=MESH)

    @pl.when(tz < TZ - 1)
    def _():
        rim(1).start()

    @pl.when(tz > 0)
    def _():
        rim(0).start()

    def lay_rows(k, c):
        planes = [OWN + 4 * k + j for j in range(4)]
        lay(planes, 0, 8)
        lay(planes, 40, 8)
        return c

    lax.fori_loop(0, CX // 4, lay_rows, 0)

    def lay_planes(k, c):
        lay([1 + k, 72 + k], 0, 48)
        return c

    lax.fori_loop(0, RIM, lay_planes, 0)

    def fill_b(k, c):
        done = [runs_of(read, 2 * k + j, 48, 0, SEG - RIM, 128 - ZB) for j in range(2)]
        for j in range(2):
            coef_ref[B0 + 2 * k + j, pl.ds(0, 48), :] = done[j]
        return c

    lax.fori_loop(0, RUN // 2, fill_b, 0)

    @pl.when(tz > 0)
    def _():
        rim(1).wait_recv()

        def patch(k, c):
            done = []
            for h in range(8):
                old = coef_ref[1 + 10 * h + k, pl.ds(0, 48), :]
                done.append(jnp.where(lane < RIM, pltpu.roll(low[k], (128 - 16 * h) % 128, 1), old))
            for h in range(8):
                coef_ref[1 + 10 * h + k, pl.ds(0, 48), :] = done[h]
            return c

        lax.fori_loop(0, 10, patch, 0)

    @pl.when(tz < TZ - 1)
    def _():
        rim(0).wait_recv()

        def patch(k, c):
            done = []
            for j in range(2):
                s = 2 * k + j
                value = coef_ref[B0 + s, pl.ds(0, 48), :]
                for g in range(RUNS):
                    i = RUN * g + s
                    turn = (SEG * g + SEG - RIM - 8 - 16 * (i // 10) + 256) % 128
                    inner = (lane >= SEG * g + SEG - RIM) & (lane < SEG * g + SEG)
                    value = jnp.where(inner, pltpu.roll(high[i % 10], turn, 1), value)
                done.append(value)
            for j in range(2):
                coef_ref[B0 + 2 * k + j, pl.ds(0, 48), :] = done[j]
            return c

        lax.fori_loop(0, RUN // 2, patch, 0)

    for n, (dx, dy) in enumerate(ways):
        @pl.when(inside(dx, dy))
        def _(n=n):
            halo(n).wait_send()

    @pl.when(tz < TZ - 1)
    def _():
        rim(1).wait_send()

    @pl.when(tz > 0)
    def _():
        rim(0).wait_send()

    pltpu.make_async_copy(everyone, everyone, gsend).wait()


def stencil(src, dst, base, coef, hx_ref, hy_ref, hz_ref, lo, hi, y0, nk, nh, scale, step):
    rk, rh, h0 = 8 * nk, 8 * nh, y0 - 1
    hr, hy_rows, kr, kl = pl.ds(h0, rh), pl.ds(y0, rh), pl.ds(y0, rk), pl.ds(h0, rk)

    def swirl(x):
        vx, vy, vz = src[0, x, hr, :], src[1, x, hr, :], src[2, x, hr, :]
        vyz, vxz = pltpu.roll(vy, 127, 1), pltpu.roll(vx, 127, 1)
        hx_ref[x, hr, :] = (src[2, x, hy_rows, :] - vz) - (vyz - vy)
        hy_ref[x, hr, :] = (vxz - vx) - (src[2, x + 1, hr, :] - vz)
        hz_ref[x, hr, :] = (src[1, x + 1, hr, :] - vy) - (src[0, x, hy_rows, :] - vx)

    def relax(x):
        hx, hy, hz = hx_ref[x, kr, :], hy_ref[x, kr, :], hz_ref[x, kr, :]
        kx = (hz - hz_ref[x, kl, :]) - (hy - pltpu.roll(hy, 1, 1))
        ky = (hx - pltpu.roll(hx, 1, 1)) - (hz - hz_ref[x - 1, kr, :])
        kz = (hy - hy_ref[x - 1, kr, :]) - (hx - hx_ref[x, kl, :])
        c = coef[x, kr, :] if scale == 1.0 else scale * coef[x, kr, :]
        keep = (scale if base is not src else 1.0 + scale) + 4.0 * c
        for i, k in enumerate((kx, ky, kz)):
            new = keep * src[i, x, kr, :] - c * k
            if base is not None and base is not src:
                new = base[i, x, kr, :] + new
            dst[i, x, kr, :] = new

    for i in range(-1, step):
        swirl(lo + i)

    def body(k, c):
        x = jnp.minimum(lo + step * k, hi - step)
        for i in range(step):
            relax(x + i)
        for i in range(step):
            swirl(x + step + i)
        return c

    lax.fori_loop(0, (hi - lo + step - 1) // step, body, 0)


def relax_kernel(list_hbm, lap_ref, short_hbm, spot_hbm, many_hbm, coef_hbm, cond_hbm, field_hbm, out_ref,
                 u, p, q, hx_ref, hy_ref, hz_ref, short_s, spot_s, many_s, rows, coef, cond, field, list_ref, spots, more, more_i, more_s, more_is, sems):
    t = lax.axis_index("tile")
    loads = [pltpu.make_async_copy(a, b, sems.at[n])
             for n, (a, b) in enumerate(((coef_hbm, coef), (cond_hbm, cond), (field_hbm, field)))]
    lists = [pltpu.make_async_copy(a, b, sems.at[n + 5])
             for n, (a, b) in enumerate(((many_hbm, many_s), (spot_hbm, spot_s), (short_hbm, short_s)))]
    for copy in lists + loads:
        copy.start()

    flat = u.reshape(3, PLANES * YR, 128)

    def clear(i, c):
        for k in range(3):
            u[k, i] = jnp.zeros((YR, 128), F32)
        return c

    lax.fori_loop(0, PLANES, clear, 0)
    lane_id = iota((1, 128), 1)
    for copy in lists:
        copy.wait()

    def drop(k, most):
        for i in range(2):
            count = many_s[0, 2 * k + i]

            def read(j, i=i):
                at, where = 384 * k + KEEP * i + 4 * j, 128 * k + KEEP * i + 4 * j
                return (tuple(spot_s[where + m] for m in range(4)),
                        tuple(short_s[at + 128 * n + m] for m in range(4) for n in range(3)))

            def four(j, held):
                coming = read(j + 1)
                for m in range(4):
                    here = lane_id == (held[0][m] & 127)
                    row = pl.ds(held[0][m] >> 7, 1)
                    for n in range(3):
                        flat[n, row, :] += jnp.where(here, held[1][3 * m + n], 0.0)
                return coming

            lax.fori_loop(0, (jnp.minimum(count, KEEP) + 3) // 4, four, read(0))
            most = jnp.maximum(most, count)
        return most

    most = lax.fori_loop(0, TILES // 2, drop, 0)

    @pl.when(most > KEEP)
    def _():
        copy = pltpu.make_async_copy(list_hbm, list_ref, sems.at[3])
        copy.start()
        copy.wait()
        find_all(list_ref, spots, t)

        def rest(b, c):
            count = many_s[0, b]

            def chunk(j, c2):
                got = squeeze(list_ref, spots, b, (KEEP * j).astype(F32))
                more[pl.ds(0, 3), pl.ds(0, KEEP)] = got[0:3]
                spot = got[3:4].astype(I32)
                more_i[pl.ds(0, 1), pl.ds(0, KEEP)] = spot
                copies = [pltpu.make_async_copy(more, more_s, sems.at[3]), pltpu.make_async_copy(more_i, more_is, sems.at[4])]
                for copy in copies:
                    copy.start()
                for copy in copies:
                    copy.wait()

                def one(k, c3):
                    spot = more_is[0, k]
                    here = lane_id == (spot & 127)
                    for n in range(3):
                        flat[n, pl.ds(spot >> 7, 1), :] += jnp.where(here, more_s[n, k], 0.0)
                    return c3

                return lax.fori_loop(0, jnp.minimum(count - KEEP * j, KEEP), one, c2)

            return lax.fori_loop(1, (count + KEEP - 1) // KEEP, chunk, c)

        lax.fori_loop(0, TILES, rest, 0)

    loads[0].wait()

    def scale_b(k, c):
        done = []
        for j in range(2):
            s = 2 * k + j
            for i in range(3):
                value = runs_of(lambda k: u[i, jnp.minimum(k, 79), pl.ds(0, 48), :], s, 48, 0, 14, 128 - ZB - RIM)
                done.append((i, B0 + s, 0.5 * coef[B0 + s, pl.ds(0, 48), :] * (value + u[i, B0 + s, pl.ds(0, 48), :])))
        for i, s, value in done:
            u[i, s, pl.ds(0, 48), :] = value
        return c

    lax.fori_loop(0, RUN // 2, scale_b, 0)

    def scale_a(k, c):
        for i in range(3):
            u[i, k] = 0.5 * coef[k] * u[i, k]
        return c

    lax.fori_loop(0, 80, scale_a, 0)

    plan = [(u, p, u, 0.5), (p, q, None, 1.0), (q, u, p, 0.25), (u, p, None, 1.0), (p, q, None, 1.0),
            (q, p, None, 1.0), (p, q, u, 0.0625)]
    for n, (src, dst, base, scale) in enumerate(plan):
        e = RIM - 1 - n
        nk, nh = -(-(CY + 2 * e) // 8), -(-(CY + 1 + 2 * e) // 8)
        for i in range(3):
            src[i, B0 - 1] = pltpu.roll(src[i, B0 + RUN - 1], SEG, 1)
            src[i, B0 + RUN] = pltpu.roll(src[i, B0], 128 - SEG, 1)
        stencil(src, dst, base, coef, hx_ref, hy_ref, hz_ref, B0, B0 + RUN, 8 - e, nk, nh, scale, NP_B)
        stencil(src, dst, base, coef, hx_ref, hy_ref, hz_ref, OWN - e, OWN + CX + e, 8 - e, nk, nh, scale, NP_A)

    loads[1].wait()
    loads[2].wait()
    lane = iota((CY, 128), 1)
    own_y = pl.ds(8, CY)
    leaving = []
    lap = lap_ref[0]
    for g in range(RUNS):
        begin, end = max(0, RUN * g - RIM), min(CX, RUN * (g + 1) - RIM)

        def combine(k, c, g=g, begin=begin, end=end):
            for j in range(4):
                x = jnp.minimum(begin + 4 * k + j, end - 1)
                total = jnp.zeros((CY, 128), F32)
                for i in range(3):
                    rims = q[i, B0 + x + RIM - RUN * g, own_y, :]
                    value = jnp.where(lane >= CZ - 2 * RIM, pltpu.roll(rims, (ZB - SEG * g) % 128, 1),
                                      pltpu.roll(q[i, OWN + x, own_y, :], 128 - RIM, 1))
                    total = total + field[i, x].astype(F32) * value
                rows[x] = -lap * cond[x] * total
            return c

        lax.fori_loop(0, (end - begin + 3) // 4, combine, 0)
        made = pltpu.make_async_copy(rows.at[pl.ds(begin, end - begin)], out_ref.at[pl.ds(begin, end - begin)], sems.at[8 + g])
        made.start()
        leaving.append(made)
    for made in leaving:
        made.wait()


def spread_kernel(part_ref, out_ref, send, recv, lsem):
    f, t = lax.axis_index("freq"), lax.axis_index("tile")
    me = f * TILES + t
    barrier = pltpu.get_barrier_semaphore()

    def greet(i, c):
        pl.semaphore_signal(barrier, inc=1, device_id=me ^ i, device_id_type=pl.DeviceIdType.LOGICAL)
        return c

    lax.fori_loop(1, 2 * TILES, greet, 0)
    mine = pltpu.make_async_copy(part_ref.at[t, pl.ds(f * 16, 16)], out_ref.at[me], lsem)
    mine.start()
    pl.semaphore_wait(barrier, 2 * TILES - 1)

    def share(i, c):
        d = me ^ i
        pltpu.make_async_remote_copy(part_ref.at[d & (TILES - 1), pl.ds((d >> 6) * 16, 16)], out_ref.at[me], send, recv,
                                     device_id=d, device_id_type=pl.DeviceIdType.LOGICAL).start()
        return c

    lax.fori_loop(1, 2 * TILES, share, 0)
    mine.wait()
    others = out_ref.at[pl.ds(0, 2 * TILES - 1)]
    for sem in (send, recv):
        pltpu.make_async_copy(others, others, sem).wait()


def add_kernel(both_ref, out_ref):
    def body(k, c):
        done = [both_ref[8 * k + j] + both_ref[TILES + 8 * k + j] for j in range(8)]
        for j in range(8):
            out_ref[8 * k + j, 0] = done[j]
        return c

    lax.fori_loop(0, TILES // 8, body, 0)


def local(residual, row_counts, recv_owner, recv_cell, conductivity, laplace, forward_field):
    smem = pl.BlockSpec(memory_space=pltpu.SMEM)
    cond = conductivity[0]
    lists, coef, short, spot, many = pl.pallas_call(
        gather_kernel,
        name="gather_lists",
        out_shape=(jax.ShapeDtypeStruct((TILES, 8, 128), F32), jax.ShapeDtypeStruct((PLANES, YR, 128), F32),
                   jax.ShapeDtypeStruct((104, 128), F32), jax.ShapeDtypeStruct((40, 128), I32),
                   jax.ShapeDtypeStruct((8, 128), I32)),
        in_specs=[hbm(), hbm(), hbm(), hbm(), smem, hbm()],
        out_specs=(vmem(), vmem(), vmem(), vmem(), vmem()),
        scratch_shapes=[
            pltpu.VMEM((3, 1, 1024), F32),
            pltpu.VMEM((1, 256), I32),
            pltpu.VMEM((1, 256), I32),
            pltpu.VMEM((1, 256), I32),
            pltpu.VMEM((2, TILES, 256), F32),
            pltpu.VMEM((CX, CY, CZ), F32),
            pltpu.VMEM((82, 48, 128), F32),
            pltpu.VMEM((10, 48, 128), F32),
            pltpu.VMEM((10, 48, 128), F32),
            pltpu.VMEM((10, 48, 128), F32),
            pltpu.SemaphoreType.DMA((8,)),
            pltpu.SemaphoreType.DMA((8,)),
            pltpu.SemaphoreType.DMA((2,)),
            pltpu.SemaphoreType.DMA((2,)),
            pltpu.SemaphoreType.DMA,
            pltpu.SemaphoreType.DMA,
            pltpu.SemaphoreType.DMA((5,)),
        ],
        compiler_params=pltpu.CompilerParams(collective_id=0, has_side_effects=True, vmem_limit_bytes=62 * 2**20),
    )(residual.transpose(1, 0, 2), row_counts, recv_owner.reshape(1, -1), recv_cell.reshape(1, -1), laplace, cond)
    partial = pl.pallas_call(
        relax_kernel,
        name="relax_tile",
        out_shape=jax.ShapeDtypeStruct((CX, CY, CZ), F32),
        in_specs=[hbm(), smem, hbm(), hbm(), hbm(), hbm(), hbm(), hbm()],
        out_specs=hbm(),
        scratch_shapes=[pltpu.VMEM((3, PLANES, YR, 128), F32)] * 3
        + [pltpu.VMEM((PLANES, YR, 128), F32)] * 3
        + [
            pltpu.SMEM((104 * 128,), F32),
            pltpu.SMEM((40 * 128,), I32),
            pltpu.SMEM((8, 128), I32),
            pltpu.VMEM((CX, CY, CZ), F32),
            pltpu.VMEM((PLANES, YR, 128), F32),
            pltpu.VMEM((CX, CY, CZ), F32),
            pltpu.VMEM((3, CX, CY, CZ), BF16),
            pltpu.VMEM((TILES, 8, 128), F32),
            pltpu.VMEM((2, TILES, 256), F32),
            pltpu.VMEM((8, 128), F32),
            pltpu.VMEM((8, 128), I32),
            pltpu.SMEM((8, 128), F32),
            pltpu.SMEM((8, 128), I32),
            pltpu.SemaphoreType.DMA((12,)),
        ],
        compiler_params=pltpu.CompilerParams(vmem_limit_bytes=62 * 2**20),
    )(lists, laplace, short.reshape(-1), spot.reshape(-1), many, coef, cond, forward_field[0, 0])
    both = pl.pallas_call(
        spread_kernel,
        name="spread_rows",
        out_shape=jax.ShapeDtypeStruct((2 * TILES, 16, CZ), F32),
        in_specs=[hbm()],
        out_specs=hbm(),
        scratch_shapes=[pltpu.SemaphoreType.DMA] * 3,
        compiler_params=pltpu.CompilerParams(collective_id=1, has_side_effects=True, vmem_limit_bytes=62 * 2**20),
    )(partial)
    return pl.pallas_call(
        add_kernel,
        name="add_frequencies",
        out_shape=jax.ShapeDtypeStruct((TILES, 1, 16, CZ), F32),
        in_specs=[vmem()],
        out_specs=vmem(),
    )(both)


def solution(mesh):
    placed = (
        P("freq", None, "tile"),
        P("tile", None),
        P("tile", None),
        P("tile"),
        P("tile", None, None, None),
        P("freq"),
        P("freq", "tile", None, None, None, None),
    )
    return jax.shard_map(
        local, mesh=mesh, in_specs=placed, out_specs=P(None, "tile", "freq", None), check_vma=False
    )
```

```python
import functools

import jax
import jax.numpy as jnp
from jax import lax
from jax.experimental import pallas as pl
from jax.experimental.pallas import tpu as pltpu
from jax.sharding import PartitionSpec as P

F32 = jnp.float32
BF16 = jnp.bfloat16
I32 = jnp.int32
MESH = pl.DeviceIdType.MESH

TX, TY, TZ = 4, 4, 4
TILES = 64
CX, CY, CZ = 64, 32, 128
NP_A, NP_B = 8, 10
RIM = 7

YR = 64
B0 = 81
RUN = 20
SEG = 28
RUNS = 4
ZB = CZ + RIM - SEG
PLANES = 112
KEEP = 64
OWN = 8


def iota(shape, dim):
    return lax.broadcasted_iota(I32, shape, dim)


def vmem():
    return pl.BlockSpec(memory_space=pltpu.VMEM)


def hbm():
    return pl.BlockSpec(memory_space=pl.ANY)


def place(t):
    return t // (TY * TZ), (t // TZ) % TY, t % TZ


def three(value):
    hi = value.astype(BF16)
    rest = value - hi.astype(F32)
    mid = rest.astype(BF16)
    low = (rest - mid.astype(F32)).astype(BF16)
    return hi, mid, low


def runs_of(read, s, rows, begin, end, shift):
    lane = iota((rows, 128), 1)
    total = jnp.zeros((rows, 128), F32)
    for g in range(RUNS):
        plane = read(1 + RUN * g + s)
        moved = pltpu.roll(plane, (SEG * g + shift) % 128, 1)
        total = jnp.where((lane >= SEG * g + begin) & (lane < SEG * g + end), moved, total)
    return total


def locate(code, tx, ty, tz):
    x = (code >> 16) - tx * CX + RIM
    y = ((code >> 9) & 127) - ty * CY + RIM
    z = (code & 511) - tz * CZ
    ok = (x >= 0) & (x < CX + 2 * RIM) & (y >= 0) & (y < CY + 2 * RIM) & (z >= -RIM) & (z < CZ + RIM)
    run = sum((x >= RUN * g).astype(I32) for g in range(1, RUNS))
    in_a = z < 128 - RIM
    plane = jnp.where(in_a, x + 1, x - RUN * run + B0)
    lane = jnp.where(in_a, z + RIM, SEG * run + z - ZB)
    return ok, jnp.where(ok, (plane * YR + y + 1) * 128 + lane, 0).astype(F32)


def find_all(list_ref, spots, t):
    code = jnp.concatenate([list_ref[:, 3, :], list_ref[:, 7, :]], axis=1).astype(I32)
    ok, spot = locate(code, *place(t))
    before = (iota((256, 256), 0) < iota((256, 256), 1)).astype(F32).astype(BF16)
    flag = ok.astype(F32)
    rank = jnp.dot(flag.astype(BF16), before, preferred_element_type=F32)
    spots[0] = spot
    spots[1] = jnp.where(ok, rank, -1.0)
    ones = jnp.ones((8, 256), BF16)
    return lax.dot_general(ones, flag.astype(BF16), (((1,), (1,)), ((), ())), preferred_element_type=F32).astype(I32)


def squeeze(list_ref, spots, b, first):
    place_k = iota((KEEP, 256), 0).astype(F32)
    values = jnp.concatenate([list_ref[b, pl.ds(0, 3), :], list_ref[b, pl.ds(4, 3), :]], axis=1)
    both = jnp.concatenate([values, spots[0, pl.ds(b, 1), :]], axis=0)
    pick = (place_k == spots[1, pl.ds(b, 1), :] - first).astype(F32).astype(BF16)
    parts = jnp.concatenate([part.astype(F32) for part in three(both)] + [jnp.zeros((4, 256), F32)], axis=0).astype(BF16)
    got = lax.dot_general(parts, pick, (((1,), (1,)), ((), ())), preferred_element_type=F32)
    return (got[0:4] + got[4:8]) + got[8:12]


def gather_kernel(res_hbm, cnt_hbm, tile_hbm, cell_hbm, lap_ref, cond_ref, list_ref, coef_hbm, short_ref, spot_ref, many_ref,
                  res_ref, cnt_ref, tile_ref, cell_ref, spots, raw, cext, pack, low, high, sends, recvs, zsend, zrecv, gsend, grecv, lsem, coef_ref):
    f, t = lax.axis_index("freq"), lax.axis_index("tile")
    me = f * TILES + t
    tx, ty, tz = place(t)
    barrier = pltpu.get_barrier_semaphore()

    def greet(i, c):
        pl.semaphore_signal(barrier, inc=1, device_id=me ^ i, device_id_type=pl.DeviceIdType.LOGICAL)
        return c

    lax.fori_loop(1, TILES, greet, 0)
    own = pltpu.make_async_copy(cond_ref, raw, lsem.at[0])
    own.start()
    loads = [pltpu.make_async_copy(a, b, lsem.at[n + 1])
             for n, (a, b) in enumerate(((res_hbm, res_ref), (cnt_hbm, cnt_ref), (tile_hbm, tile_ref), (cell_hbm, cell_ref)))]
    for copy in loads:
        copy.start()
    for copy in loads:
        copy.wait()

    counts = cnt_ref[...].astype(F32)
    upto = (iota((256, 256), 0) <= iota((256, 256), 1)).astype(F32)
    ends = jnp.dot(jnp.broadcast_to(counts, (8, 256)).astype(BF16), upto.astype(BF16), preferred_element_type=F32)[0:1]
    starts = ends - counts
    at = iota((1024, 256), 0).astype(F32)
    member = ((at >= starts) & (at < ends)).astype(F32).astype(BF16)
    sums = jnp.zeros((3, 256), F32)
    for part in three(res_ref[:, 0, :]):
        sums = sums + jnp.dot(part, member, preferred_element_type=F32)
    means = sums / counts
    owner, cell = tile_ref[...], cell_ref[...]
    gx = (owner >> 4) * CX + (cell >> 12)
    gy = ((owner >> 2) & 3) * CY + ((cell >> 7) & 31)
    gz = (owner & 3) * CZ + (cell & 127)
    code = ((gx * (TY * CY) + gy) * (TZ * CZ) + gz).astype(F32)
    both = jnp.concatenate([means, code], axis=0)
    list_ref[t] = jnp.concatenate([both[:, :128], both[:, 128:]], axis=0)

    spans = {1: (CX - 7, 1, 7), -1: (0, 72, 7), 0: (0, 8, CX)}
    rows = {1: (CY - 7, 1, 7), -1: (0, 40, 7), 0: (0, 8, CY)}
    ways = [(dx, dy) for dx in (-1, 0, 1) for dy in (-1, 0, 1) if (dx, dy) != (0, 0)]

    def inside(dx, dy):
        x, y = tx + dx, ty + dy
        return (x >= 0) & (x < TX) & (y >= 0) & (y < TY)

    def halo(n):
        dx, dy = ways[n]
        xs, xd, xn = spans[dx]
        ys, yd, yn = rows[dy]
        return pltpu.make_async_remote_copy(
            cext.at[pl.ds(OWN + xs, xn), pl.ds(8 + ys, yn)], cext.at[pl.ds(xd, xn), pl.ds(yd, yn)],
            sends.at[n], recvs.at[n], device_id=(f, t + dx * TY * TZ + dy * TZ), device_id_type=MESH)

    for dx, dy in ways:
        @pl.when(jnp.logical_not(inside(-dx, -dy)))
        def _(dx=dx, dy=dy):
            def wipe(i, c):
                cext[spans[dx][1] + i, pl.ds(rows[dy][1], rows[dy][2]), :] = jnp.zeros((rows[dy][2], 128), F32)
                return c

            lax.fori_loop(0, spans[dx][2], wipe, 0)
    lap = lap_ref[0]
    lane = iota((48, 128), 1)
    own.wait()

    def invert(k, c):
        done = [1.0 / (4.0 + lap * raw[4 * k + j]) for j in range(4)]
        for j in range(4):
            cext[OWN + 4 * k + j, pl.ds(8, CY), :] = done[j]
        return c

    lax.fori_loop(0, CX // 4, invert, 0)
    pl.semaphore_wait(barrier, TILES - 1)

    def share(i, c):
        pltpu.make_async_remote_copy(list_ref.at[t], list_ref.at[t], gsend, grecv,
                                     device_id=me ^ i, device_id_type=pl.DeviceIdType.LOGICAL).start()
        return c

    lax.fori_loop(1, TILES, share, 0)

    for n, (dx, dy) in enumerate(ways):
        @pl.when(inside(dx, dy))
        def _(n=n):
            halo(n).start()

    def lay(planes, begin, count):
        part = pl.ds(begin, count)
        done = [jnp.where(lane[:count] < RIM, 0.0, pltpu.roll(cext[i, part, :], RIM, 1)) for i in planes]
        for i, value in zip(planes, done):
            coef_ref[i, part, :] = value

    def lay_own(k, c):
        lay([OWN + 4 * k + j for j in range(4)], 8, CY)
        return c

    lax.fori_loop(0, CX // 4, lay_own, 0)
    everyone = list_ref.at[pl.ds(0, TILES - 1)]
    pltpu.make_async_copy(everyone, everyone, grecv).wait()
    many_ref[:, pl.ds(0, TILES)] = find_all(list_ref, spots, t)

    def compact(k, c):
        for i in range(2):
            pair = jnp.concatenate([squeeze(list_ref, spots, 4 * k + 2 * i + j, 0.0) for j in range(2)], axis=1)
            short_ref[pl.ds(3 * (2 * k + i), 3), :] = pair[0:3]
            spot_ref[pl.ds(2 * k + i, 1), :] = pair[3:4].astype(I32)
        return c

    lax.fori_loop(0, TILES // 4, compact, 0)
    for n, (dx, dy) in enumerate(ways):
        @pl.when(inside(-dx, -dy))
        def _(n=n):
            halo(n).wait_recv()

    def read(i):
        return cext[jnp.minimum(i, 79)]

    def fill(k, c):
        done = []
        for j in range(2):
            total = jnp.zeros((48, 128), F32)
            for h in range(8):
                plane = read(1 + 10 * h + 2 * k + j)
                for begin, shift in ((16 * h, 16 * h - 121), (16 * h + 8, 16 * h + 8)):
                    moved = pltpu.roll(plane, shift % 128, 1)
                    total = jnp.where((lane >= begin) & (lane < begin + 7), moved, total)
            done.append(total)
        for j in range(2):
            pack[2 * k + j] = done[j]
        return c

    lax.fori_loop(0, 5, fill, 0)

    def rim(up):
        return pltpu.make_async_remote_copy(
            pack, low if up else high, zsend.at[up], zrecv.at[up],
            device_id=(f, t + (1 if up else -1)), device_id_type=MESH)

    @pl.when(tz < TZ - 1)
    def _():
        rim(1).start()

    @pl.when(tz > 0)
    def _():
        rim(0).start()

    def lay_rows(k, c):
        planes = [OWN + 4 * k + j for j in range(4)]
        lay(planes, 0, 8)
        lay(planes, 40, 8)
        return c

    lax.fori_loop(0, CX // 4, lay_rows, 0)

    def lay_planes(k, c):
        lay([1 + k, 72 + k], 0, 48)
        return c

    lax.fori_loop(0, RIM, lay_planes, 0)

    def fill_b(k, c):
        done = [runs_of(read, 2 * k + j, 48, 0, SEG - RIM, 128 - ZB) for j in range(2)]
        for j in range(2):
            coef_ref[B0 + 2 * k + j, pl.ds(0, 48), :] = done[j]
        return c

    lax.fori_loop(0, RUN // 2, fill_b, 0)

    @pl.when(tz > 0)
    def _():
        rim(1).wait_recv()

        def patch(k, c):
            done = []
            for h in range(8):
                old = coef_ref[1 + 10 * h + k, pl.ds(0, 48), :]
                done.append(jnp.where(lane < RIM, pltpu.roll(low[k], (128 - 16 * h) % 128, 1), old))
            for h in range(8):
                coef_ref[1 + 10 * h + k, pl.ds(0, 48), :] = done[h]
            return c

        lax.fori_loop(0, 10, patch, 0)

    leaving = [pltpu.make_async_copy(coef_ref.at[pl.ds(b, n)], coef_hbm.at[pl.ds(b, n)], lsem.at[5 + k])
               for k, (b, n) in enumerate(((0, 80), (80, 24)))]
    leaving[0].start()

    @pl.when(tz < TZ - 1)
    def _():
        rim(0).wait_recv()

        def patch(k, c):
            done = []
            for j in range(2):
                s = 2 * k + j
                value = coef_ref[B0 + s, pl.ds(0, 48), :]
                for g in range(RUNS):
                    i = RUN * g + s
                    turn = (SEG * g + SEG - RIM - 8 - 16 * (i // 10) + 256) % 128
                    inner = (lane >= SEG * g + SEG - RIM) & (lane < SEG * g + SEG)
                    value = jnp.where(inner, pltpu.roll(high[i % 10], turn, 1), value)
                done.append(value)
            for j in range(2):
                coef_ref[B0 + 2 * k + j, pl.ds(0, 48), :] = done[j]
            return c

        lax.fori_loop(0, RUN // 2, patch, 0)

    leaving[1].start()

    for n, (dx, dy) in enumerate(ways):
        @pl.when(inside(dx, dy))
        def _(n=n):
            halo(n).wait_send()

    @pl.when(tz < TZ - 1)
    def _():
        rim(1).wait_send()

    @pl.when(tz > 0)
    def _():
        rim(0).wait_send()

    pltpu.make_async_copy(everyone, everyone, gsend).wait()
    for copy in leaving:
        copy.wait()


def stencil(src, dst, base, coef, hx_ref, hy_ref, hz_ref, lo, hi, y0, nk, nh, scale, step):
    rk, rh, h0 = 8 * nk, 8 * nh, y0 - 1
    hr, hy_rows, kr, kl = pl.ds(h0, rh), pl.ds(y0, rh), pl.ds(y0, rk), pl.ds(h0, rk)

    def swirl(x):
        vx, vy, vz = src[0, x, hr, :], src[1, x, hr, :], src[2, x, hr, :]
        vyz, vxz = pltpu.roll(vy, 127, 1), pltpu.roll(vx, 127, 1)
        hx_ref[x, hr, :] = (src[2, x, hy_rows, :] - vz) - (vyz - vy)
        hy_ref[x, hr, :] = (vxz - vx) - (src[2, x + 1, hr, :] - vz)
        hz_ref[x, hr, :] = (src[1, x + 1, hr, :] - vy) - (src[0, x, hy_rows, :] - vx)

    def relax(x):
        hx, hy, hz = hx_ref[x, kr, :], hy_ref[x, kr, :], hz_ref[x, kr, :]
        kx = (hz - hz_ref[x, kl, :]) - (hy - pltpu.roll(hy, 1, 1))
        ky = (hx - pltpu.roll(hx, 1, 1)) - (hz - hz_ref[x - 1, kr, :])
        kz = (hy - hy_ref[x - 1, kr, :]) - (hx - hx_ref[x, kl, :])
        c = coef[x, kr, :] if scale == 1.0 else scale * coef[x, kr, :]
        keep = (scale if base is not src else 1.0 + scale) + 4.0 * c
        for i, k in enumerate((kx, ky, kz)):
            new = keep * src[i, x, kr, :] - c * k
            if base is not None and base is not src:
                new = base[i, x, kr, :] + new
            dst[i, x, kr, :] = new

    for i in range(-1, step):
        swirl(lo + i)

    def body(k, c):
        x = jnp.minimum(lo + step * k, hi - step)
        for i in range(step):
            relax(x + i)
        for i in range(step):
            swirl(x + step + i)
        return c

    lax.fori_loop(0, (hi - lo + step - 1) // step, body, 0)


def relax_kernel(list_hbm, lap_ref, short_hbm, spot_hbm, many_hbm, coef_hbm, cond_hbm, field_hbm, out_ref,
                 u, p, q, hx_ref, hy_ref, hz_ref, short_s, spot_s, many_s, rows, coef, cond, field, list_ref, spots, more, more_i, more_s, more_is, sems):
    t = lax.axis_index("tile")
    loads = [pltpu.make_async_copy(a, b, sems.at[n])
             for n, (a, b) in enumerate(((coef_hbm.at[pl.ds(0, 104)], coef.at[pl.ds(0, 104)]), (cond_hbm, cond), (field_hbm, field)))]
    lists = [pltpu.make_async_copy(a, b, sems.at[n + 5])
             for n, (a, b) in enumerate(((many_hbm, many_s), (spot_hbm, spot_s), (short_hbm, short_s)))]
    for copy in lists + loads:
        copy.start()

    flat = u.reshape(3, PLANES * YR, 128)

    def clear(i, c):
        for k in range(3):
            u[k, i] = jnp.zeros((YR, 128), F32)
        return c

    lax.fori_loop(0, PLANES, clear, 0)
    lane_id = iota((1, 128), 1)
    for copy in lists:
        copy.wait()

    def drop(k, most):
        for i in range(2):
            count = many_s[0, 2 * k + i]

            def read(j, i=i):
                at, where = 384 * k + KEEP * i + 4 * j, 128 * k + KEEP * i + 4 * j
                return (tuple(spot_s[where + m] for m in range(4)),
                        tuple(short_s[at + 128 * n + m] for m in range(4) for n in range(3)))

            def four(j, held):
                coming = read(j + 1)
                for m in range(4):
                    here = lane_id == (held[0][m] & 127)
                    row = pl.ds(held[0][m] >> 7, 1)
                    for n in range(3):
                        flat[n, row, :] += jnp.where(here, held[1][3 * m + n], 0.0)
                return coming

            lax.fori_loop(0, (jnp.minimum(count, KEEP) + 3) // 4, four, read(0))
            most = jnp.maximum(most, count)
        return most

    most = lax.fori_loop(0, TILES // 2, drop, 0)

    @pl.when(most > KEEP)
    def _():
        copy = pltpu.make_async_copy(list_hbm, list_ref, sems.at[3])
        copy.start()
        copy.wait()
        find_all(list_ref, spots, t)

        def rest(b, c):
            count = many_s[0, b]

            def chunk(j, c2):
                got = squeeze(list_ref, spots, b, (KEEP * j).astype(F32))
                more[pl.ds(0, 3), pl.ds(0, KEEP)] = got[0:3]
                spot = got[3:4].astype(I32)
                more_i[pl.ds(0, 1), pl.ds(0, KEEP)] = spot
                copies = [pltpu.make_async_copy(more, more_s, sems.at[3]), pltpu.make_async_copy(more_i, more_is, sems.at[4])]
                for copy in copies:
                    copy.start()
                for copy in copies:
                    copy.wait()

                def one(k, c3):
                    spot = more_is[0, k]
                    here = lane_id == (spot & 127)
                    for n in range(3):
                        flat[n, pl.ds(spot >> 7, 1), :] += jnp.where(here, more_s[n, k], 0.0)
                    return c3

                return lax.fori_loop(0, jnp.minimum(count - KEEP * j, KEEP), one, c2)

            return lax.fori_loop(1, (count + KEEP - 1) // KEEP, chunk, c)

        lax.fori_loop(0, TILES, rest, 0)

    loads[0].wait()

    def scale_b(k, c):
        done = []
        for j in range(2):
            s = 2 * k + j
            for i in range(3):
                value = runs_of(lambda k: u[i, jnp.minimum(k, 79), pl.ds(0, 48), :], s, 48, 0, 14, 128 - ZB - RIM)
                done.append((i, B0 + s, 0.5 * coef[B0 + s, pl.ds(0, 48), :] * (value + u[i, B0 + s, pl.ds(0, 48), :])))
        for i, s, value in done:
            u[i, s, pl.ds(0, 48), :] = value
        return c

    lax.fori_loop(0, RUN // 2, scale_b, 0)

    def scale_a(k, c):
        for i in range(3):
            u[i, k] = 0.5 * coef[k] * u[i, k]
        return c

    lax.fori_loop(0, 80, scale_a, 0)

    plan = [(u, p, u, 0.5), (p, q, None, 1.0), (q, u, p, 0.25), (u, p, None, 1.0), (p, q, None, 1.0),
            (q, p, None, 1.0), (p, q, u, 0.0625)]
    for n, (src, dst, base, scale) in enumerate(plan):
        e = RIM - 1 - n
        nk, nh = -(-(CY + 2 * e) // 8), -(-(CY + 1 + 2 * e) // 8)
        for i in range(3):
            src[i, B0 - 1] = pltpu.roll(src[i, B0 + RUN - 1], SEG, 1)
            src[i, B0 + RUN] = pltpu.roll(src[i, B0], 128 - SEG, 1)
        stencil(src, dst, base, coef, hx_ref, hy_ref, hz_ref, B0, B0 + RUN, 8 - e, nk, nh, scale, NP_B)
        stencil(src, dst, base, coef, hx_ref, hy_ref, hz_ref, OWN - e, OWN + CX + e, 8 - e, nk, nh, scale, NP_A)

    loads[1].wait()
    loads[2].wait()
    lane = iota((CY, 128), 1)
    own_y = pl.ds(8, CY)
    leaving = []
    lap = lap_ref[0]
    for g in range(RUNS):
        begin, end = max(0, RUN * g - RIM), min(CX, RUN * (g + 1) - RIM)

        def combine(k, c, g=g, begin=begin, end=end):
            for j in range(4):
                x = jnp.minimum(begin + 4 * k + j, end - 1)
                total = jnp.zeros((CY, 128), F32)
                for i in range(3):
                    rims = q[i, B0 + x + RIM - RUN * g, own_y, :]
                    value = jnp.where(lane >= CZ - 2 * RIM, pltpu.roll(rims, (ZB - SEG * g) % 128, 1),
                                      pltpu.roll(q[i, OWN + x, own_y, :], 128 - RIM, 1))
                    total = total + field[i, x].astype(F32) * value
                rows[x] = -lap * cond[x] * total
            return c

        lax.fori_loop(0, (end - begin + 3) // 4, combine, 0)
        made = pltpu.make_async_copy(rows.at[pl.ds(begin, end - begin)], out_ref.at[pl.ds(begin, end - begin)], sems.at[8 + g])
        made.start()
        leaving.append(made)
    for made in leaving:
        made.wait()


def spread_kernel(part_ref, out_ref, send, recv, lsem):
    f, t = lax.axis_index("freq"), lax.axis_index("tile")
    me = f * TILES + t
    barrier = pltpu.get_barrier_semaphore()

    def greet(i, c):
        pl.semaphore_signal(barrier, inc=1, device_id=me ^ (2 * TILES - i), device_id_type=pl.DeviceIdType.LOGICAL)
        return c

    lax.fori_loop(1, 2 * TILES, greet, 0)
    mine = pltpu.make_async_copy(part_ref.at[t, pl.ds(f * 16, 16)], out_ref.at[me], lsem)
    mine.start()
    pl.semaphore_wait(barrier, 2 * TILES - 1)

    def share(i, c):
        d = me ^ (2 * TILES - i)
        pltpu.make_async_remote_copy(part_ref.at[d & (TILES - 1), pl.ds((d >> 6) * 16, 16)], out_ref.at[me], send, recv,
                                     device_id=d, device_id_type=pl.DeviceIdType.LOGICAL).start()
        return c

    lax.fori_loop(1, 2 * TILES, share, 0)
    mine.wait()
    others = out_ref.at[pl.ds(0, 2 * TILES - 1)]
    for sem in (send, recv):
        pltpu.make_async_copy(others, others, sem).wait()


def add_kernel(both_hbm, out_ref, both_ref, sem):
    load = pltpu.make_async_copy(both_hbm, both_ref, sem)
    load.start()
    load.wait()

    def body(k, c):
        done = [both_ref[8 * k + j] + both_ref[TILES + 8 * k + j] for j in range(8)]
        for j in range(8):
            out_ref[8 * k + j, 0] = done[j]
        return c

    lax.fori_loop(0, TILES // 8, body, 0)


def local(residual, row_counts, recv_owner, recv_cell, conductivity, laplace, forward_field):
    smem = pl.BlockSpec(memory_space=pltpu.SMEM)
    cond = conductivity[0]
    lists, coef, short, spot, many = pl.pallas_call(
        gather_kernel,
        name="gather_lists",
        out_shape=(jax.ShapeDtypeStruct((TILES, 8, 128), F32), jax.ShapeDtypeStruct((PLANES, YR, 128), F32),
                   jax.ShapeDtypeStruct((104, 128), F32), jax.ShapeDtypeStruct((40, 128), I32),
                   jax.ShapeDtypeStruct((8, 128), I32)),
        in_specs=[hbm(), hbm(), hbm(), hbm(), smem, hbm()],
        out_specs=(vmem(), hbm(), vmem(), vmem(), vmem()),
        scratch_shapes=[
            pltpu.VMEM((3, 1, 1024), F32),
            pltpu.VMEM((1, 256), I32),
            pltpu.VMEM((1, 256), I32),
            pltpu.VMEM((1, 256), I32),
            pltpu.VMEM((2, TILES, 256), F32),
            pltpu.VMEM((CX, CY, CZ), F32),
            pltpu.VMEM((82, 48, 128), F32),
            pltpu.VMEM((10, 48, 128), F32),
            pltpu.VMEM((10, 48, 128), F32),
            pltpu.VMEM((10, 48, 128), F32),
            pltpu.SemaphoreType.DMA((8,)),
            pltpu.SemaphoreType.DMA((8,)),
            pltpu.SemaphoreType.DMA((2,)),
            pltpu.SemaphoreType.DMA((2,)),
            pltpu.SemaphoreType.DMA,
            pltpu.SemaphoreType.DMA,
            pltpu.SemaphoreType.DMA((7,)),
            pltpu.VMEM((PLANES, YR, 128), F32),
        ],
        compiler_params=pltpu.CompilerParams(collective_id=0, has_side_effects=True, vmem_limit_bytes=62 * 2**20),
    )(residual.transpose(1, 0, 2), row_counts, recv_owner.reshape(1, -1), recv_cell.reshape(1, -1), laplace, cond)
    partial = pl.pallas_call(
        relax_kernel,
        name="relax_tile",
        out_shape=jax.ShapeDtypeStruct((CX, CY, CZ), F32),
        in_specs=[hbm(), smem, hbm(), hbm(), hbm(), hbm(), hbm(), hbm()],
        out_specs=hbm(),
        scratch_shapes=[pltpu.VMEM((3, PLANES, YR, 128), F32)] * 3
        + [pltpu.VMEM((PLANES, YR, 128), F32)] * 3
        + [
            pltpu.SMEM((104 * 128,), F32),
            pltpu.SMEM((40 * 128,), I32),
            pltpu.SMEM((8, 128), I32),
            pltpu.VMEM((CX, CY, CZ), F32),
            pltpu.VMEM((PLANES, YR, 128), F32),
            pltpu.VMEM((CX, CY, CZ), F32),
            pltpu.VMEM((3, CX, CY, CZ), BF16),
            pltpu.VMEM((TILES, 8, 128), F32),
            pltpu.VMEM((2, TILES, 256), F32),
            pltpu.VMEM((8, 128), F32),
            pltpu.VMEM((8, 128), I32),
            pltpu.SMEM((8, 128), F32),
            pltpu.SMEM((8, 128), I32),
            pltpu.SemaphoreType.DMA((12,)),
        ],
        compiler_params=pltpu.CompilerParams(vmem_limit_bytes=62 * 2**20),
    )(lists, laplace, short.reshape(-1), spot.reshape(-1), many, coef, cond, forward_field[0, 0])
    both = pl.pallas_call(
        spread_kernel,
        name="spread_rows",
        out_shape=jax.ShapeDtypeStruct((2 * TILES, 16, CZ), F32),
        in_specs=[hbm()],
        out_specs=hbm(),
        scratch_shapes=[pltpu.SemaphoreType.DMA] * 3,
        compiler_params=pltpu.CompilerParams(collective_id=1, has_side_effects=True, vmem_limit_bytes=4 * 2**20),
    )(partial)
    return pl.pallas_call(
        add_kernel,
        name="add_frequencies",
        out_shape=jax.ShapeDtypeStruct((TILES, 1, 16, CZ), F32),
        in_specs=[hbm()],
        out_specs=vmem(),
        scratch_shapes=[pltpu.VMEM((2 * TILES, 16, CZ), F32), pltpu.SemaphoreType.DMA],
        compiler_params=pltpu.CompilerParams(vmem_limit_bytes=4 * 2**20),
    )(both)


def solution(mesh):
    placed = (
        P("freq", None, "tile"),
        P("tile", None),
        P("tile", None),
        P("tile"),
        P("tile", None, None, None),
        P("freq"),
        P("freq", "tile", None, None, None, None),
    )
    return jax.shard_map(
        local, mesh=mesh, in_specs=placed, out_specs=P(None, "tile", "freq", None), check_vma=False
    )
```

```python
import functools

import jax
import jax.numpy as jnp
from jax import lax
from jax.experimental import pallas as pl
from jax.experimental.pallas import tpu as pltpu
from jax.sharding import PartitionSpec as P

F32 = jnp.float32
BF16 = jnp.bfloat16
I32 = jnp.int32
MESH = pl.DeviceIdType.MESH

TX, TY, TZ = 4, 4, 4
TILES = 64
CX, CY, CZ = 64, 32, 128
NP_A, NP_B = 8, 10
RIM = 7

YR = 64
B0 = 81
RUN = 20
SEG = 28
RUNS = 4
ZB = CZ + RIM - SEG
PLANES = 112
KEEP = 64
OWN = 8


def iota(shape, dim):
    return lax.broadcasted_iota(I32, shape, dim)


def vmem():
    return pl.BlockSpec(memory_space=pltpu.VMEM)


def hbm():
    return pl.BlockSpec(memory_space=pl.ANY)


def place(t):
    return t // (TY * TZ), (t // TZ) % TY, t % TZ


def three(value):
    hi = value.astype(BF16)
    rest = value - hi.astype(F32)
    mid = rest.astype(BF16)
    low = (rest - mid.astype(F32)).astype(BF16)
    return hi, mid, low


def runs_of(read, s, rows, begin, end, shift):
    lane = iota((rows, 128), 1)
    total = jnp.zeros((rows, 128), F32)
    for g in range(RUNS):
        plane = read(1 + RUN * g + s)
        moved = pltpu.roll(plane, (SEG * g + shift) % 128, 1)
        total = jnp.where((lane >= SEG * g + begin) & (lane < SEG * g + end), moved, total)
    return total


def locate(code, tx, ty, tz):
    x = (code >> 16) - tx * CX + RIM
    y = ((code >> 9) & 127) - ty * CY + RIM
    z = (code & 511) - tz * CZ
    ok = (x >= 0) & (x < CX + 2 * RIM) & (y >= 0) & (y < CY + 2 * RIM) & (z >= -RIM) & (z < CZ + RIM)
    run = sum((x >= RUN * g).astype(I32) for g in range(1, RUNS))
    in_a = z < 128 - RIM
    plane = jnp.where(in_a, x + 1, x - RUN * run + B0)
    lane = jnp.where(in_a, z + RIM, SEG * run + z - ZB)
    return ok, jnp.where(ok, (plane * YR + y + 1) * 128 + lane, 0).astype(F32)


def find_all(list_ref, spots, t):
    code = jnp.concatenate([list_ref[:, 3, :], list_ref[:, 7, :]], axis=1).astype(I32)
    ok, spot = locate(code, *place(t))
    before = (iota((256, 256), 0) < iota((256, 256), 1)).astype(F32).astype(BF16)
    flag = ok.astype(F32)
    rank = jnp.dot(flag.astype(BF16), before, preferred_element_type=F32)
    spots[0] = spot
    spots[1] = jnp.where(ok, rank, -1.0)
    ones = jnp.ones((8, 256), BF16)
    return lax.dot_general(ones, flag.astype(BF16), (((1,), (1,)), ((), ())), preferred_element_type=F32).astype(I32)


def squeeze(list_ref, spots, b, first):
    place_k = iota((KEEP, 256), 0).astype(F32)
    values = jnp.concatenate([list_ref[b, pl.ds(0, 3), :], list_ref[b, pl.ds(4, 3), :]], axis=1)
    both = jnp.concatenate([values, spots[0, pl.ds(b, 1), :]], axis=0)
    pick = (place_k == spots[1, pl.ds(b, 1), :] - first).astype(F32).astype(BF16)
    parts = jnp.concatenate([part.astype(F32) for part in three(both)] + [jnp.zeros((4, 256), F32)], axis=0).astype(BF16)
    got = lax.dot_general(parts, pick, (((1,), (1,)), ((), ())), preferred_element_type=F32)
    return (got[0:4] + got[4:8]) + got[8:12]


def gather_kernel(res_hbm, cnt_hbm, tile_hbm, cell_hbm, lap_ref, cond_ref, list_ref, coef_hbm, short_ref, spot_ref, many_ref,
                  res_ref, cnt_ref, tile_ref, cell_ref, spots, raw, cext, pack, low, high, sends, recvs, zsend, zrecv, gsend, grecv, lsem, coef_ref):
    f, t = lax.axis_index("freq"), lax.axis_index("tile")
    me = f * TILES + t
    tx, ty, tz = place(t)
    barrier = pltpu.get_barrier_semaphore()

    def greet(i, c):
        pl.semaphore_signal(barrier, inc=1, device_id=me ^ i, device_id_type=pl.DeviceIdType.LOGICAL)
        return c

    lax.fori_loop(1, TILES, greet, 0)
    own = pltpu.make_async_copy(cond_ref, raw, lsem.at[0])
    own.start()
    loads = [pltpu.make_async_copy(a, b, lsem.at[n + 1])
             for n, (a, b) in enumerate(((res_hbm, res_ref), (cnt_hbm, cnt_ref), (tile_hbm, tile_ref), (cell_hbm, cell_ref)))]
    for copy in loads:
        copy.start()
    for copy in loads:
        copy.wait()

    counts = cnt_ref[...].astype(F32)
    upto = (iota((256, 256), 0) <= iota((256, 256), 1)).astype(F32)
    ends = jnp.dot(jnp.broadcast_to(counts, (8, 256)).astype(BF16), upto.astype(BF16), preferred_element_type=F32)[0:1]
    starts = ends - counts
    at = iota((1024, 256), 0).astype(F32)
    member = ((at >= starts) & (at < ends)).astype(F32).astype(BF16)
    sums = jnp.zeros((3, 256), F32)
    for part in three(res_ref[:, 0, :]):
        sums = sums + jnp.dot(part, member, preferred_element_type=F32)
    means = sums / counts
    owner, cell = tile_ref[...], cell_ref[...]
    gx = (owner >> 4) * CX + (cell >> 12)
    gy = ((owner >> 2) & 3) * CY + ((cell >> 7) & 31)
    gz = (owner & 3) * CZ + (cell & 127)
    code = ((gx * (TY * CY) + gy) * (TZ * CZ) + gz).astype(F32)
    both = jnp.concatenate([means, code], axis=0)
    list_ref[t] = jnp.concatenate([both[:, :128], both[:, 128:]], axis=0)

    spans = {1: (CX - 7, 1, 7), -1: (0, 72, 7), 0: (0, 8, CX)}
    rows = {1: (CY - 7, 1, 7), -1: (0, 40, 7), 0: (0, 8, CY)}
    ways = [(dx, dy) for dx in (-1, 0, 1) for dy in (-1, 0, 1) if (dx, dy) != (0, 0)]

    def inside(dx, dy):
        x, y = tx + dx, ty + dy
        return (x >= 0) & (x < TX) & (y >= 0) & (y < TY)

    def halo(n):
        dx, dy = ways[n]
        xs, xd, xn = spans[dx]
        ys, yd, yn = rows[dy]
        return pltpu.make_async_remote_copy(
            cext.at[pl.ds(OWN + xs, xn), pl.ds(8 + ys, yn)], cext.at[pl.ds(xd, xn), pl.ds(yd, yn)],
            sends.at[n], recvs.at[n], device_id=(f, t + dx * TY * TZ + dy * TZ), device_id_type=MESH)

    for dx, dy in ways:
        @pl.when(jnp.logical_not(inside(-dx, -dy)))
        def _(dx=dx, dy=dy):
            def wipe(i, c):
                cext[spans[dx][1] + i, pl.ds(rows[dy][1], rows[dy][2]), :] = jnp.zeros((rows[dy][2], 128), F32)
                return c

            lax.fori_loop(0, spans[dx][2], wipe, 0)
    lap = lap_ref[0]
    lane = iota((48, 128), 1)
    own.wait()

    def invert(k, c):
        done = [1.0 / (4.0 + lap * raw[4 * k + j]) for j in range(4)]
        for j in range(4):
            cext[OWN + 4 * k + j, pl.ds(8, CY), :] = done[j]
        return c

    lax.fori_loop(0, CX // 4, invert, 0)
    pl.semaphore_wait(barrier, TILES - 1)

    def share(i, c):
        pltpu.make_async_remote_copy(list_ref.at[t], list_ref.at[t], gsend, grecv,
                                     device_id=me ^ i, device_id_type=pl.DeviceIdType.LOGICAL).start()
        return c

    lax.fori_loop(1, TILES, share, 0)

    for n, (dx, dy) in enumerate(ways):
        @pl.when(inside(dx, dy))
        def _(n=n):
            halo(n).start()

    def lay(planes, begin, count):
        part = pl.ds(begin, count)
        done = [jnp.where(lane[:count] < RIM, 0.0, pltpu.roll(cext[i, part, :], RIM, 1)) for i in planes]
        for i, value in zip(planes, done):
            coef_ref[i, part, :] = value

    def lay_own(k, c):
        lay([OWN + 4 * k + j for j in range(4)], 8, CY)
        return c

    lax.fori_loop(0, CX // 4, lay_own, 0)
    everyone = list_ref.at[pl.ds(0, TILES - 1)]
    pltpu.make_async_copy(everyone, everyone, grecv).wait()
    many_ref[:, pl.ds(0, TILES)] = find_all(list_ref, spots, t)

    def compact(k, c):
        for i in range(2):
            pair = jnp.concatenate([squeeze(list_ref, spots, 4 * k + 2 * i + j, 0.0) for j in range(2)], axis=1)
            short_ref[pl.ds(3 * (2 * k + i), 3), :] = pair[0:3]
            spot_ref[pl.ds(2 * k + i, 1), :] = pair[3:4].astype(I32)
        return c

    lax.fori_loop(0, TILES // 4, compact, 0)
    for n, (dx, dy) in enumerate(ways):
        @pl.when(inside(-dx, -dy))
        def _(n=n):
            halo(n).wait_recv()

    def read(i):
        return cext[jnp.minimum(i, 79)]

    def fill(k, c):
        done = []
        for j in range(2):
            total = jnp.zeros((48, 128), F32)
            for h in range(8):
                plane = read(1 + 10 * h + 2 * k + j)
                for begin, shift in ((16 * h, 16 * h - 121), (16 * h + 8, 16 * h + 8)):
                    moved = pltpu.roll(plane, shift % 128, 1)
                    total = jnp.where((lane >= begin) & (lane < begin + 7), moved, total)
            done.append(total)
        for j in range(2):
            pack[2 * k + j] = done[j]
        return c

    lax.fori_loop(0, 5, fill, 0)

    def rim(up):
        return pltpu.make_async_remote_copy(
            pack, low if up else high, zsend.at[up], zrecv.at[up],
            device_id=(f, t + (1 if up else -1)), device_id_type=MESH)

    @pl.when(tz < TZ - 1)
    def _():
        rim(1).start()

    @pl.when(tz > 0)
    def _():
        rim(0).start()

    def lay_rows(k, c):
        planes = [OWN + 4 * k + j for j in range(4)]
        lay(planes, 0, 8)
        lay(planes, 40, 8)
        return c

    lax.fori_loop(0, CX // 4, lay_rows, 0)

    def lay_planes(k, c):
        lay([1 + k, 72 + k], 0, 48)
        return c

    lax.fori_loop(0, RIM, lay_planes, 0)

    def fill_b(k, c):
        done = [runs_of(read, 2 * k + j, 48, 0, SEG - RIM, 128 - ZB) for j in range(2)]
        for j in range(2):
            coef_ref[B0 + 2 * k + j, pl.ds(0, 48), :] = done[j]
        return c

    lax.fori_loop(0, RUN // 2, fill_b, 0)

    @pl.when(tz > 0)
    def _():
        rim(1).wait_recv()

        def patch(k, c):
            done = []
            for h in range(8):
                old = coef_ref[1 + 10 * h + k, pl.ds(0, 48), :]
                done.append(jnp.where(lane < RIM, pltpu.roll(low[k], (128 - 16 * h) % 128, 1), old))
            for h in range(8):
                coef_ref[1 + 10 * h + k, pl.ds(0, 48), :] = done[h]
            return c

        lax.fori_loop(0, 10, patch, 0)

    leaving = [pltpu.make_async_copy(coef_ref.at[pl.ds(b, n)], coef_hbm.at[pl.ds(b, n)], lsem.at[5 + k])
               for k, (b, n) in enumerate(((0, 80), (80, 24)))]
    leaving[0].start()

    @pl.when(tz < TZ - 1)
    def _():
        rim(0).wait_recv()

        def patch(k, c):
            done = []
            for j in range(2):
                s = 2 * k + j
                value = coef_ref[B0 + s, pl.ds(0, 48), :]
                for g in range(RUNS):
                    i = RUN * g + s
                    turn = (SEG * g + SEG - RIM - 8 - 16 * (i // 10) + 256) % 128
                    inner = (lane >= SEG * g + SEG - RIM) & (lane < SEG * g + SEG)
                    value = jnp.where(inner, pltpu.roll(high[i % 10], turn, 1), value)
                done.append(value)
            for j in range(2):
                coef_ref[B0 + 2 * k + j, pl.ds(0, 48), :] = done[j]
            return c

        lax.fori_loop(0, RUN // 2, patch, 0)

    leaving[1].start()

    for n, (dx, dy) in enumerate(ways):
        @pl.when(inside(dx, dy))
        def _(n=n):
            halo(n).wait_send()

    @pl.when(tz < TZ - 1)
    def _():
        rim(1).wait_send()

    @pl.when(tz > 0)
    def _():
        rim(0).wait_send()

    pltpu.make_async_copy(everyone, everyone, gsend).wait()
    for copy in leaving:
        copy.wait()


def stencil(src, dst, base, coef, hx_ref, hy_ref, hz_ref, lo, hi, y0, nk, nh, scale, step):
    rk, rh, h0 = 8 * nk, 8 * nh, y0 - 1
    hr, hy_rows, kr, kl = pl.ds(h0, rh), pl.ds(y0, rh), pl.ds(y0, rk), pl.ds(h0, rk)

    def swirl(x):
        vx, vy, vz = src[0, x, hr, :], src[1, x, hr, :], src[2, x, hr, :]
        vyz, vxz = pltpu.roll(vy, 127, 1), pltpu.roll(vx, 127, 1)
        hx_ref[x, hr, :] = (src[2, x, hy_rows, :] - vz) - (vyz - vy)
        hy_ref[x, hr, :] = (vxz - vx) - (src[2, x + 1, hr, :] - vz)
        hz_ref[x, hr, :] = (src[1, x + 1, hr, :] - vy) - (src[0, x, hy_rows, :] - vx)

    def relax(x):
        hx, hy, hz = hx_ref[x, kr, :], hy_ref[x, kr, :], hz_ref[x, kr, :]
        kx = (hz - hz_ref[x, kl, :]) - (hy - pltpu.roll(hy, 1, 1))
        ky = (hx - pltpu.roll(hx, 1, 1)) - (hz - hz_ref[x - 1, kr, :])
        kz = (hy - hy_ref[x - 1, kr, :]) - (hx - hx_ref[x, kl, :])
        c = coef[x, kr, :] if scale == 1.0 else scale * coef[x, kr, :]
        keep = (scale if base is not src else 1.0 + scale) + 4.0 * c
        for i, k in enumerate((kx, ky, kz)):
            new = keep * src[i, x, kr, :] - c * k
            if base is not None and base is not src:
                new = base[i, x, kr, :] + new
            dst[i, x, kr, :] = new

    for i in range(-1, step):
        swirl(lo + i)

    def body(k, c):
        x = jnp.minimum(lo + step * k, hi - step)
        for i in range(step):
            relax(x + i)
        for i in range(step):
            swirl(x + step + i)
        return c

    lax.fori_loop(0, (hi - lo + step - 1) // step, body, 0)


def relax_kernel(list_hbm, lap_ref, short_hbm, spot_hbm, many_hbm, coef_hbm, cond_hbm, field_hbm, out_ref,
                 u, p, q, hx_ref, hy_ref, hz_ref, short_s, spot_s, many_s, rows, coef, cond, field, list_ref, spots, more, more_i, more_s, more_is, sems):
    t = lax.axis_index("tile")
    loads = [pltpu.make_async_copy(a, b, sems.at[n])
             for n, (a, b) in enumerate(((coef_hbm.at[pl.ds(0, 104)], coef.at[pl.ds(0, 104)]), (cond_hbm, cond), (field_hbm, field)))]
    lists = [pltpu.make_async_copy(a, b, sems.at[n + 5])
             for n, (a, b) in enumerate(((many_hbm, many_s), (spot_hbm, spot_s), (short_hbm, short_s)))]
    for copy in lists + loads:
        copy.start()

    flat = u.reshape(3, PLANES * YR, 128)

    def clear(i, c):
        for k in range(3):
            u[k, i] = jnp.zeros((YR, 128), F32)
        return c

    lax.fori_loop(0, PLANES, clear, 0)
    lane_id = iota((1, 128), 1)
    for copy in lists:
        copy.wait()

    def drop(k, most):
        for i in range(2):
            count = many_s[0, 2 * k + i]

            def read(j, i=i):
                at, where = 384 * k + KEEP * i + 4 * j, 128 * k + KEEP * i + 4 * j
                return (tuple(spot_s[where + m] for m in range(4)),
                        tuple(short_s[at + 128 * n + m] for m in range(4) for n in range(3)))

            def four(j, held):
                coming = read(j + 1)
                for m in range(4):
                    here = lane_id == (held[0][m] & 127)
                    row = pl.ds(held[0][m] >> 7, 1)
                    for n in range(3):
                        flat[n, row, :] += jnp.where(here, held[1][3 * m + n], 0.0)
                return coming

            lax.fori_loop(0, (jnp.minimum(count, KEEP) + 3) // 4, four, read(0))
            most = jnp.maximum(most, count)
        return most

    most = lax.fori_loop(0, TILES // 2, drop, 0)

    @pl.when(most > KEEP)
    def _():
        copy = pltpu.make_async_copy(list_hbm, list_ref, sems.at[3])
        copy.start()
        copy.wait()
        find_all(list_ref, spots, t)

        def rest(b, c):
            count = many_s[0, b]

            def chunk(j, c2):
                got = squeeze(list_ref, spots, b, (KEEP * j).astype(F32))
                more[pl.ds(0, 3), pl.ds(0, KEEP)] = got[0:3]
                spot = got[3:4].astype(I32)
                more_i[pl.ds(0, 1), pl.ds(0, KEEP)] = spot
                copies = [pltpu.make_async_copy(more, more_s, sems.at[3]), pltpu.make_async_copy(more_i, more_is, sems.at[4])]
                for copy in copies:
                    copy.start()
                for copy in copies:
                    copy.wait()

                def one(k, c3):
                    spot = more_is[0, k]
                    here = lane_id == (spot & 127)
                    for n in range(3):
                        flat[n, pl.ds(spot >> 7, 1), :] += jnp.where(here, more_s[n, k], 0.0)
                    return c3

                return lax.fori_loop(0, jnp.minimum(count - KEEP * j, KEEP), one, c2)

            return lax.fori_loop(1, (count + KEEP - 1) // KEEP, chunk, c)

        lax.fori_loop(0, TILES, rest, 0)

    loads[0].wait()

    def scale_b(k, c):
        done = []
        for j in range(2):
            s = 2 * k + j
            for i in range(3):
                value = runs_of(lambda k: u[i, jnp.minimum(k, 79), pl.ds(0, 48), :], s, 48, 0, 14, 128 - ZB - RIM)
                done.append((i, B0 + s, 0.5 * coef[B0 + s, pl.ds(0, 48), :] * (value + u[i, B0 + s, pl.ds(0, 48), :])))
        for i, s, value in done:
            u[i, s, pl.ds(0, 48), :] = value
        return c

    lax.fori_loop(0, RUN // 2, scale_b, 0)

    def scale_a(k, c):
        for i in range(3):
            u[i, k] = 0.5 * coef[k] * u[i, k]
        return c

    lax.fori_loop(0, 80, scale_a, 0)

    plan = [(u, p, u, 0.5), (p, q, None, 1.0), (q, u, p, 0.25), (u, p, None, 1.0), (p, q, None, 1.0),
            (q, p, None, 1.0), (p, q, u, 0.0625)]
    for n, (src, dst, base, scale) in enumerate(plan):
        e = RIM - 1 - n
        nk, nh = -(-(CY + 2 * e) // 8), -(-(CY + 1 + 2 * e) // 8)
        for i in range(3):
            src[i, B0 - 1] = pltpu.roll(src[i, B0 + RUN - 1], SEG, 1)
            src[i, B0 + RUN] = pltpu.roll(src[i, B0], 128 - SEG, 1)
        stencil(src, dst, base, coef, hx_ref, hy_ref, hz_ref, B0, B0 + RUN, 8 - e, nk, nh, scale, NP_B)
        stencil(src, dst, base, coef, hx_ref, hy_ref, hz_ref, OWN - e, OWN + CX + e, 8 - e, nk, nh, scale, NP_A)

    loads[1].wait()
    loads[2].wait()
    lane = iota((CY, 128), 1)
    own_y = pl.ds(8, CY)
    leaving = []
    lap = lap_ref[0]
    for g in range(RUNS):
        begin, end = max(0, RUN * g - RIM), min(CX, RUN * (g + 1) - RIM)

        def combine(k, c, g=g, begin=begin, end=end):
            for j in range(4):
                x = jnp.minimum(begin + 4 * k + j, end - 1)
                total = jnp.zeros((CY, 128), F32)
                for i in range(3):
                    rims = q[i, B0 + x + RIM - RUN * g, own_y, :]
                    value = jnp.where(lane >= CZ - 2 * RIM, pltpu.roll(rims, (ZB - SEG * g) % 128, 1),
                                      pltpu.roll(q[i, OWN + x, own_y, :], 128 - RIM, 1))
                    total = total + field[i, x].astype(F32) * value
                rows[x] = -lap * cond[x] * total
            return c

        lax.fori_loop(0, (end - begin + 3) // 4, combine, 0)
        made = pltpu.make_async_copy(rows.at[pl.ds(begin, end - begin)], out_ref.at[pl.ds(begin, end - begin)], sems.at[8 + g])
        made.start()
        leaving.append(made)
    for made in leaving:
        made.wait()


def spread_kernel(part_ref, out_ref, got, send, recv, lsem):
    f, t = lax.axis_index("freq"), lax.axis_index("tile")
    me = f * TILES + t
    barrier = pltpu.get_barrier_semaphore()

    def greet(i, c):
        pl.semaphore_signal(barrier, inc=1, device_id=me ^ (2 * TILES - i), device_id_type=pl.DeviceIdType.LOGICAL)
        return c

    lax.fori_loop(1, 2 * TILES, greet, 0)
    mine = pltpu.make_async_copy(part_ref.at[t, pl.ds(f * 16, 16)], got.at[me], lsem)
    mine.start()
    pl.semaphore_wait(barrier, 2 * TILES - 1)

    def share(i, c):
        d = me ^ (2 * TILES - i)
        pltpu.make_async_remote_copy(part_ref.at[d & (TILES - 1), pl.ds((d >> 6) * 16, 16)], got.at[me], send, recv,
                                     device_id=d, device_id_type=pl.DeviceIdType.LOGICAL).start()
        return c

    lax.fori_loop(1, 2 * TILES, share, 0)
    mine.wait()
    others = got.at[pl.ds(0, 2 * TILES - 1)]
    for sem in (send, recv):
        pltpu.make_async_copy(others, others, sem).wait()

    def add(k, c):
        done = [got[8 * k + j] + got[TILES + 8 * k + j] for j in range(8)]
        for j in range(8):
            out_ref[8 * k + j, 0] = done[j]
        return c

    lax.fori_loop(0, TILES // 8, add, 0)


def local(residual, row_counts, recv_owner, recv_cell, conductivity, laplace, forward_field):
    smem = pl.BlockSpec(memory_space=pltpu.SMEM)
    cond = conductivity[0]
    lists, coef, short, spot, many = pl.pallas_call(
        gather_kernel,
        name="gather_lists",
        out_shape=(jax.ShapeDtypeStruct((TILES, 8, 128), F32), jax.ShapeDtypeStruct((PLANES, YR, 128), F32),
                   jax.ShapeDtypeStruct((104, 128), F32), jax.ShapeDtypeStruct((40, 128), I32),
                   jax.ShapeDtypeStruct((8, 128), I32)),
        in_specs=[hbm(), hbm(), hbm(), hbm(), smem, hbm()],
        out_specs=(vmem(), hbm(), vmem(), vmem(), vmem()),
        scratch_shapes=[
            pltpu.VMEM((3, 1, 1024), F32),
            pltpu.VMEM((1, 256), I32),
            pltpu.VMEM((1, 256), I32),
            pltpu.VMEM((1, 256), I32),
            pltpu.VMEM((2, TILES, 256), F32),
            pltpu.VMEM((CX, CY, CZ), F32),
            pltpu.VMEM((82, 48, 128), F32),
            pltpu.VMEM((10, 48, 128), F32),
            pltpu.VMEM((10, 48, 128), F32),
            pltpu.VMEM((10, 48, 128), F32),
            pltpu.SemaphoreType.DMA((8,)),
            pltpu.SemaphoreType.DMA((8,)),
            pltpu.SemaphoreType.DMA((2,)),
            pltpu.SemaphoreType.DMA((2,)),
            pltpu.SemaphoreType.DMA,
            pltpu.SemaphoreType.DMA,
            pltpu.SemaphoreType.DMA((7,)),
            pltpu.VMEM((PLANES, YR, 128), F32),
        ],
        compiler_params=pltpu.CompilerParams(collective_id=0, has_side_effects=True, vmem_limit_bytes=62 * 2**20),
    )(residual.transpose(1, 0, 2), row_counts, recv_owner.reshape(1, -1), recv_cell.reshape(1, -1), laplace, cond)
    partial = pl.pallas_call(
        relax_kernel,
        name="relax_tile",
        out_shape=jax.ShapeDtypeStruct((CX, CY, CZ), F32),
        in_specs=[hbm(), smem, hbm(), hbm(), hbm(), hbm(), hbm(), hbm()],
        out_specs=hbm(),
        scratch_shapes=[pltpu.VMEM((3, PLANES, YR, 128), F32)] * 3
        + [pltpu.VMEM((PLANES, YR, 128), F32)] * 3
        + [
            pltpu.SMEM((104 * 128,), F32),
            pltpu.SMEM((40 * 128,), I32),
            pltpu.SMEM((8, 128), I32),
            pltpu.VMEM((CX, CY, CZ), F32),
            pltpu.VMEM((PLANES, YR, 128), F32),
            pltpu.VMEM((CX, CY, CZ), F32),
            pltpu.VMEM((3, CX, CY, CZ), BF16),
            pltpu.VMEM((TILES, 8, 128), F32),
            pltpu.VMEM((2, TILES, 256), F32),
            pltpu.VMEM((8, 128), F32),
            pltpu.VMEM((8, 128), I32),
            pltpu.SMEM((8, 128), F32),
            pltpu.SMEM((8, 128), I32),
            pltpu.SemaphoreType.DMA((12,)),
        ],
        compiler_params=pltpu.CompilerParams(vmem_limit_bytes=62 * 2**20),
    )(lists, laplace, short.reshape(-1), spot.reshape(-1), many, coef, cond, forward_field[0, 0])
    return pl.pallas_call(
        spread_kernel,
        name="spread_rows",
        out_shape=jax.ShapeDtypeStruct((TILES, 1, 16, CZ), F32),
        in_specs=[hbm()],
        out_specs=vmem(),
        scratch_shapes=[pltpu.VMEM((2 * TILES, 16, CZ), F32)] + [pltpu.SemaphoreType.DMA] * 3,
        compiler_params=pltpu.CompilerParams(collective_id=1, has_side_effects=True, vmem_limit_bytes=63 * 2**20),
    )(partial)


def solution(mesh):
    placed = (
        P("freq", None, "tile"),
        P("tile", None),
        P("tile", None),
        P("tile"),
        P("tile", None, None, None),
        P("freq"),
        P("freq", "tile", None, None, None, None),
    )
    return jax.shard_map(
        local, mesh=mesh, in_specs=placed, out_specs=P(None, "tile", "freq", None), check_vma=False
    )
```

```python
import functools

import jax
import jax.numpy as jnp
from jax import lax
from jax.experimental import pallas as pl
from jax.experimental.pallas import tpu as pltpu
from jax.sharding import PartitionSpec as P

F32 = jnp.float32
BF16 = jnp.bfloat16
I32 = jnp.int32
MESH = pl.DeviceIdType.MESH

TX, TY, TZ = 4, 4, 4
TILES = 64
CX, CY, CZ = 64, 32, 128
NP_A, NP_B = 8, 10
RIM = 7

YR = 64
B0 = 81
RUN = 20
SEG = 28
RUNS = 4
ZB = CZ + RIM - SEG
PLANES = 112
KEEP = 64
OWN = 8


def iota(shape, dim):
    return lax.broadcasted_iota(I32, shape, dim)


def vmem():
    return pl.BlockSpec(memory_space=pltpu.VMEM)


def hbm():
    return pl.BlockSpec(memory_space=pl.ANY)


def place(t):
    return t // (TY * TZ), (t // TZ) % TY, t % TZ


def three(value):
    hi = value.astype(BF16)
    rest = value - hi.astype(F32)
    mid = rest.astype(BF16)
    low = (rest - mid.astype(F32)).astype(BF16)
    return hi, mid, low


def runs_of(read, s, rows, begin, end, shift):
    lane = iota((rows, 128), 1)
    total = jnp.zeros((rows, 128), F32)
    for g in range(RUNS):
        plane = read(1 + RUN * g + s)
        moved = pltpu.roll(plane, (SEG * g + shift) % 128, 1)
        total = jnp.where((lane >= SEG * g + begin) & (lane < SEG * g + end), moved, total)
    return total


def locate(code, tx, ty, tz):
    x = (code >> 16) - tx * CX + RIM
    y = ((code >> 9) & 127) - ty * CY + RIM
    z = (code & 511) - tz * CZ
    ok = (x >= 0) & (x < CX + 2 * RIM) & (y >= 0) & (y < CY + 2 * RIM) & (z >= -RIM) & (z < CZ + RIM)
    run = sum((x >= RUN * g).astype(I32) for g in range(1, RUNS))
    in_a = z < 128 - RIM
    plane = jnp.where(in_a, x + 1, x - RUN * run + B0)
    lane = jnp.where(in_a, z + RIM, SEG * run + z - ZB)
    return ok, jnp.where(ok, (plane * YR + y + 1) * 128 + lane, 0).astype(F32)


def find_all(list_ref, spots, t):
    code = jnp.concatenate([list_ref[:, 3, :], list_ref[:, 7, :]], axis=1).astype(I32)
    ok, spot = locate(code, *place(t))
    before = (iota((256, 256), 0) < iota((256, 256), 1)).astype(F32).astype(BF16)
    flag = ok.astype(F32)
    rank = jnp.dot(flag.astype(BF16), before, preferred_element_type=F32)
    spots[0] = spot
    spots[1] = jnp.where(ok, rank, -1.0)
    ones = jnp.ones((8, 256), BF16)
    return lax.dot_general(ones, flag.astype(BF16), (((1,), (1,)), ((), ())), preferred_element_type=F32).astype(I32)


def squeeze(list_ref, spots, b, first):
    place_k = iota((KEEP, 256), 0).astype(F32)
    values = jnp.concatenate([list_ref[b, pl.ds(0, 3), :], list_ref[b, pl.ds(4, 3), :]], axis=1)
    both = jnp.concatenate([values, spots[0, pl.ds(b, 1), :]], axis=0)
    pick = (place_k == spots[1, pl.ds(b, 1), :] - first).astype(F32).astype(BF16)
    parts = jnp.concatenate([part.astype(F32) for part in three(both)] + [jnp.zeros((4, 256), F32)], axis=0).astype(BF16)
    got = lax.dot_general(parts, pick, (((1,), (1,)), ((), ())), preferred_element_type=F32)
    return (got[0:4] + got[4:8]) + got[8:12]


def gather_kernel(res_hbm, cnt_hbm, tile_hbm, cell_hbm, lap_ref, cond_ref, list_ref, coef_hbm, short_ref, spot_ref, many_ref,
                  res_ref, cnt_ref, tile_ref, cell_ref, spots, raw, cext, pack, low, high, sends, recvs, zsend, zrecv, gsend, grecv, lsem, coef_ref):
    f, t = lax.axis_index("freq"), lax.axis_index("tile")
    me = f * TILES + t
    tx, ty, tz = place(t)
    barrier = pltpu.get_barrier_semaphore()

    def greet(i, c):
        pl.semaphore_signal(barrier, inc=1, device_id=me ^ i, device_id_type=pl.DeviceIdType.LOGICAL)
        return c

    lax.fori_loop(1, TILES, greet, 0)
    own = pltpu.make_async_copy(cond_ref, raw, lsem.at[0])
    own.start()
    loads = [pltpu.make_async_copy(a, b, lsem.at[n + 1])
             for n, (a, b) in enumerate(((res_hbm, res_ref), (cnt_hbm, cnt_ref), (tile_hbm, tile_ref), (cell_hbm, cell_ref)))]
    for copy in loads:
        copy.start()
    for copy in loads:
        copy.wait()

    counts = cnt_ref[...].astype(F32)
    upto = (iota((256, 256), 0) <= iota((256, 256), 1)).astype(F32)
    ends = jnp.dot(jnp.broadcast_to(counts, (8, 256)).astype(BF16), upto.astype(BF16), preferred_element_type=F32)[0:1]
    starts = ends - counts
    at = iota((1024, 256), 0).astype(F32)
    member = ((at >= starts) & (at < ends)).astype(F32).astype(BF16)
    sums = jnp.zeros((3, 256), F32)
    for part in three(res_ref[:, 0, :]):
        sums = sums + jnp.dot(part, member, preferred_element_type=F32)
    means = sums / counts
    owner, cell = tile_ref[...], cell_ref[...]
    gx = (owner >> 4) * CX + (cell >> 12)
    gy = ((owner >> 2) & 3) * CY + ((cell >> 7) & 31)
    gz = (owner & 3) * CZ + (cell & 127)
    code = ((gx * (TY * CY) + gy) * (TZ * CZ) + gz).astype(F32)
    both = jnp.concatenate([means, code], axis=0)
    list_ref[t] = jnp.concatenate([both[:, :128], both[:, 128:]], axis=0)

    spans = {1: (CX - 7, 1, 7), -1: (0, 72, 7), 0: (0, 8, CX)}
    rows = {1: (CY - 7, 1, 7), -1: (0, 40, 7), 0: (0, 8, CY)}
    ways = [(dx, dy) for dx in (-1, 0, 1) for dy in (-1, 0, 1) if (dx, dy) != (0, 0)]

    def inside(dx, dy):
        x, y = tx + dx, ty + dy
        return (x >= 0) & (x < TX) & (y >= 0) & (y < TY)

    def halo(n):
        dx, dy = ways[n]
        xs, xd, xn = spans[dx]
        ys, yd, yn = rows[dy]
        return pltpu.make_async_remote_copy(
            cext.at[pl.ds(OWN + xs, xn), pl.ds(8 + ys, yn)], cext.at[pl.ds(xd, xn), pl.ds(yd, yn)],
            sends.at[n], recvs.at[n], device_id=(f, t + dx * TY * TZ + dy * TZ), device_id_type=MESH)

    for dx, dy in ways:
        @pl.when(jnp.logical_not(inside(-dx, -dy)))
        def _(dx=dx, dy=dy):
            def wipe(i, c):
                cext[spans[dx][1] + i, pl.ds(rows[dy][1], rows[dy][2]), :] = jnp.zeros((rows[dy][2], 128), F32)
                return c

            lax.fori_loop(0, spans[dx][2], wipe, 0)
    lap = lap_ref[0]
    lane = iota((48, 128), 1)
    own.wait()

    def invert(k, c):
        done = [1.0 / (4.0 + lap * raw[4 * k + j]) for j in range(4)]
        for j in range(4):
            cext[OWN + 4 * k + j, pl.ds(8, CY), :] = done[j]
        return c

    lax.fori_loop(0, CX // 4, invert, 0)
    pl.semaphore_wait(barrier, TILES - 1)

    def share(i, c):
        pltpu.make_async_remote_copy(list_ref.at[t], list_ref.at[t], gsend, grecv,
                                     device_id=me ^ i, device_id_type=pl.DeviceIdType.LOGICAL).start()
        return c

    lax.fori_loop(1, TILES, share, 0)

    for n, (dx, dy) in enumerate(ways):
        @pl.when(inside(dx, dy))
        def _(n=n):
            halo(n).start()

    def lay(planes, begin, count):
        part = pl.ds(begin, count)
        done = [jnp.where(lane[:count] < RIM, 0.0, pltpu.roll(cext[i, part, :], RIM, 1)) for i in planes]
        for i, value in zip(planes, done):
            coef_ref[i, part, :] = value

    def lay_own(k, c):
        lay([OWN + 4 * k + j for j in range(4)], 8, CY)
        return c

    lax.fori_loop(0, CX // 4, lay_own, 0)
    everyone = list_ref.at[pl.ds(0, TILES - 1)]
    pltpu.make_async_copy(everyone, everyone, grecv).wait()
    many_ref[:, pl.ds(0, TILES)] = find_all(list_ref, spots, t)

    def compact(k, c):
        for i in range(2):
            pair = jnp.concatenate([squeeze(list_ref, spots, 4 * k + 2 * i + j, 0.0) for j in range(2)], axis=1)
            short_ref[pl.ds(3 * (2 * k + i), 3), :] = pair[0:3]
            spot_ref[pl.ds(2 * k + i, 1), :] = pair[3:4].astype(I32)
        return c

    lax.fori_loop(0, TILES // 4, compact, 0)
    for n, (dx, dy) in enumerate(ways):
        @pl.when(inside(-dx, -dy))
        def _(n=n):
            halo(n).wait_recv()

    def read(i):
        return cext[jnp.minimum(i, 79)]

    def fill(k, c):
        done = []
        for j in range(2):
            total = jnp.zeros((48, 128), F32)
            for h in range(8):
                plane = read(1 + 10 * h + 2 * k + j)
                for begin, shift in ((16 * h, 16 * h - 121), (16 * h + 8, 16 * h + 8)):
                    moved = pltpu.roll(plane, shift % 128, 1)
                    total = jnp.where((lane >= begin) & (lane < begin + 7), moved, total)
            done.append(total)
        for j in range(2):
            pack[2 * k + j] = done[j]
        return c

    lax.fori_loop(0, 5, fill, 0)

    def rim(up):
        return pltpu.make_async_remote_copy(
            pack, low if up else high, zsend.at[up], zrecv.at[up],
            device_id=(f, t + (1 if up else -1)), device_id_type=MESH)

    @pl.when(tz < TZ - 1)
    def _():
        rim(1).start()

    @pl.when(tz > 0)
    def _():
        rim(0).start()

    def lay_rows(k, c):
        planes = [OWN + 4 * k + j for j in range(4)]
        lay(planes, 0, 8)
        lay(planes, 40, 8)
        return c

    lax.fori_loop(0, CX // 4, lay_rows, 0)

    def lay_planes(k, c):
        lay([1 + k, 72 + k], 0, 48)
        return c

    lax.fori_loop(0, RIM, lay_planes, 0)

    def fill_b(k, c):
        done = [runs_of(read, 2 * k + j, 48, 0, SEG - RIM, 128 - ZB) for j in range(2)]
        for j in range(2):
            coef_ref[B0 + 2 * k + j, pl.ds(0, 48), :] = done[j]
        return c

    lax.fori_loop(0, RUN // 2, fill_b, 0)

    @pl.when(tz > 0)
    def _():
        rim(1).wait_recv()

        def patch(k, c):
            done = []
            for h in range(8):
                old = coef_ref[1 + 10 * h + k, pl.ds(0, 48), :]
                done.append(jnp.where(lane < RIM, pltpu.roll(low[k], (128 - 16 * h) % 128, 1), old))
            for h in range(8):
                coef_ref[1 + 10 * h + k, pl.ds(0, 48), :] = done[h]
            return c

        lax.fori_loop(0, 10, patch, 0)

    leaving = [pltpu.make_async_copy(coef_ref.at[pl.ds(b, n)], coef_hbm.at[pl.ds(b, n)], lsem.at[5 + k])
               for k, (b, n) in enumerate(((0, 80), (80, 24)))]
    leaving[0].start()

    @pl.when(tz < TZ - 1)
    def _():
        rim(0).wait_recv()

        def patch(k, c):
            done = []
            for j in range(2):
                s = 2 * k + j
                value = coef_ref[B0 + s, pl.ds(0, 48), :]
                for g in range(RUNS):
                    i = RUN * g + s
                    turn = (SEG * g + SEG - RIM - 8 - 16 * (i // 10) + 256) % 128
                    inner = (lane >= SEG * g + SEG - RIM) & (lane < SEG * g + SEG)
                    value = jnp.where(inner, pltpu.roll(high[i % 10], turn, 1), value)
                done.append(value)
            for j in range(2):
                coef_ref[B0 + 2 * k + j, pl.ds(0, 48), :] = done[j]
            return c

        lax.fori_loop(0, RUN // 2, patch, 0)

    leaving[1].start()

    for n, (dx, dy) in enumerate(ways):
        @pl.when(inside(dx, dy))
        def _(n=n):
            halo(n).wait_send()

    @pl.when(tz < TZ - 1)
    def _():
        rim(1).wait_send()

    @pl.when(tz > 0)
    def _():
        rim(0).wait_send()

    pltpu.make_async_copy(everyone, everyone, gsend).wait()
    for copy in leaving:
        copy.wait()


def stencil(src, dst, base, coef, hx_ref, hy_ref, hz_ref, lo, hi, y0, nk, nh, scale, step):
    rk, rh, h0 = 8 * nk, 8 * nh, y0 - 1
    hr, hy_rows, kr, kl = pl.ds(h0, rh), pl.ds(y0, rh), pl.ds(y0, rk), pl.ds(h0, rk)

    def swirl(x):
        vx, vy, vz = src[0, x, hr, :], src[1, x, hr, :], src[2, x, hr, :]
        vyz, vxz = pltpu.roll(vy, 127, 1), pltpu.roll(vx, 127, 1)
        hx_ref[x, hr, :] = (src[2, x, hy_rows, :] - vz) - (vyz - vy)
        hy_ref[x, hr, :] = (vxz - vx) - (src[2, x + 1, hr, :] - vz)
        hz_ref[x, hr, :] = (src[1, x + 1, hr, :] - vy) - (src[0, x, hy_rows, :] - vx)

    def relax(x):
        hx, hy, hz = hx_ref[x, kr, :], hy_ref[x, kr, :], hz_ref[x, kr, :]
        kx = (hz - hz_ref[x, kl, :]) - (hy - pltpu.roll(hy, 1, 1))
        ky = (hx - pltpu.roll(hx, 1, 1)) - (hz - hz_ref[x - 1, kr, :])
        kz = (hy - hy_ref[x - 1, kr, :]) - (hx - hx_ref[x, kl, :])
        c = coef[x, kr, :] if scale == 1.0 else scale * coef[x, kr, :]
        keep = (scale if base is not src else 1.0 + scale) + 4.0 * c
        for i, k in enumerate((kx, ky, kz)):
            new = keep * src[i, x, kr, :] - c * k
            if base is not None and base is not src:
                new = base[i, x, kr, :] + new
            dst[i, x, kr, :] = new

    for i in range(-1, step):
        swirl(lo + i)

    def body(k, c):
        x = jnp.minimum(lo + step * k, hi - step)
        for i in range(step):
            relax(x + i)
        for i in range(step):
            swirl(x + step + i)
        return c

    lax.fori_loop(0, (hi - lo + step - 1) // step, body, 0)


def relax_kernel(list_hbm, lap_ref, short_hbm, spot_hbm, many_hbm, coef_hbm, cond_hbm, field_hbm, out_ref,
                 u, p, q, hx_ref, hy_ref, hz_ref, short_s, spot_s, many_s, rows, coef, cond, field, list_ref, spots, more, more_i, more_s, more_is, sems):
    t = lax.axis_index("tile")
    loads = [pltpu.make_async_copy(a, b, sems.at[n])
             for n, (a, b) in enumerate(((coef_hbm.at[pl.ds(0, 104)], coef.at[pl.ds(0, 104)]), (cond_hbm, cond), (field_hbm, field)))]
    lists = [pltpu.make_async_copy(a, b, sems.at[n + 5])
             for n, (a, b) in enumerate(((many_hbm, many_s), (spot_hbm, spot_s), (short_hbm, short_s)))]
    for copy in lists + loads:
        copy.start()

    flat = u.reshape(3, PLANES * YR, 128)

    def clear(i, c):
        for k in range(3):
            u[k, i] = jnp.zeros((YR, 128), F32)
        return c

    lax.fori_loop(0, PLANES, clear, 0)
    lane_id = iota((1, 128), 1)
    for copy in lists:
        copy.wait()

    def drop(k, most):
        for i in range(2):
            count = many_s[0, 2 * k + i]

            def read(j, i=i):
                at, where = 384 * k + KEEP * i + 4 * j, 128 * k + KEEP * i + 4 * j
                return (tuple(spot_s[where + m] for m in range(4)),
                        tuple(short_s[at + 128 * n + m] for m in range(4) for n in range(3)))

            def four(j, held):
                coming = read(j + 1)
                for m in range(4):
                    here = lane_id == (held[0][m] & 127)
                    row = pl.ds(held[0][m] >> 7, 1)
                    for n in range(3):
                        flat[n, row, :] += jnp.where(here, held[1][3 * m + n], 0.0)
                return coming

            lax.fori_loop(0, (jnp.minimum(count, KEEP) + 3) // 4, four, read(0))
            most = jnp.maximum(most, count)
        return most

    most = lax.fori_loop(0, TILES // 2, drop, 0)

    @pl.when(most > KEEP)
    def _():
        copy = pltpu.make_async_copy(list_hbm, list_ref, sems.at[3])
        copy.start()
        copy.wait()
        find_all(list_ref, spots, t)

        def rest(b, c):
            count = many_s[0, b]

            def chunk(j, c2):
                got = squeeze(list_ref, spots, b, (KEEP * j).astype(F32))
                more[pl.ds(0, 3), pl.ds(0, KEEP)] = got[0:3]
                spot = got[3:4].astype(I32)
                more_i[pl.ds(0, 1), pl.ds(0, KEEP)] = spot
                copies = [pltpu.make_async_copy(more, more_s, sems.at[3]), pltpu.make_async_copy(more_i, more_is, sems.at[4])]
                for copy in copies:
                    copy.start()
                for copy in copies:
                    copy.wait()

                def one(k, c3):
                    spot = more_is[0, k]
                    here = lane_id == (spot & 127)
                    for n in range(3):
                        flat[n, pl.ds(spot >> 7, 1), :] += jnp.where(here, more_s[n, k], 0.0)
                    return c3

                return lax.fori_loop(0, jnp.minimum(count - KEEP * j, KEEP), one, c2)

            return lax.fori_loop(1, (count + KEEP - 1) // KEEP, chunk, c)

        lax.fori_loop(0, TILES, rest, 0)

    loads[0].wait()

    def scale_b(k, c):
        done = []
        for j in range(2):
            s = 2 * k + j
            for i in range(3):
                value = runs_of(lambda k: u[i, jnp.minimum(k, 79), pl.ds(0, 48), :], s, 48, 0, 14, 128 - ZB - RIM)
                done.append((i, B0 + s, 0.5 * coef[B0 + s, pl.ds(0, 48), :] * (value + u[i, B0 + s, pl.ds(0, 48), :])))
        for i, s, value in done:
            u[i, s, pl.ds(0, 48), :] = value
        return c

    lax.fori_loop(0, RUN // 2, scale_b, 0)

    def scale_a(k, c):
        for i in range(3):
            u[i, k] = 0.5 * coef[k] * u[i, k]
        return c

    lax.fori_loop(0, 80, scale_a, 0)

    plan = [(u, p, u, 0.5), (p, q, None, 1.0), (q, u, p, 0.25), (u, p, None, 1.0), (p, q, None, 1.0),
            (q, p, None, 1.0), (p, q, u, 0.0625)]
    for n, (src, dst, base, scale) in enumerate(plan):
        e = RIM - 1 - n
        nk, nh = -(-(CY + 2 * e) // 8), -(-(CY + 1 + 2 * e) // 8)
        for i in range(3):
            src[i, B0 - 1] = pltpu.roll(src[i, B0 + RUN - 1], SEG, 1)
            src[i, B0 + RUN] = pltpu.roll(src[i, B0], 128 - SEG, 1)
        stencil(src, dst, base, coef, hx_ref, hy_ref, hz_ref, B0, B0 + RUN, 8 - e, nk, nh, scale, NP_B)
        stencil(src, dst, base, coef, hx_ref, hy_ref, hz_ref, OWN - e, OWN + CX + e, 8 - e, nk, nh, scale, NP_A)

    loads[1].wait()
    loads[2].wait()
    lane = iota((CY, 128), 1)
    own_y = pl.ds(8, CY)
    leaving = []
    lap = lap_ref[0]
    for g in range(RUNS):
        begin, end = max(0, RUN * g - RIM), min(CX, RUN * (g + 1) - RIM)

        def combine(k, c, g=g, begin=begin, end=end):
            for j in range(7):
                x = jnp.minimum(begin + 7 * k + j, end - 1)
                total = jnp.zeros((CY, 128), F32)
                for i in range(3):
                    rims = q[i, B0 + x + RIM - RUN * g, own_y, :]
                    value = jnp.where(lane >= CZ - 2 * RIM, pltpu.roll(rims, (ZB - SEG * g) % 128, 1),
                                      pltpu.roll(q[i, OWN + x, own_y, :], 128 - RIM, 1))
                    total = total + field[i, x].astype(F32) * value
                rows[x] = -lap * cond[x] * total
            return c

        lax.fori_loop(0, (end - begin + 6) // 7, combine, 0)
        made = pltpu.make_async_copy(rows.at[pl.ds(begin, end - begin)], out_ref.at[pl.ds(begin, end - begin)], sems.at[8 + g])
        made.start()
        leaving.append(made)
    for made in leaving:
        made.wait()


def spread_kernel(part_ref, out_ref, send, recv, lsem):
    f, t = lax.axis_index("freq"), lax.axis_index("tile")
    me = f * TILES + t
    barrier = pltpu.get_barrier_semaphore()

    def greet(i, c):
        pl.semaphore_signal(barrier, inc=1, device_id=me ^ (2 * TILES - i), device_id_type=pl.DeviceIdType.LOGICAL)
        return c

    lax.fori_loop(1, 2 * TILES, greet, 0)
    mine = pltpu.make_async_copy(part_ref.at[t, pl.ds(f * 16, 16)], out_ref.at[me], lsem)
    mine.start()
    pl.semaphore_wait(barrier, 2 * TILES - 1)

    def share(i, c):
        d = me ^ (2 * TILES - i)
        pltpu.make_async_remote_copy(part_ref.at[d & (TILES - 1), pl.ds((d >> 6) * 16, 16)], out_ref.at[me], send, recv,
                                     device_id=d, device_id_type=pl.DeviceIdType.LOGICAL).start()
        return c

    lax.fori_loop(1, 2 * TILES, share, 0)
    mine.wait()
    others = out_ref.at[pl.ds(0, 2 * TILES - 1)]
    for sem in (send, recv):
        pltpu.make_async_copy(others, others, sem).wait()


def add_kernel(both_hbm, out_ref, both_ref, sem):
    load = pltpu.make_async_copy(both_hbm, both_ref, sem)
    load.start()
    load.wait()

    def body(k, c):
        done = [both_ref[8 * k + j] + both_ref[TILES + 8 * k + j] for j in range(8)]
        for j in range(8):
            out_ref[8 * k + j, 0] = done[j]
        return c

    lax.fori_loop(0, TILES // 8, body, 0)


def local(residual, row_counts, recv_owner, recv_cell, conductivity, laplace, forward_field):
    smem = pl.BlockSpec(memory_space=pltpu.SMEM)
    cond = conductivity[0]
    lists, coef, short, spot, many = pl.pallas_call(
        gather_kernel,
        name="gather_lists",
        out_shape=(jax.ShapeDtypeStruct((TILES, 8, 128), F32), jax.ShapeDtypeStruct((PLANES, YR, 128), F32),
                   jax.ShapeDtypeStruct((104, 128), F32), jax.ShapeDtypeStruct((40, 128), I32),
                   jax.ShapeDtypeStruct((8, 128), I32)),
        in_specs=[hbm(), hbm(), hbm(), hbm(), smem, hbm()],
        out_specs=(vmem(), hbm(), vmem(), vmem(), vmem()),
        scratch_shapes=[
            pltpu.VMEM((3, 1, 1024), F32),
            pltpu.VMEM((1, 256), I32),
            pltpu.VMEM((1, 256), I32),
            pltpu.VMEM((1, 256), I32),
            pltpu.VMEM((2, TILES, 256), F32),
            pltpu.VMEM((CX, CY, CZ), F32),
            pltpu.VMEM((82, 48, 128), F32),
            pltpu.VMEM((10, 48, 128), F32),
            pltpu.VMEM((10, 48, 128), F32),
            pltpu.VMEM((10, 48, 128), F32),
            pltpu.SemaphoreType.DMA((8,)),
            pltpu.SemaphoreType.DMA((8,)),
            pltpu.SemaphoreType.DMA((2,)),
            pltpu.SemaphoreType.DMA((2,)),
            pltpu.SemaphoreType.DMA,
            pltpu.SemaphoreType.DMA,
            pltpu.SemaphoreType.DMA((7,)),
            pltpu.VMEM((PLANES, YR, 128), F32),
        ],
        compiler_params=pltpu.CompilerParams(collective_id=0, has_side_effects=True, vmem_limit_bytes=62 * 2**20),
    )(residual.transpose(1, 0, 2), row_counts, recv_owner.reshape(1, -1), recv_cell.reshape(1, -1), laplace, cond)
    partial = pl.pallas_call(
        relax_kernel,
        name="relax_tile",
        out_shape=jax.ShapeDtypeStruct((CX, CY, CZ), F32),
        in_specs=[hbm(), smem, hbm(), hbm(), hbm(), hbm(), hbm(), hbm()],
        out_specs=hbm(),
        scratch_shapes=[pltpu.VMEM((3, PLANES, YR, 128), F32)] * 3
        + [pltpu.VMEM((PLANES, YR, 128), F32)] * 3
        + [
            pltpu.SMEM((104 * 128,), F32),
            pltpu.SMEM((40 * 128,), I32),
            pltpu.SMEM((8, 128), I32),
            pltpu.VMEM((CX, CY, CZ), F32),
            pltpu.VMEM((PLANES, YR, 128), F32),
            pltpu.VMEM((CX, CY, CZ), F32),
            pltpu.VMEM((3, CX, CY, CZ), BF16),
            pltpu.VMEM((TILES, 8, 128), F32),
            pltpu.VMEM((2, TILES, 256), F32),
            pltpu.VMEM((8, 128), F32),
            pltpu.VMEM((8, 128), I32),
            pltpu.SMEM((8, 128), F32),
            pltpu.SMEM((8, 128), I32),
            pltpu.SemaphoreType.DMA((12,)),
        ],
        compiler_params=pltpu.CompilerParams(vmem_limit_bytes=62 * 2**20),
    )(lists, laplace, short.reshape(-1), spot.reshape(-1), many, coef, cond, forward_field[0, 0])
    both = pl.pallas_call(
        spread_kernel,
        name="spread_rows",
        out_shape=jax.ShapeDtypeStruct((2 * TILES, 16, CZ), F32),
        in_specs=[hbm()],
        out_specs=hbm(),
        scratch_shapes=[pltpu.SemaphoreType.DMA] * 3,
        compiler_params=pltpu.CompilerParams(collective_id=1, has_side_effects=True, vmem_limit_bytes=4 * 2**20),
    )(partial)
    return pl.pallas_call(
        add_kernel,
        name="add_frequencies",
        out_shape=jax.ShapeDtypeStruct((TILES, 1, 16, CZ), F32),
        in_specs=[hbm()],
        out_specs=vmem(),
        scratch_shapes=[pltpu.VMEM((2 * TILES, 16, CZ), F32), pltpu.SemaphoreType.DMA],
        compiler_params=pltpu.CompilerParams(vmem_limit_bytes=4 * 2**20),
    )(both)


def solution(mesh):
    placed = (
        P("freq", None, "tile"),
        P("tile", None),
        P("tile", None),
        P("tile"),
        P("tile", None, None, None),
        P("freq"),
        P("freq", "tile", None, None, None, None),
    )
    return jax.shard_map(
        local, mesh=mesh, in_specs=placed, out_specs=P(None, "tile", "freq", None), check_vma=False
    )
```
